128 devices in a mesh: depth: 32 (over z, y, core), rows: 4 (over x).
Axes of the slice: x: 4, y: 4, z: 4, core: 2. Of those that a mesh axis runs over, the one named last changes fastest.
Arguments:
- populations: float32 [19, 192, 128, 256], P(None, 'depth', 'rows'), may hold values from 0 to 1, as said below
- fluid_mask: int32 [192, 128, 256], P('depth', 'rows'), may hold values from 0 to 1
- tissue_tag: int32 [192, 128, 256], P('depth', 'rows'), may hold values from 0 to 3
- colour_table: float32 [4, 4, 256], replicated, may hold values from 0 to 1
Outputs:
- advanced: float32 [19, 192, 128, 256], P(None, 'depth', 'rows')
- rendered: float32 [4, 512, 512], P(None, ('rows', 'depth'))
The draws below stay inside these ranges and needn't reach their ends.
Inputs may be any that keep to these rules, and one draw needn't show every extreme that they name: Every site's populations are positive and close to a lattice equilibrium.
All inputs are finite; a program needn't handle non-finite values.
Results may differ from the reference program's by a relative error of at most 0.0003.
Values sent between devices are 32-bit elements; how exact they have to be, the bound alone decides.
A program may use at most 64 MiB of HBM per device.

```python
import jax
import jax.numpy as jnp
from jax import lax

NX = 256
IMG = 512
BINS = 256
TAGS = 4
NY = 128
NZ = 192


VELOCITIES = ((0, 0, 0), (1, 0, 0), (-1, 0, 0), (0, 1, 0), (0, -1, 0), (0, 0, 1), (0, 0, -1), (1, 1, 0), (-1, -1, 0), (1, -1, 0), (-1, 1, 0), (1, 0, 1), (-1, 0, -1), (1, 0, -1), (-1, 0, 1), (0, 1, 1), (0, -1, -1), (0, 1, -1), (0, -1, 1))


WEIGHTS = (1.0 / 3.0,) + (1.0 / 18.0,) * 6 + (1.0 / 36.0,) * 12


def draw_populations(key, part):
    key_density, key_velocity, key_jitter = jax.random.split(jax.random.fold_in(key, 7), 3)
    grid_shape = (NZ, NY, NX)
    density = jax.random.uniform(key_density, grid_shape, jnp.float32, 0.9, 1.1)
    velocity = 0.025 * jax.random.truncated_normal(key_velocity, -2.4, 2.4, (3,) + grid_shape, jnp.float32)
    jitter = 0.08 * jax.random.truncated_normal(key_jitter, -2.5, 2.5, (19,) + grid_shape, jnp.float32)
    square = velocity[0] * velocity[0] + velocity[1] * velocity[1] + velocity[2] * velocity[2]
    layers_out = []
    for direction in range(19):
        step_x, step_y, step_z = VELOCITIES[direction]
        projection = step_x * velocity[0] + step_y * velocity[1] + step_z * velocity[2]
        balance = WEIGHTS[direction] * density * (1.0 + 3.0 * projection + 4.5 * projection * projection - 1.5 * square)
        layers_out.append(balance * (1.0 + jitter[direction]))
    return jnp.stack(layers_out)


def draw_fluid_mask(key, part):
    key_column, key_site = jax.random.split(jax.random.fold_in(key, 11), 2)
    column_roll = jax.random.randint(key_column, (1, NY, NX), 0, 4, jnp.int32)
    site_roll = jax.random.randint(key_site, (NZ, NY, NX), 0, 8, jnp.int32)
    open_column = column_roll < 3
    opened = jnp.where(open_column, site_roll < 7, site_roll < 1)
    return opened.astype(jnp.int32)


def with_ends(array, rng, least, largest):
    shape = array.shape
    index_at = [jax.random.randint(jax.random.fold_in(rng, axis), (), 0, shape[axis]) for axis in range(len(shape))]
    array = array.at[tuple(index_at)].set(least)
    longest = shape.index(max(shape))
    index_at[longest] = (index_at[longest] + 1) % shape[longest]
    return array.at[tuple(index_at)].set(largest)


def setup_inputs(seed: int = 0) -> dict:
    arg_keys = jax.random.split(jax.random.key(seed), 5)
    return {
        "populations": draw_populations(jax.random.fold_in(arg_keys[4], 71), 0),
        "fluid_mask": draw_fluid_mask(jax.random.fold_in(arg_keys[4], 71), 0),
        "tissue_tag": with_ends(jax.random.randint(arg_keys[2], (NZ, NY, NX), 0, TAGS), jax.random.fold_in(arg_keys[2], 1), 0, TAGS - 1).astype(jnp.int32),
        "colour_table": jnp.clip(jax.random.uniform(arg_keys[3], (TAGS, 4, BINS), jnp.float32, 0.0, 1.0), 0.0, 1.0),
    }


VELOCITIES = ((0, 0, 0), (1, 0, 0), (-1, 0, 0), (0, 1, 0), (0, -1, 0), (0, 0, 1), (0, 0, -1), (1, 1, 0), (-1, -1, 0), (1, -1, 0), (-1, 1, 0), (1, 0, 1), (-1, 0, -1), (1, 0, -1), (-1, 0, 1), (0, 1, 1), (0, -1, -1), (0, 1, -1), (0, -1, 1))
WEIGHTS = (1.0 / 3.0,) + (1.0 / 18.0,) * 6 + (1.0 / 36.0,) * 12
OPPOSITE = (0, 2, 1, 4, 3, 6, 5, 8, 7, 10, 9, 12, 11, 14, 13, 16, 15, 18, 17)
NU_ZERO = 0.12
NU_INFINITY = 0.02
LAMBDA_TIME = 15.0
POWER_INDEX = 0.3568
TAU_ZERO = 0.8
SPEED_SCALE = 0.04
SHEAR_SCALE = 0.07
HIGHEST = lax.Precision.HIGHEST

def signed_sum(populations_in, coefficients):
    result = None
    for direction in range(19):
        factor = coefficients[direction]
        if factor == 0:
            continue
        addend = populations_in[direction] if factor > 0 else -populations_in[direction]
        result = addend if result is None else result + addend
    return result

def moments(populations_in, fluid_share):
    raw_density = lax.optimization_barrier(jnp.sum(populations_in, axis=0))
    density = jnp.where(fluid_share > 0.5, raw_density, 1.0)
    velocity = tuple((signed_sum(populations_in, [vector[axis_number] for vector in VELOCITIES]) / density for axis_number in range(3)))
    return (density, velocity)

def equilibrium(density, velocity):
    square = velocity[0] * velocity[0] + velocity[1] * velocity[1] + velocity[2] * velocity[2]
    layers_out = []
    for direction in range(19):
        step_x, step_y, step_z = VELOCITIES[direction]
        projection = step_x * velocity[0] + step_y * velocity[1] + step_z * velocity[2]
        layers_out.append(WEIGHTS[direction] * density * (1.0 + 3.0 * projection + 4.5 * projection * projection - 1.5 * square))
    return jnp.stack(layers_out)

def shear_measure(non_equilibrium, density):
    contracted = 0.0
    for first_axis, second_axis in ((0, 0), (1, 1), (2, 2), (0, 1), (0, 2), (1, 2)):
        stress = signed_sum(non_equilibrium, [vector[first_axis] * vector[second_axis] for vector in VELOCITIES])
        factor = 1.0 if first_axis == second_axis else 2.0
        contracted = contracted + factor * stress * stress
    return 1.5 / (density * TAU_ZERO) * jnp.sqrt(2.0 * contracted + 1e-10)

def collide(populations_in, fluid_share):
    density, velocity = moments(populations_in, fluid_share)
    balance = equilibrium(density, velocity)
    strain_rate = shear_measure(populations_in - balance, density)
    viscosity = NU_INFINITY + (NU_ZERO - NU_INFINITY) * (1.0 + (LAMBDA_TIME * strain_rate) ** 2) ** ((POWER_INDEX - 1.0) / 2.0)
    relaxation = 3.0 * viscosity + 0.5
    return populations_in - (populations_in - balance) / relaxation

def stream_step(padded, padded_fluid, relaxed, previous, fluid_share):
    extent = relaxed.shape[1:]
    arrived = []
    for direction in range(19):
        step_x, step_y, step_z = VELOCITIES[direction]
        window = (slice(1 - step_z, 1 - step_z + extent[0]), slice(1 - step_y, 1 - step_y + extent[1]), slice(1 - step_x, 1 - step_x + extent[2]))
        source = padded[direction][window]
        opened = padded_fluid[window]
        arrived.append(jnp.where(opened > 0.5, source, relaxed[OPPOSITE[direction]]))
    return jnp.where(fluid_share > 0.5, jnp.stack(arrived), previous)

def diagnostics(populations_in, fluid_share):
    density, velocity = moments(populations_in, fluid_share)
    balance = equilibrium(density, velocity)
    strain_rate = shear_measure(populations_in - balance, density)
    flow_speed = jnp.sqrt(velocity[0] * velocity[0] + velocity[1] * velocity[1] + velocity[2] * velocity[2] + 1e-12)
    return (flow_speed, strain_rate)

def classify(flow_speed, strain_rate, fluid_share, tissue, colour_table, opacity):
    plane_shape = flow_speed.shape
    bin_count = colour_table.shape[2]
    kind_count = colour_table.shape[0]
    bin_grid = jnp.arange(bin_count, dtype=jnp.int32).astype(jnp.float32)[:, None]
    at_speed = ((bin_count - 1) * (flow_speed / (flow_speed + SPEED_SCALE))).reshape(1, -1)
    at_shear = ((bin_count - 1) * (strain_rate / (strain_rate + SHEAR_SCALE))).reshape(1, -1)
    hat_speed = jnp.maximum(0.0, 1.0 - jnp.abs(at_speed - bin_grid))
    hat_shear = jnp.maximum(0.0, 1.0 - jnp.abs(at_shear - bin_grid))
    colour_rows = colour_table[:, 0:3, :].reshape(kind_count * 3, bin_count)
    by_speed = jnp.dot(colour_rows, hat_speed, precision=HIGHEST).reshape(kind_count, 3, -1)
    by_shear = jnp.dot(colour_table[:, 3, :], hat_shear, precision=HIGHEST)
    chosen = (tissue.reshape(1, -1) == jnp.arange(kind_count, dtype=jnp.int32)[:, None]).astype(jnp.float32)
    colour = lax.optimization_barrier(jnp.sum(by_speed * chosen[:, None, :], axis=0))
    coverage = lax.optimization_barrier(jnp.sum(by_shear * chosen, axis=0)) * fluid_share.reshape(-1) * opacity
    joined = jnp.concatenate([colour * coverage[None, :], coverage[None, :]], axis=0)
    return joined.reshape((4,) + plane_shape)

def tent_weights(targets, sources, spacing):
    centre = (targets.astype(jnp.float32) + 0.5) * spacing - 0.5
    return jnp.maximum(0.0, 1.0 - jnp.abs(centre[:, None] - sources.astype(jnp.float32)[None, :]))

def over_pair(nearer, behind):
    return nearer + (1.0 - nearer[3:4]) * behind

def reference(populations, fluid_mask, tissue_tag, colour_table):
    fluid_share = fluid_mask.astype(jnp.float32)
    padded_fluid = jnp.pad(fluid_share, 1)
    current = populations
    for time_step in range(2):
        relaxed = collide(current, fluid_share)
        padded = jnp.pad(relaxed, ((0, 0), (1, 1), (1, 1), (1, 1)))
        current = stream_step(padded, padded_fluid, relaxed, current, fluid_share)
    flow_speed, strain_rate = diagnostics(current, fluid_share)
    opacity = 3.0 / NZ
    weight_rows = tent_weights(jnp.arange(IMG, dtype=jnp.int32), jnp.arange(NX, dtype=jnp.int32), NX / IMG)
    weight_columns = tent_weights(jnp.arange(IMG, dtype=jnp.int32), jnp.arange(NY, dtype=jnp.int32), NY / IMG)

    def add_slice(carry_image, inputs_slice):
        speed_plane, strain_plane, fluid_plane, tissue_plane = inputs_slice
        layer_rgba = classify(speed_plane, strain_plane, fluid_plane, tissue_plane, colour_table, opacity)
        resampled = jnp.einsum('cab,ub->cua', layer_rgba, weight_rows, precision=HIGHEST)
        projected = jnp.einsum('cua,va->cuv', resampled, weight_columns, precision=HIGHEST)
        return (over_pair(carry_image, projected), None)
    start_image = jnp.zeros((4, IMG, IMG), jnp.float32)
    rendered = lax.scan(add_slice, start_image, (flow_speed, strain_rate, fluid_share, tissue_tag))[0]
    return (current, rendered)
```

```python
import functools

import jax
import jax.numpy as jnp
from jax import lax
from jax.experimental import pallas as pl
from jax.experimental.pallas import tpu as pltpu
from jax.sharding import PartitionSpec as P

F32 = jnp.float32
BF16 = jnp.bfloat16
MESH = pl.DeviceIdType.MESH

VELOCITIES = (
    (0, 0, 0), (1, 0, 0), (-1, 0, 0), (0, 1, 0), (0, -1, 0), (0, 0, 1), (0, 0, -1),
    (1, 1, 0), (-1, -1, 0), (1, -1, 0), (-1, 1, 0),
    (1, 0, 1), (-1, 0, -1), (1, 0, -1), (-1, 0, 1),
    (0, 1, 1), (0, -1, -1), (0, 1, -1), (0, -1, 1),
)
OPPOSITE = (0, 2, 1, 4, 3, 6, 5, 8, 7, 10, 9, 12, 11, 14, 13, 16, 15, 18, 17)
PAIRS = tuple((q, q + 1) for q in range(1, 19, 2))
NU_ZERO = 0.12
NU_INFINITY = 0.02
LAMBDA_TIME = 15.0
POWER_INDEX = 0.3568
TAU_ZERO = 0.8
SPEED_SCALE = 0.04
SHEAR_SCALE = 0.07

ORDER = (16, 6, 12, 13, 17, 3, 7, 10, 15, 5, 11, 14, 18, 4, 8, 9, 0, 1, 2)
POS = tuple(ORDER.index(q) for q in range(19))
UP_Z, DOWN_Z = 8, 0
UP_Y = (4, 5, 6, 7, 8)
DOWN_Y = (12, 13, 14, 15, 0)
WALL = -1e30
WALL_LIMIT = -1e29

NQ, NZL, NYL, NX = 19, 6, 32, 256
ND, NR, NC = 32, 4, 16
IMG = 512


def moments(f):
    sums = [f[a] + f[b] for a, b in PAIRS]
    diffs = [f[a] - f[b] for a, b in PAIRS]
    density = f[0]
    for s in sums:
        density = density + s
    mx = diffs[0] + (diffs[3] + diffs[4]) + (diffs[5] + diffs[6])
    my = diffs[1] + (diffs[3] - diffs[4]) + (diffs[7] + diffs[8])
    mz = diffs[2] + (diffs[5] - diffs[6]) + (diffs[7] - diffs[8])
    return sums, diffs, density, mx, my, mz


def analyse(f):
    sums, diffs, density, mx, my, mz = moments(f)
    inverse = 1.0 / density
    ux, uy, uz = mx * inverse, my * inverse, mz * inverse
    square = ux * ux + uy * uy + uz * uz
    base = 1.0 - 1.5 * square
    projections = (ux, uy, uz, ux + uy, ux - uy, ux + uz, ux - uz, uy + uz, uy - uz)
    scale_axis = density * (2.0 / 18.0)
    scale_diag = density * (2.0 / 36.0)
    even, odd = [], []
    for k, e in enumerate(projections):
        scale = scale_axis if k < 3 else scale_diag
        even.append(sums[k] - scale * (base + 4.5 * (e * e)))
        odd.append(diffs[k] - scale * (3.0 * e))
    pxx = even[0] + (even[3] + even[4]) + (even[5] + even[6])
    pyy = even[1] + (even[3] + even[4]) + (even[7] + even[8])
    pzz = even[2] + (even[5] + even[6]) + (even[7] + even[8])
    pxy = even[3] - even[4]
    pxz = even[5] - even[6]
    pyz = even[7] - even[8]
    contracted = pxx * pxx + pyy * pyy + pzz * pzz + 2.0 * (pxy * pxy + pxz * pxz + pyz * pyz)
    shear = (1.5 / TAU_ZERO) * inverse * jnp.sqrt(2.0 * contracted + 1e-10)
    return density, base, square, even, odd, shear


def collide(f):
    density, base, _, even, odd, shear = analyse(f)
    scaled = LAMBDA_TIME * shear
    factor = jnp.exp(((POWER_INDEX - 1.0) / 2.0) * jnp.log(1.0 + scaled * scaled))
    tau = 3.0 * (NU_INFINITY + (NU_ZERO - NU_INFINITY) * factor) + 0.5
    omega = 1.0 / tau
    half = 0.5 * omega
    out = [None] * 19
    out[0] = f[0] - omega * (f[0] - (density * (1.0 / 3.0)) * base)
    for k, (a, b) in enumerate(PAIRS):
        s, d = half * even[k], half * odd[k]
        out[a] = f[a] - (s + d)
        out[b] = f[b] - (s - d)
    return out


def kernel(
    pops, mask, tag, table, adv, image,
    pbuf, r1, r2, ysend, yrecv, csend, crecv, bins, cbuf, ssend, srecv, wcols, wrows, vbuf,
    acc, xrecv, pieces, gathered, fsend, frecv,
    in_sem, out_sem, hs_sem, hr_sem, c_send_sem, c_recv_sem, x_sem, g_send_sem, g_recv_sem, f_send_sem, f_recv_sem,
):
    d = lax.axis_index("depth")
    r = lax.axis_index("rows")
    core = lax.rem(d, 2)
    chip = d // 2
    up_d, down_d = lax.rem(d + 1, ND), lax.rem(d + ND - 1, ND)
    up_r, down_r = lax.rem(r + 1, NR), lax.rem(r + NR - 1, NR)

    def at(dd, rr):
        return {"depth": dd, "rows": rr}

    loads = [pltpu.make_async_copy(pops.at[:, z], pbuf.at[:, z], in_sem.at[z]) for z in range(NZL)]
    for z in (0, 5, 1, 2, 3, 4):
        loads[z].start()

    barrier = pltpu.get_barrier_semaphore()
    peers = [at(up_d, r), at(down_d, r), at(up_d, up_r), at(up_d, down_r), at(down_d, up_r), at(down_d, down_r)]
    peers += [at(d, lax.rem(r + k, NR)) for k in range(1, NR)]
    peers += [at(lax.rem(d + 2 * k, ND), r) for k in range(1, NC)]
    peers += [at(d + 1 - 2 * core, r)]
    for peer in peers:
        pl.semaphore_signal(barrier, inc=1, device_id=peer, device_id_type=MESH)

    lane = lax.broadcasted_iota(jnp.int32, (8, 128), 1)
    first_lane, last_lane = lane == 0, lane == 127

    jj = lax.broadcasted_iota(jnp.int32, (128, 96), 0).astype(F32)
    yy = lax.broadcasted_iota(jnp.int32, (128, 96), 1)
    yy = (jnp.where(yy >= 48, yy - 48, yy) - 8).astype(F32)
    wcols[...] = jnp.maximum(0.0, 1.0 - jnp.abs((jj + 0.5) * 0.25 - 0.5 - yy)).astype(BF16)

    def fill_rows(b, carry):
        rho = b * 16 + lax.broadcasted_iota(jnp.int32, (16, NX), 0)
        which = rho & 15
        ii = (which >> 2) * 128 + (((rho >> 4) & 15) * 2 + (rho >> 8)) * 4 + (which & 3)
        xx = lax.broadcasted_iota(jnp.int32, (16, NX), 1).astype(F32)
        wt = jnp.maximum(0.0, 1.0 - jnp.abs((ii.astype(F32) + 0.5) * 0.5 - 0.5 - xx))
        wrows[pl.ds(pl.multiple_of(b * 16, 16), 16), :] = wt.astype(BF16)
        return carry

    lax.fori_loop(0, IMG // 16, fill_rows, 0)

    for k in range(4):
        for c in range(4):
            now = [jnp.broadcast_to(table[k, c:c + 1, h * 128:(h + 1) * 128], (8, 128)) for h in range(2)]
            turned = [pltpu.roll(half, 127, 1) for half in now]
            following = (jnp.where(last_lane, turned[1], turned[0]), jnp.where(last_lane, now[1], turned[1]))
            for h in range(2):
                bins[k, c, 0, h] = now[h]
                bins[k, c, 1, h] = following[h]

    def clear(z, carry):
        for c in range(4):
            cbuf[c, z, 0:8, :] = jnp.zeros((8, NX), F32)
            cbuf[c, z, 40:48, :] = jnp.zeros((8, NX), F32)
        return carry

    lax.fori_loop(0, NZL, clear, 0)

    def fluid_tiles(z, t):
        rows = pl.ds(pl.multiple_of(8 * t, 8), 8)
        return [mask[z, rows, h * 128:(h + 1) * 128] > 0 for h in range(2)]

    def store_relaxed(target, z, t, h, fluid, relaxed):
        rows = pl.ds(pl.multiple_of(8 * t + 8, 8), 8)
        for q in range(19):
            target[POS[q], z + 1, h, rows, :] = jnp.where(fluid, relaxed[q], WALL)

    def first_tile(z, t):
        rows = pl.ds(pl.multiple_of(8 * t, 8), 8)
        fluids = fluid_tiles(z, t)
        for h in range(2):
            f = [pbuf[q, z, rows, h * 128:(h + 1) * 128] for q in range(19)]
            store_relaxed(r1, z, t, h, fluids[h], collide(f))

    def arrive(source, z, t):
        own = pl.ds(pl.multiple_of(8 * t + 8, 8), 8)
        out = [[None] * 19, [None] * 19]
        for q in range(19):
            cx, cy, cz = VELOCITIES[q]
            if q == 0:
                for h in range(2):
                    out[h][0] = source[POS[0], z + 1, h, own, :]
                continue
            rows = own if cy == 0 else pl.ds(8 * t + 8 - cy, 8)
            a = [source[POS[q], z + 1 - cz, h, rows, :] for h in range(2)]
            if cx == 1:
                b0, b1 = pltpu.roll(a[0], 1, 1), pltpu.roll(a[1], 1, 1)
                a = [jnp.where(first_lane, WALL, b0), jnp.where(first_lane, b0, b1)]
            elif cx == -1:
                b0, b1 = pltpu.roll(a[0], 127, 1), pltpu.roll(a[1], 127, 1)
                a = [jnp.where(last_lane, b1, b0), jnp.where(last_lane, WALL, b1)]
            for h in range(2):
                back = source[POS[OPPOSITE[q]], z + 1, h, own, :]
                out[h][q] = jnp.where(a[h] > WALL_LIMIT, a[h], back)
        return out

    def second_tile(z, t):
        fluids = fluid_tiles(z, t)
        f = arrive(r1, z, t)
        for h in range(2):
            store_relaxed(r2, z, t, h, fluids[h], collide(f[h]))

    def lookup(c, after, low, upper, tags):
        picked = []
        for k in range(4):
            a = jnp.take_along_axis(bins[k, c, after, 0], low, axis=1, mode="promise_in_bounds")
            b = jnp.take_along_axis(bins[k, c, after, 1], low, axis=1, mode="promise_in_bounds")
            picked.append(jnp.where(upper, b, a))
        return jnp.where(
            tags[0], jnp.where(tags[1], picked[3], picked[2]), jnp.where(tags[1], picked[1], picked[0])
        )

    def third_tile(z, t):
        fluids = fluid_tiles(z, t)
        rows = pl.ds(pl.multiple_of(8 * t, 8), 8)
        padded = pl.ds(pl.multiple_of(8 * t + 8, 8), 8)
        f = arrive(r2, z, t)
        for h in range(2):
            lanes = slice(h * 128, (h + 1) * 128)
            fluid = fluids[h]
            for q in range(19):
                pbuf[q, z, rows, lanes] = jnp.where(fluid, f[h][q], pbuf[q, z, rows, lanes])
            _, _, square, _, _, shear = analyse(f[h])
            speed = jnp.sqrt(square + 1e-12)
            tags = tag[z, rows, lanes]
            tags = (tags >= 2, (tags & 1) == 1)
            place = []
            for value, scale in ((speed, SPEED_SCALE), (shear, SHEAR_SCALE)):
                where = 255.0 * (value / (value + scale))
                where = jnp.where(fluid, where, 0.0)
                bin_number = jnp.clip(where.astype(jnp.int32), 0, 255)
                place.append((where - bin_number.astype(F32), bin_number & 127, bin_number >= 128))
            result = []
            for c in range(4):
                share, low, upper = place[1 if c == 3 else 0]
                here = lookup(c, 0, low, upper, tags)
                after = lookup(c, 1, low, upper, tags)
                result.append(here + share * (after - here))
            coverage = jnp.where(fluid, result[3] * (3.0 / (NZL * ND)), 0.0)
            for c in range(3):
                cbuf[c, z, padded, lanes] = result[c] * coverage
            cbuf[3, z, padded, lanes] = coverage

    def tiles(count, body, z_of, t_of):
        def step(i, carry):
            body(z_of(i), t_of(i))
            return carry

        lax.fori_loop(0, count, step, 0)

    def remote(src, dst, send, recv, target):
        return pltpu.make_async_remote_copy(
            src_ref=src, dst_ref=dst, send_sem=send, recv_sem=recv, device_id=target, device_id_type=MESH
        )

    def halo_copies(s, rel):
        layers = [
            remote(rel.at[UP_Z:UP_Z + 5, 6, :, 8:40, :], rel.at[UP_Z:UP_Z + 5, 0, :, 8:40, :],
                   hs_sem.at[s, 0], hr_sem.at[s, 0], at(up_d, r)),
            remote(rel.at[DOWN_Z:DOWN_Z + 5, 1, :, 8:40, :], rel.at[DOWN_Z:DOWN_Z + 5, 7, :, 8:40, :],
                   hs_sem.at[s, 1], hr_sem.at[s, 1], at(down_d, r)),
        ]
        rows = [
            remote(ysend.at[s, 0], yrecv.at[s, 0], hs_sem.at[s, 2], hr_sem.at[s, 2], at(d, up_r)),
            remote(ysend.at[s, 1], yrecv.at[s, 1], hs_sem.at[s, 3], hr_sem.at[s, 3], at(d, down_r)),
        ]
        corners = [
            remote(csend.at[s, n], crecv.at[s, n], hs_sem.at[s, 4 + n], hr_sem.at[s, 4 + n], at(dd, rr))
            for n, (dd, rr) in enumerate(((up_d, up_r), (down_d, down_r), (down_d, up_r), (up_d, down_r)))
        ]
        return layers, rows, corners

    corner_places = ((15, 6, 39, 0, 7), (16, 1, 8, 7, 40), (17, 1, 39, 7, 7), (18, 6, 8, 0, 40))

    def pack_corners(s, rel):
        for n, (q, layer, row, _, _) in enumerate(corner_places):
            for h in range(2):
                csend[s, n, h:h + 1, :] = rel[POS[q], layer, h, row:row + 1, :]

    def pack_rows(s, rel):
        def step(z, carry):
            for side, (slots, row) in enumerate(((UP_Y, 39), (DOWN_Y, 8))):
                for n, slot in enumerate(slots):
                    for h in range(2):
                        ysend[s, side, z, 2 * n + h:2 * n + h + 1, :] = rel[slot, z + 1, h, row:row + 1, :]
            return carry

        lax.fori_loop(0, NZL, step, 0)

    def unpack_rows(s, rel):
        def step(z, carry):
            for side, (slots, row, edge) in enumerate(((UP_Y, 7, r == 0), (DOWN_Y, 40, r == NR - 1))):
                for n, slot in enumerate(slots):
                    for h in range(2):
                        rel[slot, z + 1, h, row:row + 1, :] = jnp.where(
                            edge, WALL, yrecv[s, side, z, 2 * n + h:2 * n + h + 1, :]
                        )
            return carry

        lax.fori_loop(0, NZL, step, 0)

    def unpack_layers(s, rel):
        @pl.when(d == 0)
        def _():
            rel[UP_Z:UP_Z + 5, 0] = jnp.full((5, 2, 48, 128), WALL, F32)

        @pl.when(d == ND - 1)
        def _():
            rel[DOWN_Z:DOWN_Z + 5, 7] = jnp.full((5, 2, 48, 128), WALL, F32)

        edges = (
            (d == 0) | (r == 0), (d == ND - 1) | (r == NR - 1), (d == ND - 1) | (r == 0), (d == 0) | (r == NR - 1)
        )
        for n, (q, _, _, layer, row) in enumerate(corner_places):
            for h in range(2):
                rel[POS[q], layer, h, row:row + 1, :] = jnp.where(edges[n], WALL, crecv[s, n, h:h + 1, :])

    loads[0].wait()
    loads[5].wait()
    tiles(8, first_tile, lambda i: (i // 4) * 5, lambda i: lax.rem(i, 4))
    pack_corners(0, r1)
    pl.semaphore_wait(barrier, len(peers))
    layers1, rows1, corners1 = halo_copies(0, r1)
    for copy in layers1 + corners1:
        copy.start()
    for z in range(1, 5):
        loads[z].wait()
    tiles(16, first_tile, lambda i: 1 + i // 4, lambda i: lax.rem(i, 4))
    pack_rows(0, r1)
    for copy in rows1:
        copy.start()

    tiles(8, second_tile, lambda i: 1 + i // 2, lambda i: 1 + lax.rem(i, 2))
    for copy in rows1:
        copy.wait()
    unpack_rows(0, r1)
    tiles(8, second_tile, lambda i: 1 + i // 2, lambda i: 3 * lax.rem(i, 2))
    for copy in layers1 + corners1:
        copy.wait()
    unpack_layers(0, r1)
    tiles(8, second_tile, lambda i: (i // 4) * 5, lambda i: lax.rem(i, 4))
    layers2, rows2, corners2 = halo_copies(1, r2)
    pack_corners(1, r2)
    for copy in layers2 + corners2:
        copy.start()
    pack_rows(1, r2)
    for copy in rows2:
        copy.start()

    tiles(8, third_tile, lambda i: 1 + i // 2, lambda i: 1 + lax.rem(i, 2))
    for copy in rows2:
        copy.wait()
    unpack_rows(1, r2)
    tiles(8, third_tile, lambda i: 1 + i // 2, lambda i: 3 * lax.rem(i, 2))
    for copy in layers2 + corners2:
        copy.wait()
    unpack_layers(1, r2)
    tiles(8, third_tile, lambda i: (i // 4) * 5, lambda i: lax.rem(i, 4))
    stores = [pltpu.make_async_copy(pbuf.at[:, z], adv.at[:, z], out_sem.at[z]) for z in range(NZL)]
    for copy in stores:
        copy.start()

    site_copies = []
    for side, row in enumerate((39, 8)):
        for z in range(NZL):
            for c in range(4):
                place = (z % 2) * 4 + c
                ssend[side, z // 2, place:place + 1, :] = cbuf[c, z, row:row + 1, :]
    for side, target in enumerate((at(d, up_r), at(d, down_r))):
        site_copies.append(remote(ssend.at[side], srecv.at[side], c_send_sem.at[side], c_recv_sem.at[side], target))
        site_copies[-1].start()
    for copy in site_copies:
        copy.wait()
    for side, (row, edge) in enumerate(((7, r == 0), (40, r == NR - 1))):
        for z in range(NZL):
            for c in range(4):
                place = (z % 2) * 4 + c
                cbuf[c, z, row:row + 1, :] = jnp.where(edge, 0.0, srecv[side, z // 2, place:place + 1, :])

    def columns(z, carry):
        for c in range(4):
            sites = cbuf[c, z]
            high = sites.astype(BF16)
            low = (sites - high.astype(F32)).astype(BF16)
            wide = lax.dot_general(
                wcols[...], jnp.concatenate([high, low], axis=0), (((1,), (0,)), ((), ())),
                preferred_element_type=F32,
            )
            high = wide.astype(BF16)
            low = (wide - high.astype(F32)).astype(BF16)
            place = slice((c % 2) * 128, (c % 2) * 128 + 128)
            vbuf[z, c // 2, 0, place, :] = high
            vbuf[z, c // 2, 1, place, :] = low
        return carry

    lax.fori_loop(0, NZL, columns, 0)

    def render(slot, which):
        weights = wrows[pl.ds(pl.multiple_of(which * 256, 256), 256), :]
        acc[slot] = jnp.zeros((4, 256, 128), F32)

        def layer(z, carry):
            drawn = []
            for pair in range(2):
                parts = [
                    lax.dot_general(
                        weights, vbuf[z, pair, n], (((1,), (1,)), ((), ())), preferred_element_type=F32
                    )
                    for n in range(2)
                ]
                drawn.append(parts[0] + parts[1])
            through = 1.0 - acc[slot, 3]
            for c in range(4):
                part = drawn[c // 2][:, (c % 2) * 128:(c % 2) * 128 + 128]
                acc[slot, c] = acc[slot, c] + through * part
            return carry

        lax.fori_loop(0, NZL, layer, 0)

    partner = at(d + 1 - 2 * core, r)
    render(0, 1 - core)
    swap = remote(acc.at[0], xrecv, x_sem.at[0], x_sem.at[1], partner)
    swap.start()
    render(1, core)
    swap.wait()

    def join(n, carry):
        rows = pl.ds(pl.multiple_of(n * 16, 16), 16)
        front = core == 0
        mine = [acc[1, c, rows, :] for c in range(4)]
        theirs = [xrecv[c, rows, :] for c in range(4)]
        near = [jnp.where(front, mine[c], theirs[c]) for c in range(4)]
        far = [jnp.where(front, theirs[c], mine[c]) for c in range(4)]
        through = 1.0 - near[3]
        for c in range(4):
            pieces[n, c] = near[c] + through * far[c]
        return carry

    lax.fori_loop(0, NC, join, 0)

    exchange = []
    for k in range(1, NC):
        other = lax.rem(chip + k, NC)
        exchange.append(
            remote(pieces.at[other], gathered.at[chip], g_send_sem.at[k], g_recv_sem.at[k], at(2 * other + core, r))
        )
        exchange[-1].start()
    gathered[chip] = pieces[chip]
    for copy in exchange:
        copy.wait()

    def over(n, carry):
        through = 1.0 - carry[3]
        return tuple(carry[c] + through * gathered[n, c] for c in range(4))

    final = lax.fori_loop(1, NC, over, tuple(gathered[0, c] for c in range(4)))

    for rr in range(NR):
        for c in range(4):
            fsend[rr, 4 * c:4 * c + 4, :] = final[c][4 * rr:4 * rr + 4, :]
    last = []
    for k in range(1, NR):
        other = lax.rem(r + k, NR)
        last.append(remote(fsend.at[other], frecv.at[r], f_send_sem.at[k], f_recv_sem.at[k], at(d, other)))
        last[-1].start()
    frecv[r] = fsend[r]
    for copy in last:
        copy.wait()
    for rr in range(NR):
        for c in range(4):
            image[c, :, rr * 128:(rr + 1) * 128] = frecv[rr, 4 * c:4 * c + 4, :]
    for copy in stores:
        copy.wait()


def shards(populations, fluid_mask, tissue_tag, colour_table):
    dma = pltpu.SemaphoreType.DMA
    vmem = pl.BlockSpec(memory_space=pltpu.VMEM)
    anywhere = pl.BlockSpec(memory_space=pl.ANY)
    return pl.pallas_call(
        kernel,
        out_shape=(
            jax.ShapeDtypeStruct(populations.shape, F32),
            jax.ShapeDtypeStruct((4, IMG // (ND * NR), IMG), F32),
        ),
        in_specs=[anywhere, vmem, vmem, vmem],
        out_specs=(anywhere, vmem),
        scratch_shapes=[
            pltpu.VMEM((NQ, NZL, NYL, NX), F32),
            pltpu.VMEM((NQ, NZL + 2, 2, 48, 128), F32),
            pltpu.VMEM((NQ, NZL + 2, 2, 48, 128), F32),
            pltpu.VMEM((2, 2, NZL, 16, 128), F32),
            pltpu.VMEM((2, 2, NZL, 16, 128), F32),
            pltpu.VMEM((2, 4, 8, 128), F32),
            pltpu.VMEM((2, 4, 8, 128), F32),
            pltpu.VMEM((4, 4, 2, 2, 8, 128), F32),
            pltpu.VMEM((4, NZL, 48, NX), F32),
            pltpu.VMEM((2, 3, 8, NX), F32),
            pltpu.VMEM((2, 3, 8, NX), F32),
            pltpu.VMEM((128, 96), BF16),
            pltpu.VMEM((IMG, NX), BF16),
            pltpu.VMEM((NZL, 2, 2, 256, NX), BF16),
            pltpu.VMEM((2, 4, 256, 128), F32),
            pltpu.VMEM((4, 256, 128), F32),
            pltpu.VMEM((NC, 4, 16, 128), F32),
            pltpu.VMEM((NC, 4, 16, 128), F32),
            pltpu.VMEM((NR, 16, 128), F32),
            pltpu.VMEM((NR, 16, 128), F32),
            dma((NZL,)), dma((NZL,)), dma((2, 8)), dma((2, 8)), dma((2,)), dma((2,)), dma((2,)),
            dma((NC,)), dma((NC,)), dma((NR,)), dma((NR,)),
        ],
        compiler_params=pltpu.CompilerParams(
            collective_id=0, has_side_effects=True, vmem_limit_bytes=56 * 2**20
        ),
        name="vessel",
    )(populations, fluid_mask, tissue_tag, colour_table)


def solution(mesh):
    placed = (
        P(None, "depth", "rows", None),
        P("depth", "rows", None),
        P("depth", "rows", None),
        P(),
    )
    return jax.shard_map(
        shards,
        mesh=mesh,
        in_specs=placed,
        out_specs=(P(None, "depth", "rows", None), P(None, ("rows", "depth"), None)),
        check_vma=False,
    )
```

```python
import functools

import jax
import jax.numpy as jnp
from jax import lax
from jax.experimental import pallas as pl
from jax.experimental.pallas import tpu as pltpu
from jax.sharding import PartitionSpec as P

F32 = jnp.float32
BF16 = jnp.bfloat16
MESH = pl.DeviceIdType.MESH

VELOCITIES = (
    (0, 0, 0), (1, 0, 0), (-1, 0, 0), (0, 1, 0), (0, -1, 0), (0, 0, 1), (0, 0, -1),
    (1, 1, 0), (-1, -1, 0), (1, -1, 0), (-1, 1, 0),
    (1, 0, 1), (-1, 0, -1), (1, 0, -1), (-1, 0, 1),
    (0, 1, 1), (0, -1, -1), (0, 1, -1), (0, -1, 1),
)
OPPOSITE = (0, 2, 1, 4, 3, 6, 5, 8, 7, 10, 9, 12, 11, 14, 13, 16, 15, 18, 17)
PAIRS = tuple((q, q + 1) for q in range(1, 19, 2))
NU_ZERO = 0.12
NU_INFINITY = 0.02
LAMBDA_TIME = 15.0
POWER_INDEX = 0.3568
TAU_ZERO = 0.8
SPEED_SCALE = 0.04
SHEAR_SCALE = 0.07

ORDER = (16, 6, 12, 13, 17, 3, 7, 10, 15, 5, 11, 14, 18, 4, 8, 9, 0, 1, 2)
POS = tuple(ORDER.index(q) for q in range(19))
UP_Z, DOWN_Z = 8, 0
UP_Y = (4, 5, 6, 7, 8)
DOWN_Y = (12, 13, 14, 15, 0)
WALL = -1e30
WALL_REST = (-1e8, -1e12)
LIMIT = -1e5

NQ, NZL, NYL, NX = 19, 6, 32, 256
ND, NR, NC = 32, 4, 16
IMG = 512


def analyse(f, fluid=None, wall=None):
    sums = [f[a] + f[b] for a, b in PAIRS]
    diffs = [f[a] - f[b] for a, b in PAIRS]
    density = ((f[0] + sums[0]) + (sums[1] + sums[2])) + (
        ((sums[3] + sums[4]) + (sums[5] + sums[6])) + (sums[7] + sums[8])
    )
    mx = diffs[0] + ((diffs[3] + diffs[4]) + (diffs[5] + diffs[6]))
    my = diffs[1] + ((diffs[3] - diffs[4]) + (diffs[7] + diffs[8]))
    mz = diffs[2] + ((diffs[5] - diffs[6]) + (diffs[7] - diffs[8]))
    inverse = 1.0 / density
    third = (mx * (1.0 / 3.0), my * (1.0 / 3.0), mz * (1.0 / 3.0))
    hx, hy, hz = (0.5 * q for q in third)
    squares = [q * q for q in third]
    total = squares[0] + squares[1] + squares[2]
    axis_scale = 4.5 * inverse
    diag_scale = 9.0 * inverse
    rest = density - 3.0 * (total * axis_scale)
    if wall is not None:
        rest = jnp.where(fluid, rest, wall)
    axis_rest, diag_rest = rest * (1.0 / 9.0), rest * (1.0 / 18.0)
    diag = (hx + hy, hx - hy, hx + hz, hx - hz, hy + hz, hy - hz)
    even = [(sums[k] - axis_rest) - axis_scale * squares[k] for k in range(3)]
    even += [(sums[3 + k] - diag_rest) - diag_scale * (diag[k] * diag[k]) for k in range(6)]
    odd = [diffs[k] - third[k] for k in range(3)] + [diffs[3 + k] - diag[k] for k in range(6)]
    pxx = even[0] + ((even[3] + even[4]) + (even[5] + even[6]))
    pyy = even[1] + ((even[3] + even[4]) + (even[7] + even[8]))
    pzz = even[2] + ((even[5] + even[6]) + (even[7] + even[8]))
    pxy = even[3] - even[4]
    pxz = even[5] - even[6]
    pyz = even[7] - even[8]
    contracted = (pxx * pxx + pyy * pyy + pzz * pzz) + 2.0 * (pxy * pxy + pxz * pxz + pyz * pyz)
    return inverse, total, rest, even, odd, 2.0 * contracted + 1e-10


def collide(f, fluid, wall):
    inverse, _, rest, even, odd, stress = analyse(f, fluid, wall)
    squared = ((LAMBDA_TIME * 1.5 / TAU_ZERO) ** 2) * ((inverse * inverse) * stress)
    factor = jnp.exp(((POWER_INDEX - 1.0) / 2.0) * jnp.log(1.0 + squared))
    half = 1.0 / ((6.0 * NU_INFINITY + 1.0) + (6.0 * (NU_ZERO - NU_INFINITY)) * factor)
    out = [None] * 19
    out[0] = f[0] - (half + half) * (f[0] - rest * (1.0 / 3.0))
    for k, (a, b) in enumerate(PAIRS):
        s, d = half * even[k], half * odd[k]
        out[a] = f[a] - (s + d)
        out[b] = f[b] - (s - d)
    return out


def diagnose(f):
    inverse, total, _, _, _, stress = analyse(f)
    square = (9.0 * total) * (inverse * inverse) + 1e-12
    speed = square * lax.rsqrt(square)
    shear = (1.5 / TAU_ZERO) * inverse * (stress * lax.rsqrt(stress))
    return speed, shear


def kernel(
    pops, mask_in, tag_in, table, pbuf, image,
    mask, tag, r1, r2, ysend, yrecv, csend, crecv, bins, cbuf, ssend, srecv, wcols, wrows, vbuf,
    acc, xrecv, pieces, gathered, fsend, frecv,
    in_sem, hs_sem, hr_sem, c_send_sem, c_recv_sem, x_sem, g_send_sem, g_recv_sem, f_send_sem, f_recv_sem,
):
    d = lax.axis_index("depth")
    r = lax.axis_index("rows")
    core = lax.rem(d, 2)
    chip = d // 2
    up_d, down_d = lax.rem(d + 1, ND), lax.rem(d + ND - 1, ND)
    up_r, down_r = lax.rem(r + 1, NR), lax.rem(r + NR - 1, NR)

    def at(dd, rr):
        return {"depth": dd, "rows": rr}

    barrier = pltpu.get_barrier_semaphore()
    peers = [at(up_d, r), at(down_d, r), at(up_d, up_r), at(up_d, down_r), at(down_d, up_r), at(down_d, down_r)]
    peers += [at(d, lax.rem(r + k, NR)) for k in range(1, NR)]
    peers += [at(lax.rem(d + 2 * k, ND), r) for k in range(1, NC)]
    peers += [at(d + 1 - 2 * core, r)]
    for peer in peers:
        pl.semaphore_signal(barrier, inc=1, device_id=peer, device_id_type=MESH)

    loads = [pltpu.make_async_copy(pops.at[:, z], pbuf.at[:, z], in_sem.at[z]) for z in range(NZL)]
    loads.append(pltpu.make_async_copy(mask_in, mask, in_sem.at[NZL]))
    loads.append(pltpu.make_async_copy(tag_in, tag, in_sem.at[NZL + 1]))
    for n in (NZL, 0, 5, 1, 2, 3, 4, NZL + 1):
        loads[n].start()

    lane = lax.broadcasted_iota(jnp.int32, (8, 128), 1)
    first_lane, last_lane = lane == 0, lane == 127
    first_limit = jnp.where(first_lane, 1e30, LIMIT)
    last_limit = jnp.where(last_lane, 1e30, LIMIT)

    jj = lax.broadcasted_iota(jnp.int32, (128, 96), 0).astype(F32)
    yy = lax.broadcasted_iota(jnp.int32, (128, 96), 1)
    yy = (jnp.where(yy >= 48, yy - 48, yy) - 8).astype(F32)
    wcols[...] = jnp.maximum(0.0, 1.0 - jnp.abs((jj + 0.5) * 0.25 - 0.5 - yy)).astype(BF16)

    def fill_rows(b, carry):
        rho = b * 64 + lax.broadcasted_iota(jnp.int32, (64, 128), 0)
        ii = (
            (rho >> 8) * 256 + ((rho >> 2) & 1) * 128 + ((rho >> 3) & 15) * 8 + ((rho >> 7) & 1) * 4 + (rho & 3)
        ).astype(F32)
        centre = ii * 0.5 - 0.25
        for h in range(2):
            xx = (lax.broadcasted_iota(jnp.int32, (64, 128), 1) + h * 128).astype(F32)
            wt = jnp.maximum(0.0, 1.0 - jnp.abs(centre - xx)).astype(BF16)
            rows = pl.ds(pl.multiple_of(b * 64, 64), 64)
            wrows[rows, h * 128:(h + 1) * 128] = wt
            wrows[rows, 256 + h * 128:256 + (h + 1) * 128] = wt
        return carry

    lax.fori_loop(0, IMG // 64, fill_rows, 0)

    for k in range(4):
        for c in range(4):
            now = [jnp.broadcast_to(table[k, c:c + 1, h * 128:(h + 1) * 128], (8, 128)) for h in range(2)]
            turned = [pltpu.roll(half, 127, 1) for half in now]
            following = (jnp.where(last_lane, turned[1], turned[0]), jnp.where(last_lane, now[1], turned[1]))
            for h in range(2):
                bins[k, c, 0, h] = now[h]
                bins[k, c, 1, h] = following[h]

    def clear(z, carry):
        for c in range(4):
            cbuf[c, z, 0:8, :] = jnp.zeros((8, NX), F32)
            cbuf[c, z, 40:48, :] = jnp.zeros((8, NX), F32)
        return carry

    lax.fori_loop(0, NZL, clear, 0)

    def fluid_tiles(z, t):
        rows = pl.ds(pl.multiple_of(8 * t, 8), 8)
        return [mask[z, rows, h * 128:(h + 1) * 128] > 0 for h in range(2)]

    def store_relaxed(target, z, t, h, relaxed):
        rows = pl.ds(pl.multiple_of(8 * t + 8, 8), 8)
        for q in range(19):
            target[POS[q], z + 1, h, rows, :] = relaxed[q]

    def first_tile(z, t):
        rows = pl.ds(pl.multiple_of(8 * t, 8), 8)
        fluids = fluid_tiles(z, t)
        for h in range(2):
            f = [pbuf[q, z, rows, h * 128:(h + 1) * 128] for q in range(19)]
            store_relaxed(r1, z, t, h, collide(f, fluids[h], WALL_REST[0]))

    def arrive(source, z, t):
        own = pl.ds(pl.multiple_of(8 * t + 8, 8), 8)
        out = [[None] * 19, [None] * 19]
        for q in range(19):
            cx, cy, cz = VELOCITIES[q]
            if q == 0:
                for h in range(2):
                    out[h][0] = source[POS[0], z + 1, h, own, :]
                continue
            rows = own if cy == 0 else pl.ds(8 * t + 8 - cy, 8)
            a = [source[POS[q], z + 1 - cz, h, rows, :] for h in range(2)]
            limits = [LIMIT, LIMIT]
            if cx == 1:
                b0, b1 = pltpu.roll(a[0], 1, 1), pltpu.roll(a[1], 1, 1)
                a = [b0, jnp.where(first_lane, b0, b1)]
                limits[0] = first_limit
            elif cx == -1:
                b0, b1 = pltpu.roll(a[0], 127, 1), pltpu.roll(a[1], 127, 1)
                a = [jnp.where(last_lane, b1, b0), b1]
                limits[1] = last_limit
            for h in range(2):
                back = source[POS[OPPOSITE[q]], z + 1, h, own, :]
                out[h][q] = jnp.where(a[h] > limits[h], a[h], back)
        return out

    def second_tile(z, t):
        fluids = fluid_tiles(z, t)
        f = arrive(r1, z, t)
        for h in range(2):
            store_relaxed(r2, z, t, h, collide(f[h], fluids[h], WALL_REST[1]))

    def lookup(c, after, low, upper, tags):
        picked = []
        for k in range(4):
            a = jnp.take_along_axis(bins[k, c, after, 0], low, axis=1, mode="promise_in_bounds")
            b = jnp.take_along_axis(bins[k, c, after, 1], low, axis=1, mode="promise_in_bounds")
            picked.append(jnp.where(upper, b, a))
        return jnp.where(
            tags[0], jnp.where(tags[1], picked[3], picked[2]), jnp.where(tags[1], picked[1], picked[0])
        )

    def classify(z, t, places):
        rows = pl.ds(pl.multiple_of(8 * t, 8), 8)
        padded = pl.ds(pl.multiple_of(8 * t + 8, 8), 8)
        fluids = fluid_tiles(z, t)
        for h in range(2):
            lanes = slice(h * 128, (h + 1) * 128)
            tags = tag[z, rows, lanes]
            tags = (tags >= 2, (tags & 1) == 1)
            place = []
            for where in places[2 * h:2 * h + 2]:
                bin_number = jnp.clip(where.astype(jnp.int32), 0, 255)
                place.append((where - bin_number.astype(F32), bin_number & 127, bin_number >= 128))
            result = []
            for c in range(4):
                share, low, upper = place[1 if c == 3 else 0]
                here = lookup(c, 0, low, upper, tags)
                after = lookup(c, 1, low, upper, tags)
                result.append(here + share * (after - here))
            coverage = jnp.where(fluids[h], result[3] * (3.0 / (NZL * ND)), 0.0)
            for c in range(3):
                cbuf[c, z, padded, lanes] = result[c] * coverage
            cbuf[3, z, padded, lanes] = coverage

    def third_tile(z, t):
        fluids = fluid_tiles(z, t)
        rows = pl.ds(pl.multiple_of(8 * t, 8), 8)
        f = arrive(r2, z, t)
        places = []
        for h in range(2):
            lanes = slice(h * 128, (h + 1) * 128)
            for q in range(19):
                pbuf[q, z, rows, lanes] = jnp.where(fluids[h], f[h][q], pbuf[q, z, rows, lanes])
            for value, scale in zip(diagnose(f[h]), (SPEED_SCALE, SHEAR_SCALE)):
                places.append(jnp.where(fluids[h], 255.0 * (value / (value + scale)), 0.0))
        return tuple(places)

    def tiles(count, body, z_of, t_of):
        def step(i, carry):
            body(z_of(i), t_of(i))
            return carry

        lax.fori_loop(0, count, step, 0)

    def remote(src, dst, send, recv, target):
        return pltpu.make_async_remote_copy(
            src_ref=src, dst_ref=dst, send_sem=send, recv_sem=recv, device_id=target, device_id_type=MESH
        )

    def halo_copies(s, rel):
        layers = [
            remote(rel.at[UP_Z:UP_Z + 5, 6, :, 8:40, :], rel.at[UP_Z:UP_Z + 5, 0, :, 8:40, :],
                   hs_sem.at[s, 0], hr_sem.at[s, 0], at(up_d, r)),
            remote(rel.at[DOWN_Z:DOWN_Z + 5, 1, :, 8:40, :], rel.at[DOWN_Z:DOWN_Z + 5, 7, :, 8:40, :],
                   hs_sem.at[s, 1], hr_sem.at[s, 1], at(down_d, r)),
        ]
        rows = [
            remote(ysend.at[s, 0], yrecv.at[s, 0], hs_sem.at[s, 2], hr_sem.at[s, 2], at(d, up_r)),
            remote(ysend.at[s, 1], yrecv.at[s, 1], hs_sem.at[s, 3], hr_sem.at[s, 3], at(d, down_r)),
        ]
        corners = [
            remote(csend.at[s, n], crecv.at[s, n], hs_sem.at[s, 4 + n], hr_sem.at[s, 4 + n], at(dd, rr))
            for n, (dd, rr) in enumerate(((up_d, up_r), (down_d, down_r), (down_d, up_r), (up_d, down_r)))
        ]
        return layers, rows, corners

    corner_places = ((15, 6, 39, 0, 7), (16, 1, 8, 7, 40), (17, 1, 39, 7, 7), (18, 6, 8, 0, 40))

    def pack_corners(s, rel):
        for n, (q, layer, row, _, _) in enumerate(corner_places):
            for h in range(2):
                csend[s, n, h:h + 1, :] = rel[POS[q], layer, h, row:row + 1, :]

    def pack_rows(s, rel):
        def step(z, carry):
            for side, (slots, row) in enumerate(((UP_Y, 39), (DOWN_Y, 8))):
                for n, slot in enumerate(slots):
                    for h in range(2):
                        ysend[s, side, z, 2 * n + h:2 * n + h + 1, :] = rel[slot, z + 1, h, row:row + 1, :]
            return carry

        lax.fori_loop(0, NZL, step, 0)

    def unpack_rows(s, rel):
        def step(z, carry):
            for side, (slots, row, edge) in enumerate(((UP_Y, 7, r == 0), (DOWN_Y, 40, r == NR - 1))):
                for n, slot in enumerate(slots):
                    for h in range(2):
                        rel[slot, z + 1, h, row:row + 1, :] = jnp.where(
                            edge, WALL, yrecv[s, side, z, 2 * n + h:2 * n + h + 1, :]
                        )
            return carry

        lax.fori_loop(0, NZL, step, 0)

    def unpack_layers(s, rel):
        @pl.when(d == 0)
        def _():
            rel[UP_Z:UP_Z + 5, 0] = jnp.full((5, 2, 48, 128), WALL, F32)

        @pl.when(d == ND - 1)
        def _():
            rel[DOWN_Z:DOWN_Z + 5, 7] = jnp.full((5, 2, 48, 128), WALL, F32)

        edges = (
            (d == 0) | (r == 0), (d == ND - 1) | (r == NR - 1), (d == ND - 1) | (r == 0), (d == 0) | (r == NR - 1)
        )
        for n, (q, _, _, layer, row) in enumerate(corner_places):
            for h in range(2):
                rel[POS[q], layer, h, row:row + 1, :] = jnp.where(edges[n], WALL, crecv[s, n, h:h + 1, :])

    loads[NZL].wait()
    loads[0].wait()
    loads[5].wait()
    tiles(8, first_tile, lambda i: (i >> 2) * 5, lambda i: i & 3)
    pack_corners(0, r1)
    pl.semaphore_wait(barrier, len(peers))
    layers1, rows1, corners1 = halo_copies(0, r1)
    for copy in layers1 + corners1:
        copy.start()
    for z in range(1, 5):
        loads[z].wait()
    tiles(16, first_tile, lambda i: 1 + (i >> 2), lambda i: i & 3)
    pack_rows(0, r1)
    for copy in rows1:
        copy.start()

    tiles(8, second_tile, lambda i: 1 + (i >> 1), lambda i: 1 + (i & 1))
    for copy in rows1:
        copy.wait()
    unpack_rows(0, r1)
    tiles(8, second_tile, lambda i: 1 + (i >> 1), lambda i: 3 * (i & 1))
    for copy in layers1 + corners1:
        copy.wait()
    unpack_layers(0, r1)
    tiles(8, second_tile, lambda i: (i >> 2) * 5, lambda i: i & 3)
    layers2, rows2, corners2 = halo_copies(1, r2)
    pack_corners(1, r2)
    for copy in layers2 + corners2:
        copy.start()
    pack_rows(1, r2)
    for copy in rows2:
        copy.start()

    loads[NZL + 1].wait()

    def third_tiles(count, z_of, t_of, before, carry):
        def step(i, places):
            last = jnp.maximum(i - 1, 0)
            first = i == 0
            classify(
                jnp.where(first, before[0], z_of(last)), jnp.where(first, before[1], t_of(last)), places
            )
            return third_tile(z_of(i), t_of(i))

        return lax.fori_loop(0, count, step, carry)

    site_copies = [
        [
            remote(ssend.at[side, 2 * part:3 - (1 - part)], srecv.at[side, 2 * part:3 - (1 - part)], c_send_sem.at[part, side], c_recv_sem.at[part, side], target)
            for side, target in enumerate((at(d, up_r), at(d, down_r)))
        ]
        for part in range(2)
    ]
    places = tuple(jnp.zeros((8, 128), F32) for _ in range(4))
    places = third_tiles(8, lambda i: 1 + (i >> 1), lambda i: 1 + (i & 1), (1, 1), places)
    for copy in rows2:
        copy.wait()
    unpack_rows(1, r2)
    places = third_tiles(8, lambda i: 1 + (i >> 1), lambda i: 3 * (i & 1), (4, 2), places)
    for copy in layers2 + corners2:
        copy.wait()
    unpack_layers(1, r2)
    places = third_tiles(4, lambda i: (i >> 1) * 5, lambda i: 3 * (i & 1), (4, 3), places)

    def pack_sites(part, layers):
        for n, z in enumerate(layers):
            for side, row in enumerate((39, 8)):
                for c in range(4):
                    place = 4 * (n % 2) + c
                    ssend[side, 2 * part + n // 2, place:place + 1, :] = cbuf[c, z, row:row + 1, :]
        for copy in site_copies[part]:
            copy.start()

    def unpack_sites(part, layers):
        for copy in site_copies[part]:
            copy.wait()
        for n, z in enumerate(layers):
            for side, (row, edge) in enumerate(((7, r == 0), (40, r == NR - 1))):
                for c in range(4):
                    place = 4 * (n % 2) + c
                    cbuf[c, z, row:row + 1, :] = jnp.where(
                        edge, 0.0, srecv[side, 2 * part + n // 2, place:place + 1, :]
                    )

    pack_sites(0, (1, 2, 3, 4))
    places = third_tiles(4, lambda i: (i >> 1) * 5, lambda i: 1 + (i & 1), (5, 3), places)
    pack_sites(1, (0, 5))
    classify(5, 2, places)

    def columns(z):
        for c in range(4):
            sites = cbuf[c, z]
            high = sites.astype(BF16)
            low = (sites - high.astype(F32)).astype(BF16)
            wide = lax.dot_general(
                wcols[...], jnp.concatenate([high, low], axis=0), (((1,), (0,)), ((), ())),
                preferred_element_type=F32,
            )
            high = wide.astype(BF16)
            low = (wide - high.astype(F32)).astype(BF16)
            place = slice((c % 2) * 128, (c % 2) * 128 + 128)
            vbuf[z, c // 2, place, 0:NX] = high
            vbuf[z, c // 2, place, NX:2 * NX] = low

    def columns_step(i, carry):
        columns(i + 1)
        return carry

    unpack_sites(0, (1, 2, 3, 4))
    lax.fori_loop(0, 4, columns_step, 0)
    unpack_sites(1, (0, 5))

    def columns_outer(i, carry):
        columns(5 * i)
        return carry

    lax.fori_loop(0, 2, columns_outer, 0)

    def render(group, slot, which):
        weights = wrows[pl.ds(pl.multiple_of(group * 256 + which * 128, 128), 128), :]
        for z in range(NZL):
            drawn = [
                lax.dot_general(weights, vbuf[z, pair], (((1,), (1,)), ((), ())), preferred_element_type=F32)
                for pair in range(2)
            ]
            parts = [drawn[c // 2][:, (c % 2) * 128:(c % 2) * 128 + 128] for c in range(4)]
            if z == 0:
                for c in range(4):
                    acc[group, slot, c] = parts[c]
            else:
                through = 1.0 - acc[group, slot, 3]
                for c in range(4):
                    acc[group, slot, c] = acc[group, slot, c] + through * parts[c]

    partner = at(d + 1 - 2 * core, r)
    swaps = [
        remote(acc.at[group, 0], xrecv.at[group], x_sem.at[0, group], x_sem.at[1, group], partner)
        for group in range(2)
    ]
    exchange = [[], []]
    for group in range(2):
        for k in range(1, NC):
            other = lax.rem(chip + k, NC)
            exchange[group].append(
                remote(pieces.at[group, other], gathered.at[group, chip],
                       g_send_sem.at[group, k], g_recv_sem.at[group, k], at(2 * other + core, r))
            )

    def join(group):
        def step(n, carry):
            rows = pl.ds(pl.multiple_of(n * 8, 8), 8)
            front = core == 0
            mine = [acc[group, 1, c, rows, :] for c in range(4)]
            theirs = [xrecv[group, c, rows, :] for c in range(4)]
            near = [jnp.where(front, mine[c], theirs[c]) for c in range(4)]
            far = [jnp.where(front, theirs[c], mine[c]) for c in range(4)]
            through = 1.0 - near[3]
            for c in range(4):
                pieces[group, n, c] = near[c] + through * far[c]
            return carry

        lax.fori_loop(0, NC, step, 0, unroll=4)
        for copy in exchange[group]:
            copy.start()
        gathered[group, chip] = pieces[group, chip]

    render(0, 0, 1 - core)
    swaps[0].start()
    render(0, 1, core)
    render(1, 0, 1 - core)
    swaps[1].start()
    swaps[0].wait()
    join(0)
    render(1, 1, core)
    swaps[1].wait()
    join(1)

    for group in range(2):
        for copy in exchange[group]:
            copy.wait()
        final = [gathered[group, 0, c] for c in range(4)]
        for n in range(1, NC):
            through = 1.0 - final[3]
            final = [final[c] + through * gathered[group, n, c] for c in range(4)]
        for half in range(2):
            for c in range(4):
                fsend[2 * group + half, 4 * c:4 * c + 4, :] = final[c][4 * half:4 * half + 4, :]
    last = []
    for k in range(1, NR):
        other = lax.rem(r + k, NR)
        last.append(remote(fsend.at[other], frecv.at[r], f_send_sem.at[k], f_recv_sem.at[k], at(d, other)))
        last[-1].start()
    frecv[r] = fsend[r]
    for copy in last:
        copy.wait()
    for rr in range(NR):
        for c in range(4):
            image[c, :, rr * 128:(rr + 1) * 128] = frecv[rr, 4 * c:4 * c + 4, :]


def shards(populations, fluid_mask, tissue_tag, colour_table):
    dma = pltpu.SemaphoreType.DMA
    vmem = pl.BlockSpec(memory_space=pltpu.VMEM)
    anywhere = pl.BlockSpec(memory_space=pl.ANY)
    advanced, drawn = pl.pallas_call(
        kernel,
        out_shape=(
            pltpu.VMEM(populations.shape, F32),
            pltpu.VMEM((4, IMG // (ND * NR), IMG), F32),
        ),
        in_specs=[anywhere, anywhere, anywhere, vmem],
        out_specs=(vmem, vmem),
        scratch_shapes=[
            pltpu.VMEM((NZL, NYL, NX), jnp.int32),
            pltpu.VMEM((NZL, NYL, NX), jnp.int32),
            pltpu.VMEM((NQ, NZL + 2, 2, 48, 128), F32),
            pltpu.VMEM((NQ, NZL + 2, 2, 48, 128), F32),
            pltpu.VMEM((2, 2, NZL, 16, 128), F32),
            pltpu.VMEM((2, 2, NZL, 16, 128), F32),
            pltpu.VMEM((2, 4, 8, 128), F32),
            pltpu.VMEM((2, 4, 8, 128), F32),
            pltpu.VMEM((4, 4, 2, 2, 8, 128), F32),
            pltpu.VMEM((4, NZL, 48, NX), F32),
            pltpu.VMEM((2, 3, 8, NX), F32),
            pltpu.VMEM((2, 3, 8, NX), F32),
            pltpu.VMEM((128, 96), BF16),
            pltpu.VMEM((IMG, 2 * NX), BF16),
            pltpu.VMEM((NZL, 2, 256, 2 * NX), BF16),
            pltpu.VMEM((2, 2, 4, 128, 128), F32),
            pltpu.VMEM((2, 4, 128, 128), F32),
            pltpu.VMEM((2, NC, 4, 8, 128), F32),
            pltpu.VMEM((2, NC, 4, 8, 128), F32),
            pltpu.VMEM((NR, 16, 128), F32),
            pltpu.VMEM((NR, 16, 128), F32),
            dma((NZL + 2,)), dma((2, 8)), dma((2, 8)), dma((2, 2)), dma((2, 2)), dma((2, 2)),
            dma((2, NC)), dma((2, NC)), dma((NR,)), dma((NR,)),
        ],
        compiler_params=pltpu.CompilerParams(
            collective_id=0, has_side_effects=True, vmem_limit_bytes=56 * 2**20
        ),
        name="vessel",
    )(populations, fluid_mask, tissue_tag, colour_table)
    return pl.pallas_call(
        deliver,
        out_shape=(
            jax.ShapeDtypeStruct(populations.shape, F32),
            jax.ShapeDtypeStruct((4, IMG // (ND * NR), IMG), F32),
        ),
        in_specs=[vmem, vmem],
        out_specs=(anywhere, anywhere),
        scratch_shapes=[dma((NZL + 1,))],
        compiler_params=pltpu.CompilerParams(vmem_limit_bytes=2**20),
        name="deliver",
    )(advanced, drawn)


def deliver(advanced, drawn, adv, image, sem):
    copies = [pltpu.make_async_copy(advanced.at[:, z], adv.at[:, z], sem.at[z]) for z in range(NZL)]
    copies.append(pltpu.make_async_copy(drawn, image, sem.at[NZL]))
    for copy in copies:
        copy.start()
    for copy in copies:
        copy.wait()


def solution(mesh):
    placed = (
        P(None, "depth", "rows", None),
        P("depth", "rows", None),
        P("depth", "rows", None),
        P(),
    )
    return jax.shard_map(
        shards,
        mesh=mesh,
        in_specs=placed,
        out_specs=(P(None, "depth", "rows", None), P(None, ("rows", "depth"), None)),
        check_vma=False,
    )
```

```python
import functools

import jax
import jax.numpy as jnp
from jax import lax
from jax.experimental import pallas as pl
from jax.experimental.pallas import tpu as pltpu
from jax.sharding import PartitionSpec as P

F32 = jnp.float32
BF16 = jnp.bfloat16
MESH = pl.DeviceIdType.MESH

VELOCITIES = (
    (0, 0, 0), (1, 0, 0), (-1, 0, 0), (0, 1, 0), (0, -1, 0), (0, 0, 1), (0, 0, -1),
    (1, 1, 0), (-1, -1, 0), (1, -1, 0), (-1, 1, 0),
    (1, 0, 1), (-1, 0, -1), (1, 0, -1), (-1, 0, 1),
    (0, 1, 1), (0, -1, -1), (0, 1, -1), (0, -1, 1),
)
OPPOSITE = (0, 2, 1, 4, 3, 6, 5, 8, 7, 10, 9, 12, 11, 14, 13, 16, 15, 18, 17)
PAIRS = tuple((q, q + 1) for q in range(1, 19, 2))
NU_ZERO = 0.12
NU_INFINITY = 0.02
LAMBDA_TIME = 15.0
POWER_INDEX = 0.3568
TAU_ZERO = 0.8
SPEED_SCALE = 0.04
SHEAR_SCALE = 0.07

ORDER = (16, 6, 12, 13, 17, 3, 7, 10, 15, 5, 11, 14, 18, 4, 8, 9, 0, 1, 2)
POS = tuple(ORDER.index(q) for q in range(19))
UP_Z, DOWN_Z = 8, 0
UP_Y = (4, 5, 6, 7, 8)
DOWN_Y = (12, 13, 14, 15, 0)
WALL = -1e30
WALL_REST = (-1e8, -1e12)
LIMIT = -1e5

NQ, NZL, NYL, NX = 19, 6, 32, 256
ND, NR, NC = 32, 4, 16
IMG = 512


def analyse(f, fluid=None, wall=None):
    sums = [f[a] + f[b] for a, b in PAIRS]
    diffs = [f[a] - f[b] for a, b in PAIRS]
    density = ((f[0] + sums[0]) + (sums[1] + sums[2])) + (
        ((sums[3] + sums[4]) + (sums[5] + sums[6])) + (sums[7] + sums[8])
    )
    mx = diffs[0] + ((diffs[3] + diffs[4]) + (diffs[5] + diffs[6]))
    my = diffs[1] + ((diffs[3] - diffs[4]) + (diffs[7] + diffs[8]))
    mz = diffs[2] + ((diffs[5] - diffs[6]) + (diffs[7] - diffs[8]))
    inverse = 1.0 / density
    third = (mx * (1.0 / 3.0), my * (1.0 / 3.0), mz * (1.0 / 3.0))
    hx, hy, hz = (0.5 * q for q in third)
    squares = [q * q for q in third]
    total = squares[0] + squares[1] + squares[2]
    axis_scale = 4.5 * inverse
    diag_scale = 9.0 * inverse
    rest = density - 3.0 * (total * axis_scale)
    if wall is not None:
        rest = jnp.where(fluid, rest, wall)
    axis_rest, diag_rest = rest * (1.0 / 9.0), rest * (1.0 / 18.0)
    diag = (hx + hy, hx - hy, hx + hz, hx - hz, hy + hz, hy - hz)
    even = [(sums[k] - axis_rest) - axis_scale * squares[k] for k in range(3)]
    even += [(sums[3 + k] - diag_rest) - diag_scale * (diag[k] * diag[k]) for k in range(6)]
    odd = [diffs[k] - third[k] for k in range(3)] + [diffs[3 + k] - diag[k] for k in range(6)]
    pxx = even[0] + ((even[3] + even[4]) + (even[5] + even[6]))
    pyy = even[1] + ((even[3] + even[4]) + (even[7] + even[8]))
    pzz = even[2] + ((even[5] + even[6]) + (even[7] + even[8]))
    pxy = even[3] - even[4]
    pxz = even[5] - even[6]
    pyz = even[7] - even[8]
    contracted = (pxx * pxx + pyy * pyy + pzz * pzz) + 2.0 * (pxy * pxy + pxz * pxz + pyz * pyz)
    return inverse, total, rest, even, odd, 2.0 * contracted + 1e-10


def collide(f, fluid, wall):
    inverse, _, rest, even, odd, stress = analyse(f, fluid, wall)
    squared = ((LAMBDA_TIME * 1.5 / TAU_ZERO) ** 2) * ((inverse * inverse) * stress)
    factor = jnp.exp(((POWER_INDEX - 1.0) / 2.0) * jnp.log(1.0 + squared))
    half = 1.0 / ((6.0 * NU_INFINITY + 1.0) + (6.0 * (NU_ZERO - NU_INFINITY)) * factor)
    out = [None] * 19
    out[0] = f[0] - (half + half) * (f[0] - rest * (1.0 / 3.0))
    for k, (a, b) in enumerate(PAIRS):
        s, d = half * even[k], half * odd[k]
        out[a] = f[a] - (s + d)
        out[b] = f[b] - (s - d)
    return out


def diagnose(f):
    inverse, total, _, _, _, stress = analyse(f)
    square = (9.0 * total) * (inverse * inverse) + 1e-12
    speed = square * lax.rsqrt(square)
    shear = (1.5 / TAU_ZERO) * inverse * (stress * lax.rsqrt(stress))
    return speed, shear


def kernel(
    pops, mask_in, tag_in, table, pbuf, image,
    mask, tag, r1, r2, ysend, yrecv, csend, crecv, bins, cbuf, ssend, srecv, wcols, wrows, vbuf,
    acc, xrecv, pieces, gathered, fsend, frecv,
    in_sem, ls_sem, lr_sem, hs_sem, hr_sem, c_send_sem, c_recv_sem, x_sem, g_send_sem, g_recv_sem, f_send_sem, f_recv_sem,
):
    d = lax.axis_index("depth")
    r = lax.axis_index("rows")
    core = lax.rem(d, 2)
    chip = d // 2
    up_d, down_d = lax.rem(d + 1, ND), lax.rem(d + ND - 1, ND)
    up_r, down_r = lax.rem(r + 1, NR), lax.rem(r + NR - 1, NR)

    def at(dd, rr):
        return {"depth": dd, "rows": rr}

    barrier = pltpu.get_barrier_semaphore()
    chips = sorted(range(1, NC), key=lambda k: -min(k // 4, 4 - k // 4) - min(k % 4, 4 - k % 4))
    peers = [at(lax.rem(d + 2 * k, ND), r) for k in chips]
    peers += [at(up_d, up_r), at(up_d, down_r), at(down_d, up_r), at(down_d, down_r)]
    peers += [at(d, lax.rem(r + k, NR)) for k in (2, 1, 3)]
    peers += [at(up_d, r), at(down_d, r), at(d + 1 - 2 * core, r)]
    for peer in peers:
        pl.semaphore_signal(barrier, inc=1, device_id=peer, device_id_type=MESH)

    loads = [pltpu.make_async_copy(pops.at[:, z], pbuf.at[:, z], in_sem.at[z]) for z in range(NZL)]
    loads.append(pltpu.make_async_copy(mask_in, mask, in_sem.at[NZL]))
    loads.append(pltpu.make_async_copy(tag_in, tag, in_sem.at[NZL + 1]))
    for n in (NZL, 0, 5, 1, 2, 3, 4, NZL + 1):
        loads[n].start()

    lane = lax.broadcasted_iota(jnp.int32, (8, 128), 1)
    first_lane, last_lane = lane == 0, lane == 127
    first_limit = jnp.where(first_lane, 1e30, LIMIT)
    last_limit = jnp.where(last_lane, 1e30, LIMIT)

    jj = lax.broadcasted_iota(jnp.int32, (128, 96), 0).astype(F32)
    yy = lax.broadcasted_iota(jnp.int32, (128, 96), 1)
    yy = (jnp.where(yy >= 48, yy - 48, yy) - 8).astype(F32)
    wcols[...] = jnp.maximum(0.0, 1.0 - jnp.abs((jj + 0.5) * 0.25 - 0.5 - yy)).astype(BF16)

    def fill_rows(b, carry):
        rho = b * 64 + lax.broadcasted_iota(jnp.int32, (64, 128), 0)
        ii = (
            (rho >> 8) * 256 + ((rho >> 2) & 1) * 128 + ((rho >> 3) & 15) * 8 + ((rho >> 7) & 1) * 4 + (rho & 3)
        ).astype(F32)
        centre = ii * 0.5 - 0.25
        for h in range(2):
            xx = (lax.broadcasted_iota(jnp.int32, (64, 128), 1) + h * 128).astype(F32)
            wt = jnp.maximum(0.0, 1.0 - jnp.abs(centre - xx)).astype(BF16)
            rows = pl.ds(pl.multiple_of(b * 64, 64), 64)
            wrows[rows, h * 128:(h + 1) * 128] = wt
        return carry

    lax.fori_loop(0, IMG // 64, fill_rows, 0)

    low_lanes = lane < 64
    for k in range(4):
        for c in range(4):
            halves = [jnp.broadcast_to(table[k, c:c + 1, h * 128:(h + 1) * 128], (8, 128)) for h in range(2)]
            for parity in range(2):
                index = ((lane * 2) & 127) + parity
                taken = [jnp.take_along_axis(half, index, axis=1, mode="promise_in_bounds") for half in halves]
                bins[k, c, parity] = jnp.where(low_lanes, taken[0], taken[1])

    def clear(z, carry):
        for c in range(4):
            cbuf[c, z, 0:8, :] = jnp.zeros((8, NX), F32)
            cbuf[c, z, 40:48, :] = jnp.zeros((8, NX), F32)
        return carry

    lax.fori_loop(0, NZL, clear, 0)

    def fluid_tiles(z, t):
        rows = pl.ds(pl.multiple_of(8 * t, 8), 8)
        return [mask[z, rows, h * 128:(h + 1) * 128] > 0 for h in range(2)]

    def store_relaxed(target, z, t, h, relaxed):
        rows = pl.ds(pl.multiple_of(8 * t + 8, 8), 8)
        for q in range(19):
            target[POS[q], z + 1, h, rows, :] = relaxed[q]

    def first_tile(z, t):
        rows = pl.ds(pl.multiple_of(8 * t, 8), 8)
        fluids = fluid_tiles(z, t)
        for h in range(2):
            f = [pbuf[q, z, rows, h * 128:(h + 1) * 128] for q in range(19)]
            store_relaxed(r1, z, t, h, collide(f, fluids[h], WALL_REST[0]))

    def arrive(source, z, t):
        own = pl.ds(pl.multiple_of(8 * t + 8, 8), 8)
        out = [[None] * 19, [None] * 19]
        for q in range(19):
            cx, cy, cz = VELOCITIES[q]
            if q == 0:
                for h in range(2):
                    out[h][0] = source[POS[0], z + 1, h, own, :]
                continue
            rows = own if cy == 0 else pl.ds(8 * t + 8 - cy, 8)
            a = [source[POS[q], z + 1 - cz, h, rows, :] for h in range(2)]
            limits = [LIMIT, LIMIT]
            if cx == 1:
                b0, b1 = pltpu.roll(a[0], 1, 1), pltpu.roll(a[1], 1, 1)
                a = [b0, jnp.where(first_lane, b0, b1)]
                limits[0] = first_limit
            elif cx == -1:
                b0, b1 = pltpu.roll(a[0], 127, 1), pltpu.roll(a[1], 127, 1)
                a = [jnp.where(last_lane, b1, b0), b1]
                limits[1] = last_limit
            for h in range(2):
                back = source[POS[OPPOSITE[q]], z + 1, h, own, :]
                out[h][q] = jnp.where(a[h] > limits[h], a[h], back)
        return out

    def second_tile(z, t):
        fluids = fluid_tiles(z, t)
        f = arrive(r1, z, t)
        for h in range(2):
            store_relaxed(r2, z, t, h, collide(f[h], fluids[h], WALL_REST[1]))

    def lookup(c, parity, index, tags):
        picked = [
            jnp.take_along_axis(bins[k, c, parity], index, axis=1, mode="promise_in_bounds") for k in range(4)
        ]
        return jnp.where(
            tags[0], jnp.where(tags[1], picked[3], picked[2]), jnp.where(tags[1], picked[1], picked[0])
        )

    def classify(z, t, places):
        rows = pl.ds(pl.multiple_of(8 * t, 8), 8)
        padded = pl.ds(pl.multiple_of(8 * t + 8, 8), 8)
        fluids = fluid_tiles(z, t)
        for h in range(2):
            lanes = slice(h * 128, (h + 1) * 128)
            tags = tag[z, rows, lanes]
            tags = (tags >= 2, (tags & 1) == 1)
            place = []
            for where in places[2 * h:2 * h + 2]:
                lower = jnp.clip(where.astype(jnp.int32), 0, 254)
                even, odd = (lower + 1) >> 1, lower >> 1
                place.append((1.0 - jnp.abs(where - (even + even).astype(F32)), even, odd))
            result = []
            for (share, even, odd), channels in zip(place, ((0, 1, 2), (3,))):
                at_odd = [lookup(c, 1, odd, tags) for c in channels]
                at_even = [lookup(c, 0, even, tags) for c in channels]
                result += [a + share * (b - a) for a, b in zip(at_odd, at_even)]
            coverage = jnp.where(fluids[h], result[3] * (3.0 / (NZL * ND)), 0.0)
            for c in range(3):
                cbuf[c, z, padded, lanes] = result[c] * coverage
            cbuf[3, z, padded, lanes] = coverage

    def third_tile(z, t):
        fluids = fluid_tiles(z, t)
        rows = pl.ds(pl.multiple_of(8 * t, 8), 8)
        f = arrive(r2, z, t)
        places = []
        for h in range(2):
            lanes = slice(h * 128, (h + 1) * 128)
            for q in range(19):
                pbuf[q, z, rows, lanes] = jnp.where(fluids[h], f[h][q], pbuf[q, z, rows, lanes])
            for value, scale in zip(diagnose(f[h]), (SPEED_SCALE, SHEAR_SCALE)):
                places.append(jnp.where(fluids[h], 255.0 * (value / (value + scale)), 0.0))
        return tuple(places)

    def tiles(count, body, z_of, t_of):
        def step(i, carry):
            body(z_of(i), t_of(i))
            return carry

        lax.fori_loop(0, count, step, 0, unroll=4)

    def outer_tiles(body, after):
        def step(t, carry):
            body(5, t)
            body(0, t)
            if after is not None:
                @pl.when(t > 0)
                def _():
                    for copy in after(t - 1):
                        copy.start()
            return carry

        lax.fori_loop(0, 4, step, 0, unroll=2)

    def remote(src, dst, send, recv, target):
        return pltpu.make_async_remote_copy(
            src_ref=src, dst_ref=dst, send_sem=send, recv_sem=recv, device_id=target, device_id_type=MESH
        )

    def layer_copies(s, rel, t):
        rows = pl.ds(pl.multiple_of(8 * t + 8, 8), 8)
        return [
            remote(rel.at[UP_Z:UP_Z + 5, 6, :, rows, :], rel.at[UP_Z:UP_Z + 5, 0, :, rows, :],
                   ls_sem.at[s, 0, t], lr_sem.at[s, 0, t], at(up_d, r)),
            remote(rel.at[DOWN_Z:DOWN_Z + 5, 1, :, rows, :], rel.at[DOWN_Z:DOWN_Z + 5, 7, :, rows, :],
                   ls_sem.at[s, 1, t], lr_sem.at[s, 1, t], at(down_d, r)),
        ]

    def halo_copies(s, rel):
        rows = [
            remote(ysend.at[s, 0], yrecv.at[s, 0], hs_sem.at[s, 0], hr_sem.at[s, 0], at(d, up_r)),
            remote(ysend.at[s, 1], yrecv.at[s, 1], hs_sem.at[s, 1], hr_sem.at[s, 1], at(d, down_r)),
        ]
        corners = [
            remote(csend.at[s, n], crecv.at[s, n], hs_sem.at[s, 2 + n], hr_sem.at[s, 2 + n], at(dd, rr))
            for n, (dd, rr) in enumerate(((up_d, up_r), (down_d, down_r), (down_d, up_r), (up_d, down_r)))
        ]
        return rows, corners

    corner_places = ((15, 6, 39, 0, 7), (16, 1, 8, 7, 40), (17, 1, 39, 7, 7), (18, 6, 8, 0, 40))

    def pack_corners(s, rel):
        for n, (q, layer, row, _, _) in enumerate(corner_places):
            for h in range(2):
                csend[s, n, h:h + 1, :] = rel[POS[q], layer, h, row:row + 1, :]

    def pack_rows(s, rel):
        for side, (slots, row) in enumerate(((UP_Y, 39), (DOWN_Y, 8))):
            for z in range(NZL):
                for n, slot in enumerate(slots):
                    for h in range(2):
                        place = 10 * z + 2 * n + h
                        ysend[s, side, place:place + 1, :] = rel[slot, z + 1, h, row:row + 1, :]

    def unpack_rows(s, rel):
        for side, (slots, row, edge) in enumerate(((UP_Y, 7, r == 0), (DOWN_Y, 40, r == NR - 1))):
            for z in range(NZL):
                for n, slot in enumerate(slots):
                    for h in range(2):
                        place = 10 * z + 2 * n + h
                        rel[slot, z + 1, h, row:row + 1, :] = jnp.where(
                            edge, WALL, yrecv[s, side, place:place + 1, :]
                        )

    def unpack_layers(s, rel):
        @pl.when(d == 0)
        def _():
            rel[UP_Z:UP_Z + 5, 0] = jnp.full((5, 2, 48, 128), WALL, F32)

        @pl.when(d == ND - 1)
        def _():
            rel[DOWN_Z:DOWN_Z + 5, 7] = jnp.full((5, 2, 48, 128), WALL, F32)

        edges = (
            (d == 0) | (r == 0), (d == ND - 1) | (r == NR - 1), (d == ND - 1) | (r == 0), (d == 0) | (r == NR - 1)
        )
        for n, (q, _, _, layer, row) in enumerate(corner_places):
            for h in range(2):
                rel[POS[q], layer, h, row:row + 1, :] = jnp.where(edges[n], WALL, crecv[s, n, h:h + 1, :])

    loads[NZL].wait()
    loads[0].wait()
    loads[5].wait()
    outer_tiles(first_tile, None)
    pack_corners(0, r1)
    pl.semaphore_wait(barrier, len(peers))
    layers1 = [copy for t in range(4) for copy in layer_copies(0, r1, t)]
    rows1, corners1 = halo_copies(0, r1)
    for copy in layers1 + corners1:
        copy.start()
    for z in range(1, 5):
        loads[z].wait()
    tiles(8, first_tile, lambda i: 1 + (i >> 1), lambda i: 3 * (i & 1))
    pack_rows(0, r1)
    for copy in rows1:
        copy.start()
    tiles(8, first_tile, lambda i: 1 + (i >> 1), lambda i: 1 + (i & 1))

    tiles(8, second_tile, lambda i: 1 + (i >> 1), lambda i: 1 + (i & 1))
    for copy in rows1:
        copy.wait()
    unpack_rows(0, r1)
    tiles(8, second_tile, lambda i: 1 + (i >> 1), lambda i: 3 * (i & 1))
    for copy in layers1 + corners1:
        copy.wait()
    unpack_layers(0, r1)
    outer_tiles(second_tile, lambda t: layer_copies(1, r2, t))
    layers2 = [copy for t in range(4) for copy in layer_copies(1, r2, t)]
    rows2, corners2 = halo_copies(1, r2)
    pack_corners(1, r2)
    for copy in layers2[6:] + corners2:
        copy.start()
    pack_rows(1, r2)
    for copy in rows2:
        copy.start()

    loads[NZL + 1].wait()

    def third_tiles(count, z_of, t_of, before, carry):
        def step(i, places):
            last = jnp.maximum(i - 1, 0)
            first = i == 0
            following = third_tile(z_of(i), t_of(i))
            classify(
                jnp.where(first, before[0], z_of(last)), jnp.where(first, before[1], t_of(last)), places
            )
            return following

        return lax.fori_loop(0, count, step, carry)

    site_copies = [
        [
            remote(ssend.at[side, 2 * part:3 - (1 - part)], srecv.at[side, 2 * part:3 - (1 - part)], c_send_sem.at[part, side], c_recv_sem.at[part, side], target)
            for side, target in enumerate((at(d, up_r), at(d, down_r)))
        ]
        for part in range(2)
    ]
    def pack_sites(part, layers):
        for n, z in enumerate(layers):
            for side, row in enumerate((39, 8)):
                for c in range(4):
                    place = 4 * (n % 2) + c
                    ssend[side, 2 * part + n // 2, place:place + 1, :] = cbuf[c, z, row:row + 1, :]
        for copy in site_copies[part]:
            copy.start()

    def unpack_sites(part, layers):
        for copy in site_copies[part]:
            copy.wait()
        for n, z in enumerate(layers):
            for side, (row, edge) in enumerate(((7, r == 0), (40, r == NR - 1))):
                for c in range(4):
                    place = 4 * (n % 2) + c
                    cbuf[c, z, row:row + 1, :] = jnp.where(
                        edge, 0.0, srecv[side, 2 * part + n // 2, place:place + 1, :]
                    )

    places = tuple(jnp.zeros((8, 128), F32) for _ in range(4))
    places = third_tiles(8, lambda i: 1 + (i >> 1), lambda i: 1 + (i & 1), (1, 1), places)
    for copy in rows2:
        copy.wait()
    unpack_rows(1, r2)
    places = third_tiles(8, lambda i: 1 + (i >> 1), lambda i: 3 * (i & 1), (4, 2), places)
    classify(4, 3, places)
    pack_sites(0, (1, 2, 3, 4))
    for copy in layers2 + corners2:
        copy.wait()
    unpack_layers(1, r2)
    places = third_tiles(4, lambda i: (i >> 1) * 5, lambda i: 3 * (i & 1), (4, 3), places)

    classify(5, 3, places)
    pack_sites(1, (0, 5))
    places = third_tiles(4, lambda i: (i >> 1) * 5, lambda i: 1 + (i & 1), (5, 3), places)
    classify(5, 2, places)

    def columns(z):
        for c in range(4):
            sites = cbuf[c, z]
            high = sites.astype(BF16)
            low = (sites - high.astype(F32)).astype(BF16)
            wide = lax.dot_general(
                wcols[...], jnp.concatenate([high, low], axis=0), (((1,), (0,)), ((), ())),
                preferred_element_type=F32,
            )
            high = wide.astype(BF16)
            low = (wide - high.astype(F32)).astype(BF16)
            place = slice((c % 2) * 128, (c % 2) * 128 + 128)
            vbuf[z, c // 2, 0, place, :] = high
            vbuf[z, c // 2, 1, place, :] = low

    def columns_step(i, carry):
        columns(i + 1)
        return carry

    def render(group, layers):
        weights = wrows[group * 256:(group + 1) * 256, :]
        for z in layers:
            drawn = []
            for pair in (1, 0):
                parts = [
                    lax.dot_general(
                        weights, vbuf[z, pair, n], (((1,), (1,)), ((), ())), preferred_element_type=F32
                    )
                    for n in range(2)
                ]
                drawn.append(parts[0] + parts[1])
            for half in range(2):
                rows = slice(half * 128, half * 128 + 128)
                parts = [drawn[1 - c // 2][rows, (c % 2) * 128:(c % 2) * 128 + 128] for c in range(4)]
                if z == 0:
                    through = 1.0 - parts[3]
                    parts = [parts[c] + through * acc[group, half, c] for c in range(4)]
                elif z > 1:
                    through = 1.0 - acc[group, half, 3]
                    parts = [acc[group, half, c] + through * parts[c] for c in range(4)]
                for c in range(4):
                    acc[group, half, c] = parts[c]

    def columns_inner(i, carry):
        columns(i + 1)
        return carry

    def columns_outer(i, carry):
        columns(5 * i)
        return carry

    unpack_sites(0, (1, 2, 3, 4))
    lax.fori_loop(0, 4, columns_inner, 0)
    render(0, (1, 2, 3, 4))
    unpack_sites(1, (0, 5))
    lax.fori_loop(0, 2, columns_outer, 0)

    partner = at(d + 1 - 2 * core, r)
    swaps = [
        remote(acc.at[group, 1 - core], xrecv.at[group], x_sem.at[0, group], x_sem.at[1, group], partner)
        for group in range(2)
    ]
    exchange = [[], []]
    for group in range(2):
        for k in range(1, NC):
            other = lax.rem(chip + k, NC)
            exchange[group].append(
                remote(pieces.at[group, other], gathered.at[group, chip],
                       g_send_sem.at[group, k], g_recv_sem.at[group, k], at(2 * other + core, r))
            )

    def join(group):
        def step(n, carry):
            rows = pl.ds(pl.multiple_of(n * 8, 8), 8)
            front = core == 0
            mine = [acc[group, core, c, rows, :] for c in range(4)]
            theirs = [xrecv[group, c, rows, :] for c in range(4)]
            near = [jnp.where(front, mine[c], theirs[c]) for c in range(4)]
            far = [jnp.where(front, theirs[c], mine[c]) for c in range(4)]
            through = 1.0 - near[3]
            for c in range(4):
                pieces[group, n, c] = near[c] + through * far[c]
            return carry

        lax.fori_loop(0, NC, step, 0, unroll=4)
        for copy in exchange[group]:
            copy.start()
        gathered[group, chip] = pieces[group, chip]

    render(0, (0, 5))
    swaps[0].start()
    render(1, (1, 2, 3, 4, 0, 5))
    swaps[1].start()
    swaps[0].wait()
    join(0)
    swaps[1].wait()
    join(1)

    for group in range(2):
        for copy in exchange[group]:
            copy.wait()
        final = [gathered[group, 0, c] for c in range(4)]
        for n in range(1, NC):
            through = 1.0 - final[3]
            final = [final[c] + through * gathered[group, n, c] for c in range(4)]
        for half in range(2):
            for c in range(4):
                fsend[2 * group + half, 4 * c:4 * c + 4, :] = final[c][4 * half:4 * half + 4, :]
    last = []
    for k in range(1, NR):
        other = lax.rem(r + k, NR)
        last.append(remote(fsend.at[other], frecv.at[r], f_send_sem.at[k], f_recv_sem.at[k], at(d, other)))
        last[-1].start()
    frecv[r] = fsend[r]
    for copy in last:
        copy.wait()
    for rr in range(NR):
        for c in range(4):
            image[c, :, rr * 128:(rr + 1) * 128] = frecv[rr, 4 * c:4 * c + 4, :]


def shards(populations, fluid_mask, tissue_tag, colour_table):
    dma = pltpu.SemaphoreType.DMA
    vmem = pl.BlockSpec(memory_space=pltpu.VMEM)
    anywhere = pl.BlockSpec(memory_space=pl.ANY)
    advanced, drawn = pl.pallas_call(
        kernel,
        out_shape=(
            pltpu.VMEM(populations.shape, F32),
            pltpu.VMEM((4, IMG // (ND * NR), IMG), F32),
        ),
        in_specs=[anywhere, anywhere, anywhere, vmem],
        out_specs=(vmem, vmem),
        scratch_shapes=[
            pltpu.VMEM((NZL, NYL, NX), jnp.int32),
            pltpu.VMEM((NZL, NYL, NX), jnp.int32),
            pltpu.VMEM((NQ, NZL + 2, 2, 48, 128), F32),
            pltpu.VMEM((NQ, NZL + 2, 2, 48, 128), F32),
            pltpu.VMEM((2, 2, 64, 128), F32),
            pltpu.VMEM((2, 2, 64, 128), F32),
            pltpu.VMEM((2, 4, 8, 128), F32),
            pltpu.VMEM((2, 4, 8, 128), F32),
            pltpu.VMEM((4, 4, 2, 8, 128), F32),
            pltpu.VMEM((4, NZL, 48, NX), F32),
            pltpu.VMEM((2, 3, 8, NX), F32),
            pltpu.VMEM((2, 3, 8, NX), F32),
            pltpu.VMEM((128, 96), BF16),
            pltpu.VMEM((IMG, NX), BF16),
            pltpu.VMEM((NZL, 2, 2, 256, NX), BF16),
            pltpu.VMEM((2, 2, 4, 128, 128), F32),
            pltpu.VMEM((2, 4, 128, 128), F32),
            pltpu.VMEM((2, NC, 4, 8, 128), F32),
            pltpu.VMEM((2, NC, 4, 8, 128), F32),
            pltpu.VMEM((NR, 16, 128), F32),
            pltpu.VMEM((NR, 16, 128), F32),
            dma((NZL + 2,)), dma((2, 2, 4)), dma((2, 2, 4)), dma((2, 6)), dma((2, 6)), dma((2, 2)), dma((2, 2)), dma((2, 2)),
            dma((2, NC)), dma((2, NC)), dma((NR,)), dma((NR,)),
        ],
        compiler_params=pltpu.CompilerParams(
            collective_id=0, has_side_effects=True, vmem_limit_bytes=56 * 2**20
        ),
        name="vessel",
    )(populations, fluid_mask, tissue_tag, colour_table)
    return pl.pallas_call(
        deliver,
        out_shape=(
            jax.ShapeDtypeStruct(populations.shape, F32),
            jax.ShapeDtypeStruct((4, IMG // (ND * NR), IMG), F32),
        ),
        in_specs=[vmem, vmem],
        out_specs=(anywhere, anywhere),
        scratch_shapes=[dma((NZL + 1,))],
        compiler_params=pltpu.CompilerParams(vmem_limit_bytes=2**20),
        name="deliver",
    )(advanced, drawn)


def deliver(advanced, drawn, adv, image, sem):
    copies = [pltpu.make_async_copy(advanced.at[:, z], adv.at[:, z], sem.at[z]) for z in range(NZL)]
    copies.append(pltpu.make_async_copy(drawn, image, sem.at[NZL]))
    for copy in copies:
        copy.start()
    for copy in copies:
        copy.wait()


def solution(mesh):
    placed = (
        P(None, "depth", "rows", None),
        P("depth", "rows", None),
        P("depth", "rows", None),
        P(),
    )
    return jax.shard_map(
        shards,
        mesh=mesh,
        in_specs=placed,
        out_specs=(P(None, "depth", "rows", None), P(None, ("rows", "depth"), None)),
        check_vma=False,
    )
```

```python
import functools

import jax
import jax.numpy as jnp
from jax import lax
from jax.experimental import pallas as pl
from jax.experimental.pallas import tpu as pltpu
from jax.sharding import PartitionSpec as P

F32 = jnp.float32
BF16 = jnp.bfloat16
MESH = pl.DeviceIdType.MESH

VELOCITIES = (
    (0, 0, 0), (1, 0, 0), (-1, 0, 0), (0, 1, 0), (0, -1, 0), (0, 0, 1), (0, 0, -1),
    (1, 1, 0), (-1, -1, 0), (1, -1, 0), (-1, 1, 0),
    (1, 0, 1), (-1, 0, -1), (1, 0, -1), (-1, 0, 1),
    (0, 1, 1), (0, -1, -1), (0, 1, -1), (0, -1, 1),
)
OPPOSITE = (0, 2, 1, 4, 3, 6, 5, 8, 7, 10, 9, 12, 11, 14, 13, 16, 15, 18, 17)
PAIRS = tuple((q, q + 1) for q in range(1, 19, 2))
NU_ZERO = 0.12
NU_INFINITY = 0.02
LAMBDA_TIME = 15.0
POWER_INDEX = 0.3568
TAU_ZERO = 0.8
SPEED_SCALE = 0.04
SHEAR_SCALE = 0.07

ORDER = (16, 6, 12, 13, 17, 3, 7, 10, 15, 5, 11, 14, 18, 4, 8, 9, 0, 1, 2)
POS = tuple(ORDER.index(q) for q in range(19))
UP_Z, DOWN_Z = 8, 0
UP_Y = (4, 5, 6, 7, 8)
DOWN_Y = (12, 13, 14, 15, 0)
WALL = -1e30
WALL_REST = (-1e8, -1e12)
LIMIT = -1e5

NQ, NZL, NYL, NX = 19, 6, 32, 256
ND, NR, NC = 32, 4, 16
IMG = 512


def analyse(f, fluid=None, wall=None):
    sums = [f[a] + f[b] for a, b in PAIRS]
    diffs = [f[a] - f[b] for a, b in PAIRS]
    density = ((f[0] + sums[0]) + (sums[1] + sums[2])) + (
        ((sums[3] + sums[4]) + (sums[5] + sums[6])) + (sums[7] + sums[8])
    )
    mx = diffs[0] + ((diffs[3] + diffs[4]) + (diffs[5] + diffs[6]))
    my = diffs[1] + ((diffs[3] - diffs[4]) + (diffs[7] + diffs[8]))
    mz = diffs[2] + ((diffs[5] - diffs[6]) + (diffs[7] - diffs[8]))
    inverse = 1.0 / density
    third = (mx * (1.0 / 3.0), my * (1.0 / 3.0), mz * (1.0 / 3.0))
    hx, hy, hz = (0.5 * q for q in third)
    squares = [q * q for q in third]
    total = squares[0] + squares[1] + squares[2]
    axis_scale = 4.5 * inverse
    diag_scale = 9.0 * inverse
    rest = density - 3.0 * (total * axis_scale)
    if wall is not None:
        rest = jnp.where(fluid, rest, wall)
    axis_rest, diag_rest = rest * (1.0 / 9.0), rest * (1.0 / 18.0)
    diag = (hx + hy, hx - hy, hx + hz, hx - hz, hy + hz, hy - hz)
    even = [(sums[k] - axis_rest) - axis_scale * squares[k] for k in range(3)]
    even += [(sums[3 + k] - diag_rest) - diag_scale * (diag[k] * diag[k]) for k in range(6)]
    odd = [diffs[k] - third[k] for k in range(3)] + [diffs[3 + k] - diag[k] for k in range(6)]
    pxx = even[0] + ((even[3] + even[4]) + (even[5] + even[6]))
    pyy = even[1] + ((even[3] + even[4]) + (even[7] + even[8]))
    pzz = even[2] + ((even[5] + even[6]) + (even[7] + even[8]))
    pxy = even[3] - even[4]
    pxz = even[5] - even[6]
    pyz = even[7] - even[8]
    contracted = (pxx * pxx + pyy * pyy + pzz * pzz) + 2.0 * (pxy * pxy + pxz * pxz + pyz * pyz)
    return inverse, total, rest, even, odd, 2.0 * contracted + 1e-10


def collide(f, fluid, wall):
    inverse, _, rest, even, odd, stress = analyse(f, fluid, wall)
    squared = ((LAMBDA_TIME * 1.5 / TAU_ZERO) ** 2) * ((inverse * inverse) * stress)
    factor = jnp.exp(((POWER_INDEX - 1.0) / 2.0) * jnp.log(1.0 + squared))
    half = 1.0 / ((6.0 * NU_INFINITY + 1.0) + (6.0 * (NU_ZERO - NU_INFINITY)) * factor)
    out = [None] * 19
    out[0] = f[0] - (half + half) * (f[0] - rest * (1.0 / 3.0))
    for k, (a, b) in enumerate(PAIRS):
        s, d = half * even[k], half * odd[k]
        out[a] = f[a] - (s + d)
        out[b] = f[b] - (s - d)
    return out


def diagnose(f):
    inverse, total, _, _, _, stress = analyse(f)
    square = (9.0 * total) * (inverse * inverse) + 1e-12
    speed = square * lax.rsqrt(square)
    shear = (1.5 / TAU_ZERO) * inverse * (stress * lax.rsqrt(stress))
    return speed, shear


def kernel(
    pops, mask_in, tag_in, table, pbuf, image,
    mask, tag, r1, r2, ysend, yrecv, csend, crecv, bins, cbuf, ssend, srecv, wcols, wrows, vbuf,
    acc, xrecv, pieces, gathered, fsend, frecv,
    in_sem, ls_sem, lr_sem, hs_sem, hr_sem, c_send_sem, c_recv_sem, x_sem, g_send_sem, g_recv_sem, f_send_sem, f_recv_sem, ready,
):
    d = lax.axis_index("depth")
    r = lax.axis_index("rows")
    core = lax.rem(d, 2)
    chip = d // 2
    up_d, down_d = lax.rem(d + 1, ND), lax.rem(d + ND - 1, ND)
    up_r, down_r = lax.rem(r + 1, NR), lax.rem(r + NR - 1, NR)

    def at(dd, rr):
        return {"depth": dd, "rows": rr}

    barrier = pltpu.get_barrier_semaphore()
    row_first = (chip // 4) * 4
    columns_peers = [at(2 * lax.rem(chip + 4 * k, NC) + core, r) for k in (2, 1, 3)]
    peers = [at(up_d, up_r), at(up_d, down_r), at(down_d, up_r), at(down_d, down_r)]
    peers += [at(d, lax.rem(r + 2, NR))]
    peers += columns_peers
    peers += [at(2 * (row_first + lax.rem(chip + k, 4)) + core, r) for k in (2, 1, 3)]
    peers += [at(up_d, r), at(down_d, r), at(d, up_r), at(d, down_r), at(d + 1 - 2 * core, r)]
    for peer in peers:
        pl.semaphore_signal(barrier, inc=1, device_id=peer, device_id_type=MESH)

    loads = [pltpu.make_async_copy(pops.at[:, z], pbuf.at[:, z], in_sem.at[z]) for z in range(NZL)]
    loads.append(pltpu.make_async_copy(mask_in, mask, in_sem.at[NZL]))
    loads.append(pltpu.make_async_copy(tag_in, tag, in_sem.at[NZL + 1]))
    for n in (NZL, 0, 5, 1, 2, 3, 4, NZL + 1):
        loads[n].start()

    lane = lax.broadcasted_iota(jnp.int32, (8, 128), 1)
    first_lane, last_lane = lane == 0, lane == 127
    first_limit = jnp.where(first_lane, 1e30, LIMIT)
    last_limit = jnp.where(last_lane, 1e30, LIMIT)

    jj = lax.broadcasted_iota(jnp.int32, (128, 96), 0).astype(F32)
    yy = lax.broadcasted_iota(jnp.int32, (128, 96), 1)
    yy = (jnp.where(yy >= 48, yy - 48, yy) - 8).astype(F32)
    wcols[...] = jnp.maximum(0.0, 1.0 - jnp.abs((jj + 0.5) * 0.25 - 0.5 - yy)).astype(BF16)

    def fill_rows(b, carry):
        rho = b * 64 + lax.broadcasted_iota(jnp.int32, (64, 128), 0)
        ii = (
            (rho >> 8) * 256 + ((rho >> 2) & 1) * 128 + ((rho >> 3) & 15) * 8 + ((rho >> 7) & 1) * 4 + (rho & 3)
        ).astype(F32)
        centre = ii * 0.5 - 0.25
        for h in range(2):
            xx = (lax.broadcasted_iota(jnp.int32, (64, 128), 1) + h * 128).astype(F32)
            wt = jnp.maximum(0.0, 1.0 - jnp.abs(centre - xx)).astype(BF16)
            rows = pl.ds(pl.multiple_of(b * 64, 64), 64)
            wrows[rows, h * 128:(h + 1) * 128] = wt
        return carry

    lax.fori_loop(0, IMG // 64, fill_rows, 0)

    low_lanes = lane < 64
    for k in range(4):
        for c in range(4):
            halves = [jnp.broadcast_to(table[k, c:c + 1, h * 128:(h + 1) * 128], (8, 128)) for h in range(2)]
            for parity in range(2):
                index = ((lane * 2) & 127) + parity
                taken = [jnp.take_along_axis(half, index, axis=1, mode="promise_in_bounds") for half in halves]
                bins[k, c, parity] = jnp.where(low_lanes, taken[0], taken[1])

    def clear(z, carry):
        for c in range(4):
            cbuf[c, z, 0:8, :] = jnp.zeros((8, NX), F32)
            cbuf[c, z, 40:48, :] = jnp.zeros((8, NX), F32)
        return carry

    lax.fori_loop(0, NZL, clear, 0)

    def fluid_tiles(z, t):
        rows = pl.ds(pl.multiple_of(8 * t, 8), 8)
        return [mask[z, rows, h * 128:(h + 1) * 128] > 0 for h in range(2)]

    def store_relaxed(target, z, t, h, relaxed):
        rows = pl.ds(pl.multiple_of(8 * t + 8, 8), 8)
        for q in range(19):
            target[POS[q], z + 1, h, rows, :] = relaxed[q]

    def first_tile(z, t):
        rows = pl.ds(pl.multiple_of(8 * t, 8), 8)
        fluids = fluid_tiles(z, t)
        for h in range(2):
            f = [pbuf[q, z, rows, h * 128:(h + 1) * 128] for q in range(19)]
            store_relaxed(r1, z, t, h, collide(f, fluids[h], WALL_REST[0]))

    def arrive(source, z, t):
        own = pl.ds(pl.multiple_of(8 * t + 8, 8), 8)
        out = [[None] * 19, [None] * 19]
        for q in range(19):
            cx, cy, cz = VELOCITIES[q]
            if q == 0:
                for h in range(2):
                    out[h][0] = source[POS[0], z + 1, h, own, :]
                continue
            rows = own if cy == 0 else pl.ds(8 * t + 8 - cy, 8)
            a = [source[POS[q], z + 1 - cz, h, rows, :] for h in range(2)]
            limits = [LIMIT, LIMIT]
            if cx == 1:
                b0, b1 = pltpu.roll(a[0], 1, 1), pltpu.roll(a[1], 1, 1)
                a = [b0, jnp.where(first_lane, b0, b1)]
                limits[0] = first_limit
            elif cx == -1:
                b0, b1 = pltpu.roll(a[0], 127, 1), pltpu.roll(a[1], 127, 1)
                a = [jnp.where(last_lane, b1, b0), b1]
                limits[1] = last_limit
            for h in range(2):
                back = source[POS[OPPOSITE[q]], z + 1, h, own, :]
                out[h][q] = jnp.where(a[h] > limits[h], a[h], back)
        return out

    def second_tile(z, t):
        fluids = fluid_tiles(z, t)
        f = arrive(r1, z, t)
        for h in range(2):
            store_relaxed(r2, z, t, h, collide(f[h], fluids[h], WALL_REST[1]))

    def lookup(c, parity, index, tags):
        picked = [
            jnp.take_along_axis(bins[k, c, parity], index, axis=1, mode="promise_in_bounds") for k in range(4)
        ]
        return jnp.where(
            tags[0], jnp.where(tags[1], picked[3], picked[2]), jnp.where(tags[1], picked[1], picked[0])
        )

    def classify(z, t, places):
        rows = pl.ds(pl.multiple_of(8 * t, 8), 8)
        padded = pl.ds(pl.multiple_of(8 * t + 8, 8), 8)
        fluids = fluid_tiles(z, t)
        for h in range(2):
            lanes = slice(h * 128, (h + 1) * 128)
            tags = tag[z, rows, lanes]
            tags = (tags >= 2, (tags & 1) == 1)
            place = []
            for where in places[2 * h:2 * h + 2]:
                lower = jnp.clip(where.astype(jnp.int32), 0, 254)
                even, odd = (lower + 1) >> 1, lower >> 1
                place.append((1.0 - jnp.abs(where - (even + even).astype(F32)), even, odd))
            result = []
            for (share, even, odd), channels in zip(place, ((0, 1, 2), (3,))):
                at_odd = [lookup(c, 1, odd, tags) for c in channels]
                at_even = [lookup(c, 0, even, tags) for c in channels]
                result += [a + share * (b - a) for a, b in zip(at_odd, at_even)]
            coverage = jnp.where(fluids[h], result[3] * (3.0 / (NZL * ND)), 0.0)
            for c in range(3):
                cbuf[c, z, padded, lanes] = result[c] * coverage
            cbuf[3, z, padded, lanes] = coverage

    def third_tile(z, t):
        fluids = fluid_tiles(z, t)
        rows = pl.ds(pl.multiple_of(8 * t, 8), 8)
        f = arrive(r2, z, t)
        places = []
        for h in range(2):
            lanes = slice(h * 128, (h + 1) * 128)
            for q in range(19):
                pbuf[q, z, rows, lanes] = jnp.where(fluids[h], f[h][q], pbuf[q, z, rows, lanes])
            for value, scale in zip(diagnose(f[h]), (SPEED_SCALE, SHEAR_SCALE)):
                places.append(jnp.where(fluids[h], 255.0 * (value / (value + scale)), 0.0))
        return tuple(places)

    def tiles(count, body, z_of, t_of):
        def step(i, carry):
            body(z_of(i), t_of(i))
            return carry

        lax.fori_loop(0, count, step, 0, unroll=4)

    def outer_tiles(body, after):
        def step(t, carry):
            body(5, t)
            body(0, t)
            if after is not None:
                @pl.when(t > 0)
                def _():
                    for copy in after(t - 1):
                        copy.start()
            return carry

        lax.fori_loop(0, 4, step, 0, unroll=2)

    def remote(src, dst, send, recv, target):
        return pltpu.make_async_remote_copy(
            src_ref=src, dst_ref=dst, send_sem=send, recv_sem=recv, device_id=target, device_id_type=MESH
        )

    def layer_copies(s, rel, t):
        rows = pl.ds(pl.multiple_of(8 * t + 8, 8), 8)
        return [
            remote(rel.at[UP_Z:UP_Z + 5, 6, :, rows, :], rel.at[UP_Z:UP_Z + 5, 0, :, rows, :],
                   ls_sem.at[s, 0, t], lr_sem.at[s, 0, t], at(up_d, r)),
            remote(rel.at[DOWN_Z:DOWN_Z + 5, 1, :, rows, :], rel.at[DOWN_Z:DOWN_Z + 5, 7, :, rows, :],
                   ls_sem.at[s, 1, t], lr_sem.at[s, 1, t], at(down_d, r)),
        ]

    def halo_copies(s, rel):
        rows = [
            [
                remote(ysend.at[s, side, part], yrecv.at[s, side, part], hs_sem.at[s, 4 * n + side],
                       hr_sem.at[s, 4 * n + side], target)
                for side, target in enumerate((at(d, up_r), at(d, down_r)))
            ]
            for n, part in enumerate((slice(0, 40), slice(40, 64)))
        ]
        corners = [
            remote(csend.at[s, n], crecv.at[s, n], hs_sem.at[s, 8 + n], hr_sem.at[s, 8 + n], at(dd, rr))
            for n, (dd, rr) in enumerate(((up_d, up_r), (down_d, down_r), (down_d, up_r), (up_d, down_r)))
        ]
        return rows, corners

    corner_places = ((15, 6, 39, 0, 7), (16, 1, 8, 7, 40), (17, 1, 39, 7, 7), (18, 6, 8, 0, 40))

    def pack_corners(s, rel):
        for n, (q, layer, row, _, _) in enumerate(corner_places):
            for h in range(2):
                csend[s, n, h:h + 1, :] = rel[POS[q], layer, h, row:row + 1, :]

    row_places = [[(10 * n + k, z, k // 2, k % 2) for n, z in enumerate(layers) for k in range(10)] for layers in (
        (1, 2, 3, 4), (None, None, None, None, 0, 5))]
    row_places = [[p for p in places if p[1] is not None] for places in row_places]

    def pack_rows(s, rel, part):
        for side, (slots, row) in enumerate(((UP_Y, 39), (DOWN_Y, 8))):
            for place, z, n, h in row_places[part]:
                ysend[s, side, place:place + 1, :] = rel[slots[n], z + 1, h, row:row + 1, :]

    def unpack_rows(s, rel, part):
        for side, (slots, row, edge) in enumerate(((UP_Y, 7, r == 0), (DOWN_Y, 40, r == NR - 1))):
            for place, z, n, h in row_places[part]:
                rel[slots[n], z + 1, h, row:row + 1, :] = jnp.where(
                    edge, WALL, yrecv[s, side, place:place + 1, :]
                )

    def unpack_layers(s, rel):
        @pl.when(d == 0)
        def _():
            rel[UP_Z:UP_Z + 5, 0] = jnp.full((5, 2, 48, 128), WALL, F32)

        @pl.when(d == ND - 1)
        def _():
            rel[DOWN_Z:DOWN_Z + 5, 7] = jnp.full((5, 2, 48, 128), WALL, F32)

        edges = (
            (d == 0) | (r == 0), (d == ND - 1) | (r == NR - 1), (d == ND - 1) | (r == 0), (d == 0) | (r == NR - 1)
        )
        for n, (q, _, _, layer, row) in enumerate(corner_places):
            for h in range(2):
                rel[POS[q], layer, h, row:row + 1, :] = jnp.where(edges[n], WALL, crecv[s, n, h:h + 1, :])

    loads[NZL].wait()
    loads[0].wait()
    loads[5].wait()
    outer_tiles(first_tile, None)
    pack_corners(0, r1)
    pl.semaphore_wait(barrier, len(peers))
    layers1 = [copy for t in range(4) for copy in layer_copies(0, r1, t)]
    rows1, corners1 = halo_copies(0, r1)
    for copy in layers1 + corners1:
        copy.start()
    for peer in columns_peers:
        pl.semaphore_signal(ready, inc=1, device_id=peer, device_id_type=MESH)
    pack_rows(0, r1, 1)
    for copy in rows1[1]:
        copy.start()
    for z in range(1, 5):
        loads[z].wait()
    tiles(8, first_tile, lambda i: 1 + (i >> 1), lambda i: 3 * (i & 1))
    pack_rows(0, r1, 0)
    for copy in rows1[0]:
        copy.start()
    tiles(8, first_tile, lambda i: 1 + (i >> 1), lambda i: 1 + (i & 1))

    tiles(8, second_tile, lambda i: 1 + (i >> 1), lambda i: 1 + (i & 1))
    for part in (1, 0):
        for copy in rows1[part]:
            copy.wait()
        unpack_rows(0, r1, part)
    tiles(8, second_tile, lambda i: 1 + (i >> 1), lambda i: 3 * (i & 1))
    for copy in layers1 + corners1:
        copy.wait()
    unpack_layers(0, r1)
    rows2, corners2 = halo_copies(1, r2)
    pack_rows(1, r2, 0)
    for copy in rows2[0]:
        copy.start()
    outer_tiles(second_tile, lambda t: layer_copies(1, r2, t))
    layers2 = [copy for t in range(4) for copy in layer_copies(1, r2, t)]
    pack_rows(1, r2, 1)
    pack_corners(1, r2)
    for copy in rows2[1] + layers2[6:] + corners2:
        copy.start()

    loads[NZL + 1].wait()

    def third_tiles(count, z_of, t_of, before, carry):
        def step(i, places):
            last = jnp.maximum(i - 1, 0)
            first = i == 0
            following = third_tile(z_of(i), t_of(i))
            classify(
                jnp.where(first, before[0], z_of(last)), jnp.where(first, before[1], t_of(last)), places
            )
            return following

        return lax.fori_loop(0, count, step, carry)

    site_copies = [
        [
            remote(ssend.at[side, 2 * part:3 - (1 - part)], srecv.at[side, 2 * part:3 - (1 - part)], c_send_sem.at[part, side], c_recv_sem.at[part, side], target)
            for side, target in enumerate((at(d, up_r), at(d, down_r)))
        ]
        for part in range(2)
    ]
    def pack_sites(part, layers):
        for n, z in enumerate(layers):
            for side, row in enumerate((39, 8)):
                for c in range(4):
                    place = 4 * (n % 2) + c
                    ssend[side, 2 * part + n // 2, place:place + 1, :] = cbuf[c, z, row:row + 1, :]
        for copy in site_copies[part]:
            copy.start()

    def unpack_sites(part, layers):
        for copy in site_copies[part]:
            copy.wait()
        for n, z in enumerate(layers):
            for side, (row, edge) in enumerate(((7, r == 0), (40, r == NR - 1))):
                for c in range(4):
                    place = 4 * (n % 2) + c
                    cbuf[c, z, row:row + 1, :] = jnp.where(
                        edge, 0.0, srecv[side, 2 * part + n // 2, place:place + 1, :]
                    )

    places = tuple(jnp.zeros((8, 128), F32) for _ in range(4))
    places = third_tiles(8, lambda i: 1 + (i >> 1), lambda i: 1 + (i & 1), (1, 1), places)
    for copy in rows2[0]:
        copy.wait()
    unpack_rows(1, r2, 0)
    places = third_tiles(4, lambda i: 2 + (i >> 1), lambda i: 3 * (i & 1), (4, 2), places)
    for copy in rows2[1]:
        copy.wait()
    unpack_rows(1, r2, 1)
    places = third_tiles(4, lambda i: 1 + 3 * (i >> 1), lambda i: 3 * (i & 1), (3, 3), places)
    classify(4, 3, places)
    pack_sites(0, (1, 2, 3, 4))
    for copy in layers2 + corners2:
        copy.wait()
    unpack_layers(1, r2)
    places = third_tiles(4, lambda i: (i >> 1) * 5, lambda i: 3 * (i & 1), (4, 3), places)

    classify(5, 3, places)
    pack_sites(1, (0, 5))
    places = third_tiles(4, lambda i: (i >> 1) * 5, lambda i: 1 + (i & 1), (5, 3), places)
    classify(5, 2, places)

    def columns(z):
        for c in range(4):
            sites = cbuf[c, z]
            high = sites.astype(BF16)
            low = (sites - high.astype(F32)).astype(BF16)
            wide = lax.dot_general(
                wcols[...], jnp.concatenate([high, low], axis=0), (((1,), (0,)), ((), ())),
                preferred_element_type=F32,
            )
            high = wide.astype(BF16)
            low = (wide - high.astype(F32)).astype(BF16)
            place = slice((c % 2) * 128, (c % 2) * 128 + 128)
            vbuf[z, c // 2, 0, place, :] = high
            vbuf[z, c // 2, 1, place, :] = low

    def columns_step(i, carry):
        columns(i + 1)
        return carry

    def render(group, layers):
        weights = wrows[group * 256:(group + 1) * 256, :]
        for z in layers:
            drawn = []
            for pair in (1, 0):
                parts = [
                    lax.dot_general(
                        weights, vbuf[z, pair, n], (((1,), (1,)), ((), ())), preferred_element_type=F32
                    )
                    for n in range(2)
                ]
                drawn.append(parts[0] + parts[1])
            for half in range(2):
                rows = slice(half * 128, half * 128 + 128)
                parts = [drawn[1 - c // 2][rows, (c % 2) * 128:(c % 2) * 128 + 128] for c in range(4)]
                if z == 0:
                    through = 1.0 - parts[3]
                    parts = [parts[c] + through * acc[group, half, c] for c in range(4)]
                elif z > 1:
                    through = 1.0 - acc[group, half, 3]
                    parts = [acc[group, half, c] + through * parts[c] for c in range(4)]
                for c in range(4):
                    acc[group, half, c] = parts[c]

    def columns_inner(i, carry):
        columns(i + 1)
        return carry

    def columns_outer(i, carry):
        columns(5 * i)
        return carry

    unpack_sites(0, (1, 2, 3, 4))
    lax.fori_loop(0, 4, columns_inner, 0)
    render(0, (1, 2, 3, 4))
    unpack_sites(1, (0, 5))
    lax.fori_loop(0, 2, columns_outer, 0)

    partner = at(d + 1 - 2 * core, r)
    swaps = [
        remote(acc.at[group, 1 - core], xrecv.at[group], x_sem.at[0, group], x_sem.at[1, group], partner)
        for group in range(2)
    ]
    exchange = [[], []]
    for group in range(2):
        for k in range(1, NC):
            other = lax.rem(chip + k, NC)
            exchange[group].append(
                remote(pieces.at[group, other], gathered.at[group, chip],
                       g_send_sem.at[group, k], g_recv_sem.at[group, k], at(2 * other + core, r))
            )

    def join(group):
        def step(n, carry):
            rows = pl.ds(pl.multiple_of(n * 8, 8), 8)
            front = core == 0
            mine = [acc[group, core, c, rows, :] for c in range(4)]
            theirs = [xrecv[group, c, rows, :] for c in range(4)]
            near = [jnp.where(front, mine[c], theirs[c]) for c in range(4)]
            far = [jnp.where(front, theirs[c], mine[c]) for c in range(4)]
            through = 1.0 - near[3]
            for c in range(4):
                pieces[group, n, c] = near[c] + through * far[c]
            return carry

        lax.fori_loop(0, NC, step, 0, unroll=4)
        if group == 0:
            pl.semaphore_wait(ready, len(columns_peers))
        for copy in exchange[group]:
            copy.start()
        gathered[group, chip] = pieces[group, chip]

    render(0, (0, 5))
    swaps[0].start()
    render(1, (1, 2, 3, 4, 0, 5))
    swaps[1].start()
    swaps[0].wait()
    join(0)
    swaps[1].wait()
    join(1)

    for group in range(2):
        for copy in exchange[group]:
            copy.wait()
        final = [gathered[group, 0, c] for c in range(4)]
        for n in range(1, NC):
            through = 1.0 - final[3]
            final = [final[c] + through * gathered[group, n, c] for c in range(4)]
        for half in range(2):
            for c in range(4):
                fsend[2 * group + half, 4 * c:4 * c + 4, :] = final[c][4 * half:4 * half + 4, :]
    last = []
    for k in range(1, NR):
        other = lax.rem(r + k, NR)
        last.append(remote(fsend.at[other], frecv.at[r], f_send_sem.at[k], f_recv_sem.at[k], at(d, other)))
        last[-1].start()
    frecv[r] = fsend[r]
    for copy in last:
        copy.wait()
    for rr in range(NR):
        for c in range(4):
            image[c, :, rr * 128:(rr + 1) * 128] = frecv[rr, 4 * c:4 * c + 4, :]


def shards(populations, fluid_mask, tissue_tag, colour_table):
    dma = pltpu.SemaphoreType.DMA
    vmem = pl.BlockSpec(memory_space=pltpu.VMEM)
    anywhere = pl.BlockSpec(memory_space=pl.ANY)
    advanced, drawn = pl.pallas_call(
        kernel,
        out_shape=(
            pltpu.VMEM(populations.shape, F32),
            pltpu.VMEM((4, IMG // (ND * NR), IMG), F32),
        ),
        in_specs=[anywhere, anywhere, anywhere, vmem],
        out_specs=(vmem, vmem),
        scratch_shapes=[
            pltpu.VMEM((NZL, NYL, NX), jnp.int32),
            pltpu.VMEM((NZL, NYL, NX), jnp.int32),
            pltpu.VMEM((NQ, NZL + 2, 2, 48, 128), F32),
            pltpu.VMEM((NQ, NZL + 2, 2, 48, 128), F32),
            pltpu.VMEM((2, 2, 64, 128), F32),
            pltpu.VMEM((2, 2, 64, 128), F32),
            pltpu.VMEM((2, 4, 8, 128), F32),
            pltpu.VMEM((2, 4, 8, 128), F32),
            pltpu.VMEM((4, 4, 2, 8, 128), F32),
            pltpu.VMEM((4, NZL, 48, NX), F32),
            pltpu.VMEM((2, 3, 8, NX), F32),
            pltpu.VMEM((2, 3, 8, NX), F32),
            pltpu.VMEM((128, 96), BF16),
            pltpu.VMEM((IMG, NX), BF16),
            pltpu.VMEM((NZL, 2, 2, 256, NX), BF16),
            pltpu.VMEM((2, 2, 4, 128, 128), F32),
            pltpu.VMEM((2, 4, 128, 128), F32),
            pltpu.VMEM((2, NC, 4, 8, 128), F32),
            pltpu.VMEM((2, NC, 4, 8, 128), F32),
            pltpu.VMEM((NR, 16, 128), F32),
            pltpu.VMEM((NR, 16, 128), F32),
            dma((NZL + 2,)), dma((2, 2, 4)), dma((2, 2, 4)), dma((2, 12)), dma((2, 12)), dma((2, 2)), dma((2, 2)), dma((2, 2)),
            dma((2, NC)), dma((2, NC)), dma((NR,)), dma((NR,)), pltpu.SemaphoreType.REGULAR,
        ],
        compiler_params=pltpu.CompilerParams(
            collective_id=0, has_side_effects=True, vmem_limit_bytes=56 * 2**20
        ),
        name="vessel",
    )(populations, fluid_mask, tissue_tag, colour_table)
    return pl.pallas_call(
        deliver,
        out_shape=(
            jax.ShapeDtypeStruct(populations.shape, F32),
            jax.ShapeDtypeStruct((4, IMG // (ND * NR), IMG), F32),
        ),
        in_specs=[vmem, vmem],
        out_specs=(anywhere, anywhere),
        scratch_shapes=[dma((NZL + 1,))],
        compiler_params=pltpu.CompilerParams(vmem_limit_bytes=2**20),
        name="deliver",
    )(advanced, drawn)


def deliver(advanced, drawn, adv, image, sem):
    copies = [pltpu.make_async_copy(advanced.at[:, z], adv.at[:, z], sem.at[z]) for z in range(NZL)]
    copies.append(pltpu.make_async_copy(drawn, image, sem.at[NZL]))
    for copy in copies:
        copy.start()
    for copy in copies:
        copy.wait()


def solution(mesh):
    placed = (
        P(None, "depth", "rows", None),
        P("depth", "rows", None),
        P("depth", "rows", None),
        P(),
    )
    return jax.shard_map(
        shards,
        mesh=mesh,
        in_specs=placed,
        out_specs=(P(None, "depth", "rows", None), P(None, ("rows", "depth"), None)),
        check_vma=False,
    )
```

```python
import functools

import jax
import jax.numpy as jnp
from jax import lax
from jax.experimental import pallas as pl
from jax.experimental.pallas import tpu as pltpu
from jax.sharding import PartitionSpec as P

F32 = jnp.float32
BF16 = jnp.bfloat16
MESH = pl.DeviceIdType.MESH

VELOCITIES = (
    (0, 0, 0), (1, 0, 0), (-1, 0, 0), (0, 1, 0), (0, -1, 0), (0, 0, 1), (0, 0, -1),
    (1, 1, 0), (-1, -1, 0), (1, -1, 0), (-1, 1, 0),
    (1, 0, 1), (-1, 0, -1), (1, 0, -1), (-1, 0, 1),
    (0, 1, 1), (0, -1, -1), (0, 1, -1), (0, -1, 1),
)
OPPOSITE = (0, 2, 1, 4, 3, 6, 5, 8, 7, 10, 9, 12, 11, 14, 13, 16, 15, 18, 17)
PAIRS = tuple((q, q + 1) for q in range(1, 19, 2))
NU_ZERO = 0.12
NU_INFINITY = 0.02
LAMBDA_TIME = 15.0
POWER_INDEX = 0.3568
TAU_ZERO = 0.8
SPEED_SCALE = 0.04
SHEAR_SCALE = 0.07

ORDER = (16, 6, 12, 13, 17, 3, 7, 10, 15, 5, 11, 14, 18, 4, 8, 9, 0, 1, 2)
POS = tuple(ORDER.index(q) for q in range(19))
UP_Z, DOWN_Z = 8, 0
UP_Y = (4, 5, 6, 7, 8)
DOWN_Y = (12, 13, 14, 15, 0)
WALL = -1e30
WALL_REST = (-1e8, -1e12)
LIMIT = -1e5

NQ, NZL, NYL, NX = 19, 6, 32, 256
ND, NR, NC = 32, 4, 16
IMG = 512


def analyse(f, fluid=None, wall=None):
    sums = [f[a] + f[b] for a, b in PAIRS]
    diffs = [f[a] - f[b] for a, b in PAIRS]
    density = ((f[0] + sums[0]) + (sums[1] + sums[2])) + (
        ((sums[3] + sums[4]) + (sums[5] + sums[6])) + (sums[7] + sums[8])
    )
    mx = diffs[0] + ((diffs[3] + diffs[4]) + (diffs[5] + diffs[6]))
    my = diffs[1] + ((diffs[3] - diffs[4]) + (diffs[7] + diffs[8]))
    mz = diffs[2] + ((diffs[5] - diffs[6]) + (diffs[7] - diffs[8]))
    inverse = 1.0 / density
    third = (mx * (1.0 / 3.0), my * (1.0 / 3.0), mz * (1.0 / 3.0))
    hx, hy, hz = (0.5 * q for q in third)
    squares = [q * q for q in third]
    total = squares[0] + squares[1] + squares[2]
    axis_scale = 4.5 * inverse
    diag_scale = 9.0 * inverse
    rest = density - 3.0 * (total * axis_scale)
    if wall is not None:
        rest = jnp.where(fluid, rest, wall)
    axis_rest, diag_rest = rest * (1.0 / 9.0), rest * (1.0 / 18.0)
    diag = (hx + hy, hx - hy, hx + hz, hx - hz, hy + hz, hy - hz)
    even = [(sums[k] - axis_rest) - axis_scale * squares[k] for k in range(3)]
    even += [(sums[3 + k] - diag_rest) - diag_scale * (diag[k] * diag[k]) for k in range(6)]
    odd = [diffs[k] - third[k] for k in range(3)] + [diffs[3 + k] - diag[k] for k in range(6)]
    pxx = even[0] + ((even[3] + even[4]) + (even[5] + even[6]))
    pyy = even[1] + ((even[3] + even[4]) + (even[7] + even[8]))
    pzz = even[2] + ((even[5] + even[6]) + (even[7] + even[8]))
    pxy = even[3] - even[4]
    pxz = even[5] - even[6]
    pyz = even[7] - even[8]
    contracted = (pxx * pxx + pyy * pyy + pzz * pzz) + 2.0 * (pxy * pxy + pxz * pxz + pyz * pyz)
    return inverse, total, rest, even, odd, 2.0 * contracted + 1e-10


def collide(f, fluid, wall):
    inverse, _, rest, even, odd, stress = analyse(f, fluid, wall)
    squared = ((LAMBDA_TIME * 1.5 / TAU_ZERO) ** 2) * ((inverse * inverse) * stress)
    factor = jnp.exp(((POWER_INDEX - 1.0) / 2.0) * jnp.log(1.0 + squared))
    half = 1.0 / ((6.0 * NU_INFINITY + 1.0) + (6.0 * (NU_ZERO - NU_INFINITY)) * factor)
    out = [None] * 19
    out[0] = f[0] - (half + half) * (f[0] - rest * (1.0 / 3.0))
    for k, (a, b) in enumerate(PAIRS):
        s, d = half * even[k], half * odd[k]
        out[a] = f[a] - (s + d)
        out[b] = f[b] - (s - d)
    return out


def diagnose(f):
    inverse, total, _, _, _, stress = analyse(f)
    square = (9.0 * total) * (inverse * inverse) + 1e-12
    speed = square * lax.rsqrt(square)
    shear = (1.5 / TAU_ZERO) * inverse * (stress * lax.rsqrt(stress))
    return speed, shear


def kernel(
    pops, mask_in, tag_in, table, pbuf, image,
    mask, tag, r1, r2, ysend, yrecv, csend, crecv, bins, cbuf, ssend, srecv, wcols, wrows, vbuf,
    acc, xrecv, pieces, gathered, fsend, frecv,
    in_sem, ls_sem, lr_sem, hs_sem, hr_sem, c_send_sem, c_recv_sem, x_sem, g_send_sem, g_recv_sem, f_send_sem, f_recv_sem, ready,
):
    d = lax.axis_index("depth")
    r = lax.axis_index("rows")
    core = lax.rem(d, 2)
    chip = d // 2
    up_d, down_d = lax.rem(d + 1, ND), lax.rem(d + ND - 1, ND)
    up_r, down_r = lax.rem(r + 1, NR), lax.rem(r + NR - 1, NR)

    def at(dd, rr):
        return {"depth": dd, "rows": rr}

    barrier = pltpu.get_barrier_semaphore()
    row_first = (chip // 4) * 4
    columns_peers = [at(2 * lax.rem(chip + 4 * k, NC) + core, r) for k in (2, 1, 3)]
    peers = [at(up_d, up_r), at(up_d, down_r), at(down_d, up_r), at(down_d, down_r)]
    peers += [at(d, lax.rem(r + 2, NR))]
    peers += columns_peers
    peers += [at(2 * (row_first + lax.rem(chip + k, 4)) + core, r) for k in (2, 1, 3)]
    peers += [at(up_d, r), at(down_d, r), at(d, up_r), at(d, down_r), at(d + 1 - 2 * core, r)]
    for peer in peers:
        pl.semaphore_signal(barrier, inc=1, device_id=peer, device_id_type=MESH)

    loads = [pltpu.make_async_copy(pops.at[:, z], pbuf.at[:, z], in_sem.at[z]) for z in range(NZL)]
    loads.append(pltpu.make_async_copy(mask_in, mask, in_sem.at[NZL]))
    loads.append(pltpu.make_async_copy(tag_in, tag, in_sem.at[NZL + 1]))
    for n in (NZL, 0, 5, 1, 2, 3, 4, NZL + 1):
        loads[n].start()

    lane = lax.broadcasted_iota(jnp.int32, (8, 128), 1)
    first_lane, last_lane = lane == 0, lane == 127
    first_limit = jnp.where(first_lane, 1e30, LIMIT)
    last_limit = jnp.where(last_lane, 1e30, LIMIT)

    jj = lax.broadcasted_iota(jnp.int32, (128, 96), 0).astype(F32)
    yy = lax.broadcasted_iota(jnp.int32, (128, 96), 1)
    yy = (jnp.where(yy >= 48, yy - 48, yy) - 8).astype(F32)
    wcols[...] = jnp.maximum(0.0, 1.0 - jnp.abs((jj + 0.5) * 0.25 - 0.5 - yy)).astype(BF16)

    def fill_rows(b, carry):
        rho = b * 64 + lax.broadcasted_iota(jnp.int32, (64, 128), 0)
        ii = (
            (rho >> 8) * 256 + ((rho >> 2) & 1) * 128 + ((rho >> 3) & 15) * 8 + ((rho >> 7) & 1) * 4 + (rho & 3)
        ).astype(F32)
        centre = ii * 0.5 - 0.25
        for h in range(2):
            xx = (lax.broadcasted_iota(jnp.int32, (64, 128), 1) + h * 128).astype(F32)
            wt = jnp.maximum(0.0, 1.0 - jnp.abs(centre - xx)).astype(BF16)
            rows = pl.ds(pl.multiple_of(b * 64, 64), 64)
            wrows[rows, h * 128:(h + 1) * 128] = wt
        return carry

    lax.fori_loop(0, IMG // 64, fill_rows, 0)

    low_lanes = lane < 64
    for k in range(4):
        for c in range(4):
            halves = [jnp.broadcast_to(table[k, c:c + 1, h * 128:(h + 1) * 128], (8, 128)) for h in range(2)]
            for parity in range(2):
                index = ((lane * 2) & 127) + parity
                taken = [jnp.take_along_axis(half, index, axis=1, mode="promise_in_bounds") for half in halves]
                bins[k, c, parity] = jnp.where(low_lanes, taken[0], taken[1])

    for rel in (r1, r2):
        @pl.when(d == 0)
        def _():
            rel[UP_Z:UP_Z + 5, 0, :, 8:40, :] = jnp.full((5, 2, 32, 128), WALL, F32)

        @pl.when(d == ND - 1)
        def _():
            rel[DOWN_Z:DOWN_Z + 5, 7, :, 8:40, :] = jnp.full((5, 2, 32, 128), WALL, F32)

    def clear(z, carry):
        for c in range(4):
            cbuf[c, z, 0:8, :] = jnp.zeros((8, NX), F32)
            cbuf[c, z, 40:48, :] = jnp.zeros((8, NX), F32)
        return carry

    lax.fori_loop(0, NZL, clear, 0)

    def fluid_tiles(z, t):
        rows = pl.ds(pl.multiple_of(8 * t, 8), 8)
        return [mask[z, rows, h * 128:(h + 1) * 128] > 0 for h in range(2)]

    def store_relaxed(target, z, t, h, relaxed):
        rows = pl.ds(pl.multiple_of(8 * t + 8, 8), 8)
        for q in range(19):
            target[POS[q], z + 1, h, rows, :] = relaxed[q]

    def first_tile(z, t):
        rows = pl.ds(pl.multiple_of(8 * t, 8), 8)
        fluids = fluid_tiles(z, t)
        for h in range(2):
            f = [pbuf[q, z, rows, h * 128:(h + 1) * 128] for q in range(19)]
            store_relaxed(r1, z, t, h, collide(f, fluids[h], WALL_REST[0]))

    def arrive(source, z, t):
        own = pl.ds(pl.multiple_of(8 * t + 8, 8), 8)
        out = [[None] * 19, [None] * 19]
        for q in range(19):
            cx, cy, cz = VELOCITIES[q]
            if q == 0:
                for h in range(2):
                    out[h][0] = source[POS[0], z + 1, h, own, :]
                continue
            rows = own if cy == 0 else pl.ds(8 * t + 8 - cy, 8)
            a = [source[POS[q], z + 1 - cz, h, rows, :] for h in range(2)]
            limits = [LIMIT, LIMIT]
            if cx == 1:
                b0, b1 = pltpu.roll(a[0], 1, 1), pltpu.roll(a[1], 1, 1)
                a = [b0, jnp.where(first_lane, b0, b1)]
                limits[0] = first_limit
            elif cx == -1:
                b0, b1 = pltpu.roll(a[0], 127, 1), pltpu.roll(a[1], 127, 1)
                a = [jnp.where(last_lane, b1, b0), b1]
                limits[1] = last_limit
            for h in range(2):
                back = source[POS[OPPOSITE[q]], z + 1, h, own, :]
                out[h][q] = jnp.where(a[h] > limits[h], a[h], back)
        return out

    def second_tile(z, t):
        fluids = fluid_tiles(z, t)
        f = arrive(r1, z, t)
        for h in range(2):
            store_relaxed(r2, z, t, h, collide(f[h], fluids[h], WALL_REST[1]))

    def lookup(c, parity, index, tags):
        picked = [
            jnp.take_along_axis(bins[k, c, parity], index, axis=1, mode="promise_in_bounds") for k in range(4)
        ]
        return jnp.where(
            tags[0], jnp.where(tags[1], picked[3], picked[2]), jnp.where(tags[1], picked[1], picked[0])
        )

    def classify(z, t, places):
        rows = pl.ds(pl.multiple_of(8 * t, 8), 8)
        padded = pl.ds(pl.multiple_of(8 * t + 8, 8), 8)
        fluids = fluid_tiles(z, t)
        for h in range(2):
            lanes = slice(h * 128, (h + 1) * 128)
            tags = tag[z, rows, lanes]
            tags = (tags >= 2, (tags & 1) == 1)
            place = []
            for where in places[2 * h:2 * h + 2]:
                lower = jnp.clip(where.astype(jnp.int32), 0, 254)
                even, odd = (lower + 1) >> 1, lower >> 1
                place.append((1.0 - jnp.abs(where - (even + even).astype(F32)), even, odd))
            result = []
            for (share, even, odd), channels in zip(place, ((0, 1, 2), (3,))):
                at_odd = [lookup(c, 1, odd, tags) for c in channels]
                at_even = [lookup(c, 0, even, tags) for c in channels]
                result += [a + share * (b - a) for a, b in zip(at_odd, at_even)]
            coverage = jnp.where(fluids[h], result[3] * (3.0 / (NZL * ND)), 0.0)
            for c in range(3):
                cbuf[c, z, padded, lanes] = result[c] * coverage
            cbuf[3, z, padded, lanes] = coverage

    def third_tile(z, t):
        fluids = fluid_tiles(z, t)
        rows = pl.ds(pl.multiple_of(8 * t, 8), 8)
        f = arrive(r2, z, t)
        places = []
        for h in range(2):
            lanes = slice(h * 128, (h + 1) * 128)
            for q in range(19):
                pbuf[q, z, rows, lanes] = jnp.where(fluids[h], f[h][q], pbuf[q, z, rows, lanes])
            for value, scale in zip(diagnose(f[h]), (SPEED_SCALE, SHEAR_SCALE)):
                places.append(jnp.where(fluids[h], 255.0 * (value / (value + scale)), 0.0))
        return tuple(places)

    def tiles(count, body, z_of, t_of):
        def step(i, carry):
            body(z_of(i), t_of(i))
            return carry

        lax.fori_loop(0, count, step, 0, unroll=4)

    def outer_tiles(body, before, after):
        for t in range(4):
            if before is not None:
                before(t)
            body(5, t)
            body(0, t)
            if after is not None and t:
                start(after[2 * t - 2:2 * t])

    def remote(src, dst, send, recv, target):
        return pltpu.make_async_remote_copy(
            src_ref=src, dst_ref=dst, send_sem=send, recv_sem=recv, device_id=target, device_id_type=MESH
        )

    to_up, to_down, from_down, from_up = d < ND - 1, d > 0, d > 0, d < ND - 1
    to_right, to_left, from_left, from_right = r < NR - 1, r > 0, r > 0, r < NR - 1

    def start(copies):
        for copy, sends, _ in copies:
            pl.when(sends)(copy.start)

    def finish(copies):
        for copy, sends, receives in copies:
            pl.when(receives)(copy.wait_recv)
            pl.when(sends)(copy.wait_send)

    def layer_copies(s, rel, t):
        rows = pl.ds(8 * t + 8, 8)
        return [
            (remote(rel.at[UP_Z:UP_Z + 5, 6, :, rows, :], rel.at[UP_Z:UP_Z + 5, 0, :, rows, :],
                    ls_sem.at[s, 0, t], lr_sem.at[s, 0, t], at(up_d, r)), to_up, from_down),
            (remote(rel.at[DOWN_Z:DOWN_Z + 5, 1, :, rows, :], rel.at[DOWN_Z:DOWN_Z + 5, 7, :, rows, :],
                    ls_sem.at[s, 1, t], lr_sem.at[s, 1, t], at(down_d, r)), to_down, from_up),
        ]

    sides = ((at(d, up_r), to_right, from_left), (at(d, down_r), to_left, from_right))
    corner_sides = (
        (at(up_d, up_r), to_up & to_right, from_down & from_left),
        (at(down_d, down_r), to_down & to_left, from_up & from_right),
        (at(down_d, up_r), to_down & to_right, from_up & from_left),
        (at(up_d, down_r), to_up & to_left, from_down & from_right),
    )

    def halo_copies(s, rel):
        rows = [
            [
                (remote(ysend.at[s, side, part], yrecv.at[s, side, part], hs_sem.at[s, 4 * n + side],
                        hr_sem.at[s, 4 * n + side], target), sends, receives)
                for side, (target, sends, receives) in enumerate(sides)
            ]
            for n, part in enumerate((slice(0, 40), slice(40, 64)))
        ]
        corners = [
            (remote(csend.at[s, n], crecv.at[s, n], hs_sem.at[s, 8 + n], hr_sem.at[s, 8 + n], target), sends, receives)
            for n, (target, sends, receives) in enumerate(corner_sides)
        ]
        return rows, corners

    corner_places = ((15, 6, 39, 0, 7), (16, 1, 8, 7, 40), (17, 1, 39, 7, 7), (18, 6, 8, 0, 40))

    def pack_corners(s, rel):
        for n, (q, layer, row, _, _) in enumerate(corner_places):
            for h in range(2):
                csend[s, n, h:h + 1, :] = rel[POS[q], layer, h, row:row + 1, :]

    row_places = [[(10 * n + k, z, k // 2, k % 2) for n, z in enumerate(layers) for k in range(10)] for layers in (
        (1, 2, 3, 4), (None, None, None, None, 0, 5))]
    row_places = [[p for p in places if p[1] is not None] for places in row_places]

    def pack_rows(s, rel, part):
        for side, (slots, row) in enumerate(((UP_Y, 39), (DOWN_Y, 8))):
            for place, z, n, h in row_places[part]:
                ysend[s, side, place:place + 1, :] = rel[slots[n], z + 1, h, row:row + 1, :]

    def unpack_rows(s, rel, part):
        for side, (slots, row, edge) in enumerate(((UP_Y, 7, r == 0), (DOWN_Y, 40, r == NR - 1))):
            for place, z, n, h in row_places[part]:
                rel[slots[n], z + 1, h, row:row + 1, :] = jnp.where(
                    edge, WALL, yrecv[s, side, place:place + 1, :]
                )

    def take_layers(copies, t):
        finish(copies[2 * t:2 * t + 2])

    def take_corners(s, copies, rel):
        finish(copies)
        edges = (
            (d == 0) | (r == 0), (d == ND - 1) | (r == NR - 1), (d == ND - 1) | (r == 0), (d == 0) | (r == NR - 1)
        )
        for n, (q, _, _, layer, row) in enumerate(corner_places):
            for h in range(2):
                rel[POS[q], layer, h, row:row + 1, :] = jnp.where(edges[n], WALL, crecv[s, n, h:h + 1, :])

    loads[NZL].wait()
    loads[0].wait()
    loads[5].wait()
    outer_tiles(first_tile, None, None)
    pack_corners(0, r1)
    pl.semaphore_wait(barrier, len(peers))
    layers1 = [copy for t in range(4) for copy in layer_copies(0, r1, t)]
    rows1, corners1 = halo_copies(0, r1)
    start(layers1 + corners1)
    for peer in columns_peers:
        pl.semaphore_signal(ready, inc=1, device_id=peer, device_id_type=MESH)
    pack_rows(0, r1, 1)
    start(rows1[1])
    for z in range(1, 5):
        loads[z].wait()
    tiles(8, first_tile, lambda i: 1 + (i >> 1), lambda i: 3 * (i & 1))
    pack_rows(0, r1, 0)
    start(rows1[0])
    tiles(8, first_tile, lambda i: 1 + (i >> 1), lambda i: 1 + (i & 1))

    tiles(8, second_tile, lambda i: 1 + (i >> 1), lambda i: 1 + (i & 1))
    for part in (1, 0):
        finish(rows1[part])
        unpack_rows(0, r1, part)
    tiles(8, second_tile, lambda i: 1 + (i >> 1), lambda i: 3 * (i & 1))
    rows2, corners2 = halo_copies(1, r2)
    pack_rows(1, r2, 0)
    start(rows2[0])
    layers2 = [copy for t in range(4) for copy in layer_copies(1, r2, t)]
    take_corners(0, corners1, r1)
    take_layers(layers1, 0)
    outer_tiles(second_tile, lambda t: take_layers(layers1, t + 1) if t < 3 else None, layers2)
    pack_rows(1, r2, 1)
    pack_corners(1, r2)
    start(layers2[6:] + rows2[1] + corners2)

    loads[NZL + 1].wait()

    def third_tiles(count, z_of, t_of, before, carry):
        def step(i, places):
            last = jnp.maximum(i - 1, 0)
            first = i == 0
            following = third_tile(z_of(i), t_of(i))
            classify(
                jnp.where(first, before[0], z_of(last)), jnp.where(first, before[1], t_of(last)), places
            )
            return following

        return lax.fori_loop(0, count, step, carry)

    site_copies = [
        [
            (remote(ssend.at[side, slots], srecv.at[side, slots], c_send_sem.at[part, side],
                    c_recv_sem.at[part, side], target), sends, receives)
            for side, (target, sends, receives) in enumerate(sides)
        ]
        for part, slots in enumerate((slice(0, 2), slice(2, 3)))
    ]
    def pack_sites(part, layers):
        for n, z in enumerate(layers):
            for side, row in enumerate((39, 8)):
                for c in range(4):
                    place = 4 * (n % 2) + c
                    ssend[side, 2 * part + n // 2, place:place + 1, :] = cbuf[c, z, row:row + 1, :]
        start(site_copies[part])

    def unpack_sites(part, layers):
        finish(site_copies[part])
        for n, z in enumerate(layers):
            for side, (row, edge) in enumerate(((7, r == 0), (40, r == NR - 1))):
                for c in range(4):
                    place = 4 * (n % 2) + c
                    cbuf[c, z, row:row + 1, :] = jnp.where(
                        edge, 0.0, srecv[side, 2 * part + n // 2, place:place + 1, :]
                    )

    places = tuple(jnp.zeros((8, 128), F32) for _ in range(4))
    places = third_tiles(8, lambda i: 1 + (i >> 1), lambda i: 1 + (i & 1), (1, 1), places)
    finish(rows2[0])
    unpack_rows(1, r2, 0)
    places = third_tiles(4, lambda i: 2 + (i >> 1), lambda i: 3 * (i & 1), (4, 2), places)
    finish(rows2[1])
    unpack_rows(1, r2, 1)
    places = third_tiles(4, lambda i: 1 + 3 * (i >> 1), lambda i: 3 * (i & 1), (3, 3), places)
    classify(4, 3, places)
    pack_sites(0, (1, 2, 3, 4))
    take_corners(1, corners2, r2)
    for t in range(2):
        take_layers(layers2, t)
    places = third_tiles(2, lambda i: i * 5, lambda i: 0, (4, 3), places)
    for t in range(2, 4):
        take_layers(layers2, t)
    places = third_tiles(2, lambda i: i * 5, lambda i: 3, (5, 0), places)

    classify(5, 3, places)
    pack_sites(1, (0, 5))
    places = third_tiles(4, lambda i: (i >> 1) * 5, lambda i: 1 + (i & 1), (5, 3), places)
    classify(5, 2, places)

    def columns(z):
        for c in range(4):
            sites = cbuf[c, z]
            high = sites.astype(BF16)
            low = (sites - high.astype(F32)).astype(BF16)
            wide = lax.dot_general(
                wcols[...], jnp.concatenate([high, low], axis=0), (((1,), (0,)), ((), ())),
                preferred_element_type=F32,
            )
            high = wide.astype(BF16)
            low = (wide - high.astype(F32)).astype(BF16)
            place = slice((c % 2) * 128, (c % 2) * 128 + 128)
            vbuf[z, c // 2, 0, place, :] = high
            vbuf[z, c // 2, 1, place, :] = low

    def columns_step(i, carry):
        columns(i + 1)
        return carry

    def render(group, layers):
        weights = wrows[group * 256:(group + 1) * 256, :]
        for z in layers:
            drawn = []
            for pair in (1, 0):
                parts = [
                    lax.dot_general(
                        weights, vbuf[z, pair, n], (((1,), (1,)), ((), ())), preferred_element_type=F32
                    )
                    for n in range(2)
                ]
                drawn.append(parts[0] + parts[1])
            for half in range(2):
                rows = slice(half * 128, half * 128 + 128)
                parts = [drawn[1 - c // 2][rows, (c % 2) * 128:(c % 2) * 128 + 128] for c in range(4)]
                if z == 0:
                    through = 1.0 - parts[3]
                    parts = [parts[c] + through * acc[group, half, c] for c in range(4)]
                elif z > 1:
                    through = 1.0 - acc[group, half, 3]
                    parts = [acc[group, half, c] + through * parts[c] for c in range(4)]
                for c in range(4):
                    acc[group, half, c] = parts[c]

    def columns_inner(i, carry):
        columns(i + 1)
        return carry

    def columns_outer(i, carry):
        columns(5 * i)
        return carry

    unpack_sites(0, (1, 2, 3, 4))
    lax.fori_loop(0, 4, columns_inner, 0)
    render(0, (1, 2, 3, 4))
    unpack_sites(1, (0, 5))
    lax.fori_loop(0, 2, columns_outer, 0)

    partner = at(d + 1 - 2 * core, r)
    swaps = [
        remote(acc.at[group, 1 - core], xrecv.at[group], x_sem.at[0, group], x_sem.at[1, group], partner)
        for group in range(2)
    ]
    chips = list(range(1, NC))
    exchange = [[], []]
    for group in range(2):
        for k in chips:
            other = lax.rem(chip + k, NC)
            exchange[group].append(
                remote(pieces.at[group, other], gathered.at[group, chip],
                       g_send_sem.at[group, k], g_recv_sem.at[group, k], at(2 * other + core, r))
            )

    def join(group):
        def step(n, carry):
            rows = pl.ds(pl.multiple_of(n * 8, 8), 8)
            front = core == 0
            mine = [acc[group, core, c, rows, :] for c in range(4)]
            theirs = [xrecv[group, c, rows, :] for c in range(4)]
            near = [jnp.where(front, mine[c], theirs[c]) for c in range(4)]
            far = [jnp.where(front, theirs[c], mine[c]) for c in range(4)]
            through = 1.0 - near[3]
            for c in range(4):
                pieces[group, n, c] = near[c] + through * far[c]
            return carry

        lax.fori_loop(0, NC, step, 0, unroll=4)
        if group == 0:
            pl.semaphore_wait(ready, len(columns_peers))
        for copy in exchange[group]:
            copy.start()
        gathered[group, chip] = pieces[group, chip]

    render(0, (0, 5))
    swaps[0].start()
    render(1, (1, 2, 3, 4, 0, 5))
    swaps[1].start()
    swaps[0].wait()
    join(0)
    swaps[1].wait()
    join(1)

    for group in range(2):
        for copy in exchange[group]:
            copy.wait()
        final = [gathered[group, 0, c] for c in range(4)]
        for n in range(1, NC):
            through = 1.0 - final[3]
            final = [final[c] + through * gathered[group, n, c] for c in range(4)]
        for half in range(2):
            for c in range(4):
                fsend[2 * group + half, 4 * c:4 * c + 4, :] = final[c][4 * half:4 * half + 4, :]
    last = []
    for k in range(1, NR):
        other = lax.rem(r + k, NR)
        last.append(remote(fsend.at[other], frecv.at[r], f_send_sem.at[k], f_recv_sem.at[k], at(d, other)))
        last[-1].start()
    frecv[r] = fsend[r]
    for copy in last:
        copy.wait()
    for rr in range(NR):
        for c in range(4):
            image[c, :, rr * 128:(rr + 1) * 128] = frecv[rr, 4 * c:4 * c + 4, :]


def shards(populations, fluid_mask, tissue_tag, colour_table):
    dma = pltpu.SemaphoreType.DMA
    vmem = pl.BlockSpec(memory_space=pltpu.VMEM)
    anywhere = pl.BlockSpec(memory_space=pl.ANY)
    advanced, drawn = pl.pallas_call(
        kernel,
        out_shape=(
            pltpu.VMEM(populations.shape, F32),
            pltpu.VMEM((4, IMG // (ND * NR), IMG), F32),
        ),
        in_specs=[anywhere, anywhere, anywhere, vmem],
        out_specs=(vmem, vmem),
        scratch_shapes=[
            pltpu.VMEM((NZL, NYL, NX), jnp.int32),
            pltpu.VMEM((NZL, NYL, NX), jnp.int32),
            pltpu.VMEM((NQ, NZL + 2, 2, 48, 128), F32),
            pltpu.VMEM((NQ, NZL + 2, 2, 48, 128), F32),
            pltpu.VMEM((2, 2, 64, 128), F32),
            pltpu.VMEM((2, 2, 64, 128), F32),
            pltpu.VMEM((2, 4, 8, 128), F32),
            pltpu.VMEM((2, 4, 8, 128), F32),
            pltpu.VMEM((4, 4, 2, 8, 128), F32),
            pltpu.VMEM((4, NZL, 48, NX), F32),
            pltpu.VMEM((2, 3, 8, NX), F32),
            pltpu.VMEM((2, 3, 8, NX), F32),
            pltpu.VMEM((128, 96), BF16),
            pltpu.VMEM((IMG, NX), BF16),
            pltpu.VMEM((NZL, 2, 2, 256, NX), BF16),
            pltpu.VMEM((2, 2, 4, 128, 128), F32),
            pltpu.VMEM((2, 4, 128, 128), F32),
            pltpu.VMEM((2, NC, 4, 8, 128), F32),
            pltpu.VMEM((2, NC, 4, 8, 128), F32),
            pltpu.VMEM((NR, 16, 128), F32),
            pltpu.VMEM((NR, 16, 128), F32),
            dma((NZL + 2,)), dma((2, 2, 4)), dma((2, 2, 4)), dma((2, 12)), dma((2, 12)), dma((2, 2)), dma((2, 2)), dma((2, 2)),
            dma((2, NC)), dma((2, NC)), dma((NR,)), dma((NR,)), pltpu.SemaphoreType.REGULAR,
        ],
        compiler_params=pltpu.CompilerParams(
            collective_id=0, has_side_effects=True, vmem_limit_bytes=56 * 2**20
        ),
        name="vessel",
    )(populations, fluid_mask, tissue_tag, colour_table)
    return pl.pallas_call(
        deliver,
        out_shape=(
            jax.ShapeDtypeStruct(populations.shape, F32),
            jax.ShapeDtypeStruct((4, IMG // (ND * NR), IMG), F32),
        ),
        in_specs=[vmem, vmem],
        out_specs=(anywhere, anywhere),
        scratch_shapes=[dma((8,))],
        compiler_params=pltpu.CompilerParams(vmem_limit_bytes=2**20),
        name="deliver",
    )(advanced, drawn)


def deliver(advanced, drawn, adv, image, sem):
    parts = [slice(3 * n, min(3 * n + 3, NQ)) for n in range(7)]
    copies = [pltpu.make_async_copy(advanced.at[p], adv.at[p], sem.at[n]) for n, p in enumerate(parts)]
    copies.append(pltpu.make_async_copy(drawn, image, sem.at[7]))
    for copy in copies:
        copy.start()
    for copy in copies:
        copy.wait()


def solution(mesh):
    placed = (
        P(None, "depth", "rows", None),
        P("depth", "rows", None),
        P("depth", "rows", None),
        P(),
    )
    return jax.shard_map(
        shards,
        mesh=mesh,
        in_specs=placed,
        out_specs=(P(None, "depth", "rows", None), P(None, ("rows", "depth"), None)),
        check_vma=False,
    )
```

```python
import functools

import jax
import jax.numpy as jnp
from jax import lax
from jax.experimental import pallas as pl
from jax.experimental.pallas import tpu as pltpu
from jax.sharding import PartitionSpec as P

F32 = jnp.float32
BF16 = jnp.bfloat16
MESH = pl.DeviceIdType.MESH

VELOCITIES = (
    (0, 0, 0), (1, 0, 0), (-1, 0, 0), (0, 1, 0), (0, -1, 0), (0, 0, 1), (0, 0, -1),
    (1, 1, 0), (-1, -1, 0), (1, -1, 0), (-1, 1, 0),
    (1, 0, 1), (-1, 0, -1), (1, 0, -1), (-1, 0, 1),
    (0, 1, 1), (0, -1, -1), (0, 1, -1), (0, -1, 1),
)
OPPOSITE = (0, 2, 1, 4, 3, 6, 5, 8, 7, 10, 9, 12, 11, 14, 13, 16, 15, 18, 17)
PAIRS = tuple((q, q + 1) for q in range(1, 19, 2))
NU_ZERO = 0.12
NU_INFINITY = 0.02
LAMBDA_TIME = 15.0
POWER_INDEX = 0.3568
TAU_ZERO = 0.8
SPEED_SCALE = 0.04
SHEAR_SCALE = 0.07

ORDER = (16, 6, 12, 13, 17, 3, 7, 10, 15, 5, 11, 14, 18, 4, 8, 9, 0, 1, 2)
POS = tuple(ORDER.index(q) for q in range(19))
UP_Z, DOWN_Z = 8, 0
UP_Y = (4, 5, 6, 7, 8)
DOWN_Y = (12, 13, 14, 15, 0)
WALL = -1e30
WALL_REST = (-1e8, -1e12)
LIMIT = -1e5

RED_STEPS, GREEN_STEPS = 32767.0, 65535.0

NQ, NZL, NYL, NX = 19, 6, 32, 256
ND, NR, NC = 32, 4, 16
IMG = 512


def analyse(f, fluid=None, wall=None):
    sums = [f[a] + f[b] for a, b in PAIRS]
    diffs = [f[a] - f[b] for a, b in PAIRS]
    density = ((f[0] + sums[0]) + (sums[1] + sums[2])) + (
        ((sums[3] + sums[4]) + (sums[5] + sums[6])) + (sums[7] + sums[8])
    )
    mx = diffs[0] + ((diffs[3] + diffs[4]) + (diffs[5] + diffs[6]))
    my = diffs[1] + ((diffs[3] - diffs[4]) + (diffs[7] + diffs[8]))
    mz = diffs[2] + ((diffs[5] - diffs[6]) + (diffs[7] - diffs[8]))
    inverse = 1.0 / density
    third = (mx * (1.0 / 3.0), my * (1.0 / 3.0), mz * (1.0 / 3.0))
    hx, hy, hz = (0.5 * q for q in third)
    squares = [q * q for q in third]
    total = squares[0] + squares[1] + squares[2]
    axis_scale = 4.5 * inverse
    diag_scale = 9.0 * inverse
    rest = density - 3.0 * (total * axis_scale)
    if wall is not None:
        rest = jnp.where(fluid, rest, wall)
    axis_rest, diag_rest = rest * (1.0 / 9.0), rest * (1.0 / 18.0)
    diag = (hx + hy, hx - hy, hx + hz, hx - hz, hy + hz, hy - hz)
    even = [(sums[k] - axis_rest) - axis_scale * squares[k] for k in range(3)]
    even += [(sums[3 + k] - diag_rest) - diag_scale * (diag[k] * diag[k]) for k in range(6)]
    odd = [diffs[k] - third[k] for k in range(3)] + [diffs[3 + k] - diag[k] for k in range(6)]
    pxx = even[0] + ((even[3] + even[4]) + (even[5] + even[6]))
    pyy = even[1] + ((even[3] + even[4]) + (even[7] + even[8]))
    pzz = even[2] + ((even[5] + even[6]) + (even[7] + even[8]))
    pxy = even[3] - even[4]
    pxz = even[5] - even[6]
    pyz = even[7] - even[8]
    contracted = (pxx * pxx + pyy * pyy + pzz * pzz) + 2.0 * (pxy * pxy + pxz * pxz + pyz * pyz)
    return inverse, total, rest, even, odd, 2.0 * contracted + 1e-10


def collide(f, fluid, wall):
    inverse, _, rest, even, odd, stress = analyse(f, fluid, wall)
    squared = ((LAMBDA_TIME * 1.5 / TAU_ZERO) ** 2) * ((inverse * inverse) * stress)
    factor = jnp.exp(((POWER_INDEX - 1.0) / 2.0) * jnp.log(1.0 + squared))
    half = 1.0 / ((6.0 * NU_INFINITY + 1.0) + (6.0 * (NU_ZERO - NU_INFINITY)) * factor)
    out = [None] * 19
    out[0] = f[0] - (half + half) * (f[0] - rest * (1.0 / 3.0))
    for k, (a, b) in enumerate(PAIRS):
        s, d = half * even[k], half * odd[k]
        out[a] = f[a] - (s + d)
        out[b] = f[b] - (s - d)
    return out


def diagnose(f):
    inverse, total, _, _, _, stress = analyse(f)
    square = (9.0 * total) * (inverse * inverse) + 1e-12
    speed = square * lax.rsqrt(square)
    shear = (1.5 / TAU_ZERO) * inverse * (stress * lax.rsqrt(stress))
    return speed, shear


def kernel(
    pops, mask_in, tag_in, table, pbuf, image,
    mask, tag, r1, r2, ysend, yrecv, csend, crecv, bins, pairs, cbuf, ssend, srecv, wcols, wrows, vbuf,
    acc, xrecv, pieces, gathered, fsend, frecv,
    in_sem, ls_sem, lr_sem, hs_sem, hr_sem, c_send_sem, c_recv_sem, x_sem, g_send_sem, g_recv_sem, f_send_sem, f_recv_sem, ready,
):
    d = lax.axis_index("depth")
    r = lax.axis_index("rows")
    core = lax.rem(d, 2)
    chip = d // 2
    up_d, down_d = lax.rem(d + 1, ND), lax.rem(d + ND - 1, ND)
    up_r, down_r = lax.rem(r + 1, NR), lax.rem(r + NR - 1, NR)

    def at(dd, rr):
        return {"depth": dd, "rows": rr}

    barrier = pltpu.get_barrier_semaphore()
    row_first = (chip // 4) * 4
    columns_peers = [at(2 * lax.rem(chip + 4 * k, NC) + core, r) for k in (2, 1, 3)]
    peers = [at(up_d, up_r), at(up_d, down_r), at(down_d, up_r), at(down_d, down_r)]
    peers += [at(d, lax.rem(r + 2, NR))]
    peers += columns_peers
    peers += [at(2 * (row_first + lax.rem(chip + k, 4)) + core, r) for k in (2, 1, 3)]
    peers += [at(up_d, r), at(down_d, r), at(d, up_r), at(d, down_r), at(d + 1 - 2 * core, r)]
    for peer in peers:
        pl.semaphore_signal(barrier, inc=1, device_id=peer, device_id_type=MESH)

    loads = [pltpu.make_async_copy(pops.at[:, z], pbuf.at[:, z], in_sem.at[z]) for z in range(NZL)]
    loads.append(pltpu.make_async_copy(mask_in, mask, in_sem.at[NZL]))
    loads.append(pltpu.make_async_copy(tag_in, tag, in_sem.at[NZL + 1]))
    for n in (NZL, 0, 5, 1, 2, 3, 4, NZL + 1):
        loads[n].start()

    lane = lax.broadcasted_iota(jnp.int32, (8, 128), 1)
    first_lane, last_lane = lane == 0, lane == 127
    first_limit = jnp.where(first_lane, 1e30, LIMIT)
    last_limit = jnp.where(last_lane, 1e30, LIMIT)

    jj = lax.broadcasted_iota(jnp.int32, (128, 96), 0).astype(F32)
    yy = lax.broadcasted_iota(jnp.int32, (128, 96), 1)
    yy = (jnp.where(yy >= 48, yy - 48, yy) - 8).astype(F32)
    wcols[...] = jnp.maximum(0.0, 1.0 - jnp.abs((jj + 0.5) * 0.25 - 0.5 - yy)).astype(BF16)

    def fill_rows(b, carry):
        rho = b * 64 + lax.broadcasted_iota(jnp.int32, (64, 128), 0)
        ii = (
            (rho >> 8) * 256 + ((rho >> 2) & 1) * 128 + ((rho >> 3) & 15) * 8 + ((rho >> 7) & 1) * 4 + (rho & 3)
        ).astype(F32)
        centre = ii * 0.5 - 0.25
        for h in range(2):
            xx = (lax.broadcasted_iota(jnp.int32, (64, 128), 1) + h * 128).astype(F32)
            wt = jnp.maximum(0.0, 1.0 - jnp.abs(centre - xx)).astype(BF16)
            rows = pl.ds(pl.multiple_of(b * 64, 64), 64)
            wrows[rows, h * 128:(h + 1) * 128] = wt
        return carry

    lax.fori_loop(0, IMG // 64, fill_rows, 0)

    low_lanes = lane < 64
    for k in range(4):
        for parity in range(2):
            index = ((lane * 2) & 127) + parity
            entries = []
            for c in range(4):
                halves = [jnp.broadcast_to(table[k, c:c + 1, h * 128:(h + 1) * 128], (8, 128)) for h in range(2)]
                taken = [jnp.take_along_axis(half, index, axis=1, mode="promise_in_bounds") for half in halves]
                entries.append(jnp.where(low_lanes, taken[0], taken[1]))
            red = (entries[0] * RED_STEPS + 0.5).astype(jnp.int32)
            green = (entries[1] * GREEN_STEPS + 0.5).astype(jnp.int32)
            pairs[k, parity] = red * 65536 + green
            for c in (2, 3):
                bins[k, c - 2, parity] = entries[c]

    for rel in (r1, r2):
        @pl.when(d == 0)
        def _():
            rel[UP_Z:UP_Z + 5, 0, :, 8:40, :] = jnp.full((5, 2, 32, 128), WALL, F32)

        @pl.when(d == ND - 1)
        def _():
            rel[DOWN_Z:DOWN_Z + 5, 7, :, 8:40, :] = jnp.full((5, 2, 32, 128), WALL, F32)

    def clear(z, carry):
        for c in range(4):
            cbuf[c, z, 0:8, :] = jnp.zeros((8, NX), F32)
            cbuf[c, z, 40:48, :] = jnp.zeros((8, NX), F32)
        return carry

    lax.fori_loop(0, NZL, clear, 0)

    def fluid_tiles(z, t):
        rows = pl.ds(pl.multiple_of(8 * t, 8), 8)
        return [mask[z, rows, h * 128:(h + 1) * 128] > 0 for h in range(2)]

    def store_relaxed(target, z, t, h, relaxed):
        rows = pl.ds(pl.multiple_of(8 * t + 8, 8), 8)
        for q in range(19):
            target[POS[q], z + 1, h, rows, :] = relaxed[q]

    def first_tile(z, t):
        rows = pl.ds(pl.multiple_of(8 * t, 8), 8)
        fluids = fluid_tiles(z, t)
        for h in range(2):
            f = [pbuf[q, z, rows, h * 128:(h + 1) * 128] for q in range(19)]
            store_relaxed(r1, z, t, h, collide(f, fluids[h], WALL_REST[0]))

    def arrive(source, z, t):
        own = pl.ds(pl.multiple_of(8 * t + 8, 8), 8)
        out = [[None] * 19, [None] * 19]
        for q in range(19):
            cx, cy, cz = VELOCITIES[q]
            if q == 0:
                for h in range(2):
                    out[h][0] = source[POS[0], z + 1, h, own, :]
                continue
            rows = own if cy == 0 else pl.ds(8 * t + 8 - cy, 8)
            a = [source[POS[q], z + 1 - cz, h, rows, :] for h in range(2)]
            limits = [LIMIT, LIMIT]
            if cx == 1:
                b0, b1 = pltpu.roll(a[0], 1, 1), pltpu.roll(a[1], 1, 1)
                a = [b0, jnp.where(first_lane, b0, b1)]
                limits[0] = first_limit
            elif cx == -1:
                b0, b1 = pltpu.roll(a[0], 127, 1), pltpu.roll(a[1], 127, 1)
                a = [jnp.where(last_lane, b1, b0), b1]
                limits[1] = last_limit
            for h in range(2):
                back = source[POS[OPPOSITE[q]], z + 1, h, own, :]
                out[h][q] = jnp.where(a[h] > limits[h], a[h], back)
        return out

    def second_tile(z, t):
        fluids = fluid_tiles(z, t)
        f = arrive(r1, z, t)
        for h in range(2):
            store_relaxed(r2, z, t, h, collide(f[h], fluids[h], WALL_REST[1]))

    def lookup(tables, index, tags):
        picked = [jnp.take_along_axis(each, index, axis=1, mode="promise_in_bounds") for each in tables]
        return jnp.where(
            tags[0], jnp.where(tags[1], picked[3], picked[2]), jnp.where(tags[1], picked[1], picked[0])
        )

    def lookup_pair(parity, index, tags):
        word = lookup([pairs[k, parity] for k in range(4)], index, tags)
        return (word >> 16).astype(F32), (word & 65535).astype(F32)

    def lookup_one(c, parity, index, tags):
        return lookup([bins[k, c - 2, parity] for k in range(4)], index, tags)

    def classify(z, t, places):
        rows = pl.ds(pl.multiple_of(8 * t, 8), 8)
        padded = pl.ds(pl.multiple_of(8 * t + 8, 8), 8)
        fluids = fluid_tiles(z, t)
        for h in range(2):
            lanes = slice(h * 128, (h + 1) * 128)
            tags = tag[z, rows, lanes]
            tags = (tags >= 2, (tags & 1) == 1)
            place = []
            for where in places[2 * h:2 * h + 2]:
                lower = jnp.clip(where.astype(jnp.int32), 0, 254)
                even, odd = (lower + 1) >> 1, lower >> 1
                place.append((1.0 - jnp.abs(where - (even + even).astype(F32)), even, odd))
            result = []
            for (share, even, odd), c in zip(place, (2, 3)):
                at_odd = [lookup_one(c, 1, odd, tags)]
                if c == 2:
                    at_odd += lookup_pair(1, odd, tags)
                at_even = [lookup_one(c, 0, even, tags)]
                if c == 2:
                    at_even += lookup_pair(0, even, tags)
                result += [a + share * (b - a) for a, b in zip(at_odd, at_even)]
            blue, red, green, opacity = result
            result = [red * (1.0 / RED_STEPS), green * (1.0 / GREEN_STEPS), blue, opacity]
            coverage = jnp.where(fluids[h], result[3] * (3.0 / (NZL * ND)), 0.0)
            for c in range(3):
                cbuf[c, z, padded, lanes] = result[c] * coverage
            cbuf[3, z, padded, lanes] = coverage

    def third_tile(z, t):
        fluids = fluid_tiles(z, t)
        rows = pl.ds(pl.multiple_of(8 * t, 8), 8)
        f = arrive(r2, z, t)
        places = []
        for h in range(2):
            lanes = slice(h * 128, (h + 1) * 128)
            for q in range(19):
                pbuf[q, z, rows, lanes] = jnp.where(fluids[h], f[h][q], pbuf[q, z, rows, lanes])
            for value, scale in zip(diagnose(f[h]), (SPEED_SCALE, SHEAR_SCALE)):
                places.append(jnp.where(fluids[h], 255.0 * (value / (value + scale)), 0.0))
        return tuple(places)

    def tiles(count, body, z_of, t_of):
        def step(i, carry):
            body(z_of(i), t_of(i))
            return carry

        lax.fori_loop(0, count, step, 0, unroll=4)

    def outer_tiles(body, before, after):
        for t in range(4):
            if before is not None:
                before(t)
            body(5, t)
            body(0, t)
            if after is not None and t:
                start(after[2 * t - 2:2 * t])

    def remote(src, dst, send, recv, target):
        return pltpu.make_async_remote_copy(
            src_ref=src, dst_ref=dst, send_sem=send, recv_sem=recv, device_id=target, device_id_type=MESH
        )

    to_up, to_down, from_down, from_up = d < ND - 1, d > 0, d > 0, d < ND - 1
    to_right, to_left, from_left, from_right = r < NR - 1, r > 0, r > 0, r < NR - 1

    def start(copies):
        for copy, sends, _ in copies:
            pl.when(sends)(copy.start)

    def finish(copies):
        for copy, sends, receives in copies:
            pl.when(receives)(copy.wait_recv)
            pl.when(sends)(copy.wait_send)

    def layer_copies(s, rel, t):
        rows = pl.ds(8 * t + 8, 8)
        return [
            (remote(rel.at[UP_Z:UP_Z + 5, 6, :, rows, :], rel.at[UP_Z:UP_Z + 5, 0, :, rows, :],
                    ls_sem.at[s, 0, t], lr_sem.at[s, 0, t], at(up_d, r)), to_up, from_down),
            (remote(rel.at[DOWN_Z:DOWN_Z + 5, 1, :, rows, :], rel.at[DOWN_Z:DOWN_Z + 5, 7, :, rows, :],
                    ls_sem.at[s, 1, t], lr_sem.at[s, 1, t], at(down_d, r)), to_down, from_up),
        ]

    sides = ((at(d, up_r), to_right, from_left), (at(d, down_r), to_left, from_right))
    corner_sides = (
        (at(up_d, up_r), to_up & to_right, from_down & from_left),
        (at(down_d, down_r), to_down & to_left, from_up & from_right),
        (at(down_d, up_r), to_down & to_right, from_up & from_left),
        (at(up_d, down_r), to_up & to_left, from_down & from_right),
    )

    def halo_copies(s, rel):
        rows = [
            [
                (remote(ysend.at[s, side, part], yrecv.at[s, side, part], hs_sem.at[s, 4 * n + side],
                        hr_sem.at[s, 4 * n + side], target), sends, receives)
                for side, (target, sends, receives) in enumerate(sides)
            ]
            for n, part in enumerate((slice(0, 40), slice(40, 64)))
        ]
        corners = [
            (remote(csend.at[s, n], crecv.at[s, n], hs_sem.at[s, 8 + n], hr_sem.at[s, 8 + n], target), sends, receives)
            for n, (target, sends, receives) in enumerate(corner_sides)
        ]
        return rows, corners

    corner_places = ((15, 6, 39, 0, 7), (16, 1, 8, 7, 40), (17, 1, 39, 7, 7), (18, 6, 8, 0, 40))

    def pack_corners(s, rel):
        for n, (q, layer, row, _, _) in enumerate(corner_places):
            for h in range(2):
                csend[s, n, h:h + 1, :] = rel[POS[q], layer, h, row:row + 1, :]

    row_places = [[(10 * n + k, z, k // 2, k % 2) for n, z in enumerate(layers) for k in range(10)] for layers in (
        (1, 2, 3, 4), (None, None, None, None, 0, 5))]
    row_places = [[p for p in places if p[1] is not None] for places in row_places]

    def pack_rows(s, rel, part):
        for side, (slots, row) in enumerate(((UP_Y, 39), (DOWN_Y, 8))):
            for place, z, n, h in row_places[part]:
                ysend[s, side, place:place + 1, :] = rel[slots[n], z + 1, h, row:row + 1, :]

    def unpack_rows(s, rel, part):
        for side, (slots, row, edge) in enumerate(((UP_Y, 7, r == 0), (DOWN_Y, 40, r == NR - 1))):
            for place, z, n, h in row_places[part]:
                rel[slots[n], z + 1, h, row:row + 1, :] = jnp.where(
                    edge, WALL, yrecv[s, side, place:place + 1, :]
                )

    def take_layers(copies, t):
        finish(copies[2 * t:2 * t + 2])

    def take_corners(s, copies, rel):
        finish(copies)
        edges = (
            (d == 0) | (r == 0), (d == ND - 1) | (r == NR - 1), (d == ND - 1) | (r == 0), (d == 0) | (r == NR - 1)
        )
        for n, (q, _, _, layer, row) in enumerate(corner_places):
            for h in range(2):
                rel[POS[q], layer, h, row:row + 1, :] = jnp.where(edges[n], WALL, crecv[s, n, h:h + 1, :])

    loads[NZL].wait()
    loads[0].wait()
    loads[5].wait()
    outer_tiles(first_tile, None, None)
    pack_corners(0, r1)
    pl.semaphore_wait(barrier, len(peers))
    layers1 = [copy for t in range(4) for copy in layer_copies(0, r1, t)]
    rows1, corners1 = halo_copies(0, r1)
    start(layers1 + corners1)
    for peer in columns_peers:
        pl.semaphore_signal(ready, inc=1, device_id=peer, device_id_type=MESH)
    pack_rows(0, r1, 1)
    start(rows1[1])
    for z in range(1, 5):
        loads[z].wait()
    tiles(8, first_tile, lambda i: 1 + (i >> 1), lambda i: 3 * (i & 1))
    pack_rows(0, r1, 0)
    start(rows1[0])
    tiles(8, first_tile, lambda i: 1 + (i >> 1), lambda i: 1 + (i & 1))

    tiles(8, second_tile, lambda i: 1 + (i >> 1), lambda i: 1 + (i & 1))
    for part in (1, 0):
        finish(rows1[part])
        unpack_rows(0, r1, part)
    tiles(8, second_tile, lambda i: 1 + (i >> 1), lambda i: 3 * (i & 1))
    rows2, corners2 = halo_copies(1, r2)
    pack_rows(1, r2, 0)
    start(rows2[0])
    layers2 = [copy for t in range(4) for copy in layer_copies(1, r2, t)]
    take_corners(0, corners1, r1)
    take_layers(layers1, 0)
    outer_tiles(second_tile, lambda t: take_layers(layers1, t + 1) if t < 3 else None, layers2)
    pack_rows(1, r2, 1)
    pack_corners(1, r2)
    start(layers2[6:] + rows2[1] + corners2)

    loads[NZL + 1].wait()

    def third_tiles(count, z_of, t_of, before, carry):
        def step(i, places):
            last = jnp.maximum(i - 1, 0)
            first = i == 0
            following = third_tile(z_of(i), t_of(i))
            classify(
                jnp.where(first, before[0], z_of(last)), jnp.where(first, before[1], t_of(last)), places
            )
            return following

        return lax.fori_loop(0, count, step, carry)

    site_copies = [
        [
            (remote(ssend.at[side, slots], srecv.at[side, slots], c_send_sem.at[part, side],
                    c_recv_sem.at[part, side], target), sends, receives)
            for side, (target, sends, receives) in enumerate(sides)
        ]
        for part, slots in enumerate((slice(0, 2), slice(2, 3)))
    ]
    def pack_sites(part, layers):
        for n, z in enumerate(layers):
            for side, row in enumerate((39, 8)):
                for c in range(4):
                    place = 4 * (n % 2) + c
                    ssend[side, 2 * part + n // 2, place:place + 1, :] = cbuf[c, z, row:row + 1, :]
        start(site_copies[part])

    def unpack_sites(part, layers):
        finish(site_copies[part])
        for n, z in enumerate(layers):
            for side, (row, edge) in enumerate(((7, r == 0), (40, r == NR - 1))):
                for c in range(4):
                    place = 4 * (n % 2) + c
                    cbuf[c, z, row:row + 1, :] = jnp.where(
                        edge, 0.0, srecv[side, 2 * part + n // 2, place:place + 1, :]
                    )

    places = tuple(jnp.zeros((8, 128), F32) for _ in range(4))
    places = third_tiles(8, lambda i: 1 + (i >> 1), lambda i: 1 + (i & 1), (1, 1), places)
    finish(rows2[0])
    unpack_rows(1, r2, 0)
    places = third_tiles(4, lambda i: 2 + (i >> 1), lambda i: 3 * (i & 1), (4, 2), places)
    finish(rows2[1])
    unpack_rows(1, r2, 1)
    places = third_tiles(4, lambda i: 1 + 3 * (i >> 1), lambda i: 3 * (i & 1), (3, 3), places)
    classify(4, 3, places)
    pack_sites(0, (1, 2, 3, 4))
    take_corners(1, corners2, r2)
    for t in range(2):
        take_layers(layers2, t)
    places = third_tiles(2, lambda i: i * 5, lambda i: 0, (4, 3), places)
    for t in range(2, 4):
        take_layers(layers2, t)
    places = third_tiles(2, lambda i: i * 5, lambda i: 3, (5, 0), places)

    classify(5, 3, places)
    pack_sites(1, (0, 5))
    places = third_tiles(4, lambda i: (i >> 1) * 5, lambda i: 1 + (i & 1), (5, 3), places)
    classify(5, 2, places)

    def columns(z):
        for c in range(4):
            sites = cbuf[c, z]
            high = sites.astype(BF16)
            low = (sites - high.astype(F32)).astype(BF16)
            wide = lax.dot_general(
                wcols[...], jnp.concatenate([high, low], axis=0), (((1,), (0,)), ((), ())),
                preferred_element_type=F32,
            )
            high = wide.astype(BF16)
            low = (wide - high.astype(F32)).astype(BF16)
            place = slice((c % 2) * 128, (c % 2) * 128 + 128)
            vbuf[z, c // 2, 0, place, :] = high
            vbuf[z, c // 2, 1, place, :] = low

    def columns_step(i, carry):
        columns(i + 1)
        return carry

    def render(group, layers):
        weights = wrows[group * 256:(group + 1) * 256, :]
        for z in layers:
            drawn = []
            for pair in (1, 0):
                parts = [
                    lax.dot_general(
                        weights, vbuf[z, pair, n], (((1,), (1,)), ((), ())), preferred_element_type=F32
                    )
                    for n in range(2)
                ]
                drawn.append(parts[0] + parts[1])
            for half in range(2):
                rows = slice(half * 128, half * 128 + 128)
                parts = [drawn[1 - c // 2][rows, (c % 2) * 128:(c % 2) * 128 + 128] for c in range(4)]
                if z == 0:
                    through = 1.0 - parts[3]
                    parts = [parts[c] + through * acc[group, half, c] for c in range(4)]
                elif z > 1:
                    through = 1.0 - acc[group, half, 3]
                    parts = [acc[group, half, c] + through * parts[c] for c in range(4)]
                for c in range(4):
                    acc[group, half, c] = parts[c]

    def columns_inner(i, carry):
        columns(i + 1)
        return carry

    def columns_outer(i, carry):
        columns(5 * i)
        return carry

    unpack_sites(0, (1, 2, 3, 4))
    lax.fori_loop(0, 4, columns_inner, 0, unroll=2)
    render(0, (1, 2, 3, 4))
    unpack_sites(1, (0, 5))
    lax.fori_loop(0, 2, columns_outer, 0, unroll=2)

    partner = at(d + 1 - 2 * core, r)
    swaps = [
        remote(acc.at[group, 1 - core], xrecv.at[group], x_sem.at[0, group], x_sem.at[1, group], partner)
        for group in range(2)
    ]
    chips = list(range(1, NC))
    exchange = [[], []]
    for group in range(2):
        for k in chips:
            other = lax.rem(chip + k, NC)
            exchange[group].append(
                remote(pieces.at[group, other], gathered.at[group, chip],
                       g_send_sem.at[group, k], g_recv_sem.at[group, k], at(2 * other + core, r))
            )

    def join(group):
        def step(n, carry):
            rows = pl.ds(pl.multiple_of(n * 8, 8), 8)
            front = core == 0
            mine = [acc[group, core, c, rows, :] for c in range(4)]
            theirs = [xrecv[group, c, rows, :] for c in range(4)]
            near = [jnp.where(front, mine[c], theirs[c]) for c in range(4)]
            far = [jnp.where(front, theirs[c], mine[c]) for c in range(4)]
            through = 1.0 - near[3]
            for c in range(4):
                pieces[group, n, c] = near[c] + through * far[c]
            return carry

        lax.fori_loop(0, NC, step, 0, unroll=4)
        if group == 0:
            pl.semaphore_wait(ready, len(columns_peers))
        for copy in exchange[group]:
            copy.start()
        gathered[group, chip] = pieces[group, chip]

    render(0, (0, 5))
    swaps[0].start()
    render(1, (1, 2, 3, 4, 0, 5))
    swaps[1].start()
    swaps[0].wait()
    join(0)
    swaps[1].wait()
    join(1)

    for group in range(2):
        for copy in exchange[group]:
            copy.wait()
        final = [gathered[group, 0, c] for c in range(4)]
        for n in range(1, NC):
            through = 1.0 - final[3]
            final = [final[c] + through * gathered[group, n, c] for c in range(4)]
        for half in range(2):
            for c in range(4):
                fsend[2 * group + half, 4 * c:4 * c + 4, :] = final[c][4 * half:4 * half + 4, :]
    last = []
    for k in range(1, NR):
        other = lax.rem(r + k, NR)
        last.append(remote(fsend.at[other], frecv.at[r], f_send_sem.at[k], f_recv_sem.at[k], at(d, other)))
        last[-1].start()
    frecv[r] = fsend[r]
    for copy in last:
        copy.wait()
    for rr in range(NR):
        for c in range(4):
            image[c, :, rr * 128:(rr + 1) * 128] = frecv[rr, 4 * c:4 * c + 4, :]


def shards(populations, fluid_mask, tissue_tag, colour_table):
    dma = pltpu.SemaphoreType.DMA
    vmem = pl.BlockSpec(memory_space=pltpu.VMEM)
    anywhere = pl.BlockSpec(memory_space=pl.ANY)
    advanced, drawn = pl.pallas_call(
        kernel,
        out_shape=(
            pltpu.VMEM(populations.shape, F32),
            pltpu.VMEM((4, IMG // (ND * NR), IMG), F32),
        ),
        in_specs=[anywhere, anywhere, anywhere, vmem],
        out_specs=(vmem, vmem),
        scratch_shapes=[
            pltpu.VMEM((NZL, NYL, NX), jnp.int32),
            pltpu.VMEM((NZL, NYL, NX), jnp.int32),
            pltpu.VMEM((NQ, NZL + 2, 2, 48, 128), F32),
            pltpu.VMEM((NQ, NZL + 2, 2, 48, 128), F32),
            pltpu.VMEM((2, 2, 64, 128), F32),
            pltpu.VMEM((2, 2, 64, 128), F32),
            pltpu.VMEM((2, 4, 8, 128), F32),
            pltpu.VMEM((2, 4, 8, 128), F32),
            pltpu.VMEM((4, 2, 2, 8, 128), F32),
            pltpu.VMEM((4, 2, 8, 128), jnp.int32),
            pltpu.VMEM((4, NZL, 48, NX), F32),
            pltpu.VMEM((2, 3, 8, NX), F32),
            pltpu.VMEM((2, 3, 8, NX), F32),
            pltpu.VMEM((128, 96), BF16),
            pltpu.VMEM((IMG, NX), BF16),
            pltpu.VMEM((NZL, 2, 2, 256, NX), BF16),
            pltpu.VMEM((2, 2, 4, 128, 128), F32),
            pltpu.VMEM((2, 4, 128, 128), F32),
            pltpu.VMEM((2, NC, 4, 8, 128), F32),
            pltpu.VMEM((2, NC, 4, 8, 128), F32),
            pltpu.VMEM((NR, 16, 128), F32),
            pltpu.VMEM((NR, 16, 128), F32),
            dma((NZL + 2,)), dma((2, 2, 4)), dma((2, 2, 4)), dma((2, 12)), dma((2, 12)), dma((2, 2)), dma((2, 2)), dma((2, 2)),
            dma((2, NC)), dma((2, NC)), dma((NR,)), dma((NR,)), pltpu.SemaphoreType.REGULAR,
        ],
        compiler_params=pltpu.CompilerParams(
            collective_id=0, has_side_effects=True, vmem_limit_bytes=56 * 2**20
        ),
        name="vessel",
    )(populations, fluid_mask, tissue_tag, colour_table)
    return pl.pallas_call(
        deliver,
        out_shape=(
            jax.ShapeDtypeStruct(populations.shape, F32),
            jax.ShapeDtypeStruct((4, IMG // (ND * NR), IMG), F32),
        ),
        in_specs=[vmem, vmem],
        out_specs=(anywhere, anywhere),
        scratch_shapes=[dma((8,))],
        compiler_params=pltpu.CompilerParams(vmem_limit_bytes=2**20),
        name="deliver",
    )(advanced, drawn)


def deliver(advanced, drawn, adv, image, sem):
    parts = [slice(3 * n, min(3 * n + 3, NQ)) for n in range(7)]
    copies = [pltpu.make_async_copy(advanced.at[p], adv.at[p], sem.at[n]) for n, p in enumerate(parts)]
    copies.append(pltpu.make_async_copy(drawn, image, sem.at[7]))
    for copy in copies:
        copy.start()
    for copy in copies:
        copy.wait()


def solution(mesh):
    placed = (
        P(None, "depth", "rows", None),
        P("depth", "rows", None),
        P("depth", "rows", None),
        P(),
    )
    return jax.shard_map(
        shards,
        mesh=mesh,
        in_specs=placed,
        out_specs=(P(None, "depth", "rows", None), P(None, ("rows", "depth"), None)),
        check_vma=False,
    )
```

```python
import functools

import jax
import jax.numpy as jnp
from jax import lax
from jax.experimental import pallas as pl
from jax.experimental.pallas import tpu as pltpu
from jax.sharding import PartitionSpec as P

F32 = jnp.float32
BF16 = jnp.bfloat16
MESH = pl.DeviceIdType.MESH

VELOCITIES = (
    (0, 0, 0), (1, 0, 0), (-1, 0, 0), (0, 1, 0), (0, -1, 0), (0, 0, 1), (0, 0, -1),
    (1, 1, 0), (-1, -1, 0), (1, -1, 0), (-1, 1, 0),
    (1, 0, 1), (-1, 0, -1), (1, 0, -1), (-1, 0, 1),
    (0, 1, 1), (0, -1, -1), (0, 1, -1), (0, -1, 1),
)
OPPOSITE = (0, 2, 1, 4, 3, 6, 5, 8, 7, 10, 9, 12, 11, 14, 13, 16, 15, 18, 17)
PAIRS = tuple((q, q + 1) for q in range(1, 19, 2))
NU_ZERO = 0.12
NU_INFINITY = 0.02
LAMBDA_TIME = 15.0
POWER_INDEX = 0.3568
TAU_ZERO = 0.8
SPEED_SCALE = 0.04
SHEAR_SCALE = 0.07

ORDER = (16, 6, 12, 13, 17, 3, 7, 10, 15, 5, 11, 14, 18, 4, 8, 9, 0, 1, 2)
POS = tuple(ORDER.index(q) for q in range(19))
UP_Z, DOWN_Z = 8, 0
UP_Y = (4, 5, 6, 7, 8)
DOWN_Y = (12, 13, 14, 15, 0)
WALL = -1e30
WALL_REST = (-1e8, -1e12)
LIMIT = -1e5

RED_STEPS, GREEN_STEPS = 32767.0, 65535.0

NQ, NZL, NYL, NX = 19, 6, 32, 256
ND, NR, NC = 32, 4, 16
IMG = 512


def analyse(f, fluid=None, wall=None):
    sums = [f[a] + f[b] for a, b in PAIRS]
    diffs = [f[a] - f[b] for a, b in PAIRS]
    density = ((f[0] + sums[0]) + (sums[1] + sums[2])) + (
        ((sums[3] + sums[4]) + (sums[5] + sums[6])) + (sums[7] + sums[8])
    )
    mx = diffs[0] + ((diffs[3] + diffs[4]) + (diffs[5] + diffs[6]))
    my = diffs[1] + ((diffs[3] - diffs[4]) + (diffs[7] + diffs[8]))
    mz = diffs[2] + ((diffs[5] - diffs[6]) + (diffs[7] - diffs[8]))
    inverse = 1.0 / density
    third = (mx * (1.0 / 3.0), my * (1.0 / 3.0), mz * (1.0 / 3.0))
    hx, hy, hz = (0.5 * q for q in third)
    squares = [q * q for q in third]
    total = squares[0] + squares[1] + squares[2]
    axis_scale = 4.5 * inverse
    diag_scale = 9.0 * inverse
    rest = density - 3.0 * (total * axis_scale)
    if wall is not None:
        rest = jnp.where(fluid, rest, wall)
    axis_rest, diag_rest = rest * (1.0 / 9.0), rest * (1.0 / 18.0)
    diag = (hx + hy, hx - hy, hx + hz, hx - hz, hy + hz, hy - hz)
    even = [(sums[k] - axis_rest) - axis_scale * squares[k] for k in range(3)]
    even += [(sums[3 + k] - diag_rest) - diag_scale * (diag[k] * diag[k]) for k in range(6)]
    odd = [diffs[k] - third[k] for k in range(3)] + [diffs[3 + k] - diag[k] for k in range(6)]
    pxx = even[0] + ((even[3] + even[4]) + (even[5] + even[6]))
    pyy = even[1] + ((even[3] + even[4]) + (even[7] + even[8]))
    pzz = even[2] + ((even[5] + even[6]) + (even[7] + even[8]))
    pxy = even[3] - even[4]
    pxz = even[5] - even[6]
    pyz = even[7] - even[8]
    contracted = (pxx * pxx + pyy * pyy + pzz * pzz) + 2.0 * (pxy * pxy + pxz * pxz + pyz * pyz)
    return inverse, total, rest, even, odd, 2.0 * contracted + 1e-10


def collide(f, fluid, wall):
    inverse, _, rest, even, odd, stress = analyse(f, fluid, wall)
    squared = ((LAMBDA_TIME * 1.5 / TAU_ZERO) ** 2) * ((inverse * inverse) * stress)
    factor = jnp.exp(((POWER_INDEX - 1.0) / 2.0) * jnp.log(1.0 + squared))
    half = 1.0 / ((6.0 * NU_INFINITY + 1.0) + (6.0 * (NU_ZERO - NU_INFINITY)) * factor)
    out = [None] * 19
    out[0] = f[0] - (half + half) * (f[0] - rest * (1.0 / 3.0))
    for k, (a, b) in enumerate(PAIRS):
        s, d = half * even[k], half * odd[k]
        out[a] = f[a] - (s + d)
        out[b] = f[b] - (s - d)
    return out


def diagnose(f):
    inverse, total, _, _, _, stress = analyse(f)
    square = (9.0 * total) * (inverse * inverse) + 1e-12
    speed = square * lax.rsqrt(square)
    shear = (1.5 / TAU_ZERO) * inverse * (stress * lax.rsqrt(stress))
    return speed, shear


def kernel(
    pops, mask_in, tag_in, table, pbuf, image,
    mask, tag, r1, r2, ysend, yrecv, csend, crecv, bins, pairs, cbuf, ssend, srecv, wcols, wrows, vbuf,
    acc, xrecv, pieces, gathered, fsend, frecv,
    in_sem, ls_sem, lr_sem, hs_sem, hr_sem, c_send_sem, c_recv_sem, x_sem, g_send_sem, g_recv_sem, f_send_sem, f_recv_sem, ready,
):
    d = lax.axis_index("depth")
    r = lax.axis_index("rows")
    core = lax.rem(d, 2)
    chip = d // 2
    up_d, down_d = lax.rem(d + 1, ND), lax.rem(d + ND - 1, ND)
    up_r, down_r = lax.rem(r + 1, NR), lax.rem(r + NR - 1, NR)

    def at(dd, rr):
        return {"depth": dd, "rows": rr}

    barrier = pltpu.get_barrier_semaphore()
    row_first = (chip // 4) * 4
    columns_peers = [at(2 * lax.rem(chip + 4 * k, NC) + core, r) for k in (2, 1, 3)]
    peers = [at(up_d, up_r), at(up_d, down_r), at(down_d, up_r), at(down_d, down_r)]
    peers += [at(d, lax.rem(r + 2, NR))]
    peers += columns_peers
    peers += [at(2 * (row_first + lax.rem(chip + k, 4)) + core, r) for k in (2, 1, 3)]
    peers += [at(up_d, r), at(down_d, r), at(d, up_r), at(d, down_r), at(d + 1 - 2 * core, r)]
    loads = [pltpu.make_async_copy(pops.at[:, z], pbuf.at[:, z], in_sem.at[z]) for z in range(NZL)]
    loads.append(pltpu.make_async_copy(mask_in, mask, in_sem.at[NZL]))
    loads.append(pltpu.make_async_copy(tag_in, tag, in_sem.at[NZL + 1]))
    for n in (NZL, 5, 0):
        loads[n].start()

    for peer in peers:
        pl.semaphore_signal(barrier, inc=1, device_id=peer, device_id_type=MESH)
    for n in (1, 2, 3, 4, NZL + 1):
        loads[n].start()


    lane = lax.broadcasted_iota(jnp.int32, (8, 128), 1)
    first_lane, last_lane = lane == 0, lane == 127
    first_limit = jnp.where(first_lane, 1e30, LIMIT)
    last_limit = jnp.where(last_lane, 1e30, LIMIT)

    jj = lax.broadcasted_iota(jnp.int32, (128, 96), 0).astype(F32)
    yy = lax.broadcasted_iota(jnp.int32, (128, 96), 1)
    yy = (jnp.where(yy >= 48, yy - 48, yy) - 8).astype(F32)
    wcols[...] = jnp.maximum(0.0, 1.0 - jnp.abs((jj + 0.5) * 0.25 - 0.5 - yy)).astype(BF16)

    def fill_rows(b, carry):
        rho = b * 64 + lax.broadcasted_iota(jnp.int32, (64, 128), 0)
        ii = (
            (rho >> 8) * 256 + ((rho >> 2) & 1) * 128 + ((rho >> 3) & 15) * 8 + ((rho >> 7) & 1) * 4 + (rho & 3)
        ).astype(F32)
        centre = ii * 0.5 - 0.25
        for h in range(2):
            xx = (lax.broadcasted_iota(jnp.int32, (64, 128), 1) + h * 128).astype(F32)
            wt = jnp.maximum(0.0, 1.0 - jnp.abs(centre - xx)).astype(BF16)
            rows = pl.ds(pl.multiple_of(b * 64, 64), 64)
            wrows[rows, h * 128:(h + 1) * 128] = wt
        return carry

    lax.fori_loop(0, IMG // 64, fill_rows, 0)

    low_lanes = lane < 64
    for k in range(4):
        for parity in range(2):
            index = ((lane * 2) & 127) + parity
            entries = []
            for c in range(4):
                halves = [jnp.broadcast_to(table[k, c:c + 1, h * 128:(h + 1) * 128], (8, 128)) for h in range(2)]
                taken = [jnp.take_along_axis(half, index, axis=1, mode="promise_in_bounds") for half in halves]
                entries.append(jnp.where(low_lanes, taken[0], taken[1]))
            red = (entries[0] * RED_STEPS + 0.5).astype(jnp.int32)
            green = (entries[1] * GREEN_STEPS + 0.5).astype(jnp.int32)
            pairs[k, parity] = red * 65536 + green
            for c in (2, 3):
                bins[k, c - 2, parity] = entries[c]

    for rel in (r1, r2):
        @pl.when(d == 0)
        def _():
            rel[UP_Z:UP_Z + 5, 0, :, 8:40, :] = jnp.full((5, 2, 32, 128), WALL, F32)

        @pl.when(d == ND - 1)
        def _():
            rel[DOWN_Z:DOWN_Z + 5, 7, :, 8:40, :] = jnp.full((5, 2, 32, 128), WALL, F32)

    def clear(z, carry):
        for c in range(4):
            cbuf[c, z, 0:8, :] = jnp.zeros((8, NX), F32)
            cbuf[c, z, 40:48, :] = jnp.zeros((8, NX), F32)
        return carry

    lax.fori_loop(0, NZL, clear, 0)

    def fluid_tiles(z, t):
        rows = pl.ds(pl.multiple_of(8 * t, 8), 8)
        return [mask[z, rows, h * 128:(h + 1) * 128] > 0 for h in range(2)]

    def store_relaxed(target, z, t, h, relaxed):
        rows = pl.ds(pl.multiple_of(8 * t + 8, 8), 8)
        for q in range(19):
            target[POS[q], z + 1, h, rows, :] = relaxed[q]

    def first_tile(z, t):
        rows = pl.ds(pl.multiple_of(8 * t, 8), 8)
        fluids = fluid_tiles(z, t)
        for h in range(2):
            f = [pbuf[q, z, rows, h * 128:(h + 1) * 128] for q in range(19)]
            store_relaxed(r1, z, t, h, collide(f, fluids[h], WALL_REST[0]))

    def arrive(source, z, t):
        own = pl.ds(pl.multiple_of(8 * t + 8, 8), 8)
        out = [[None] * 19, [None] * 19]
        for q in range(19):
            cx, cy, cz = VELOCITIES[q]
            if q == 0:
                for h in range(2):
                    out[h][0] = source[POS[0], z + 1, h, own, :]
                continue
            rows = own if cy == 0 else pl.ds(8 * t + 8 - cy, 8)
            a = [source[POS[q], z + 1 - cz, h, rows, :] for h in range(2)]
            limits = [LIMIT, LIMIT]
            if cx == 1:
                b0, b1 = pltpu.roll(a[0], 1, 1), pltpu.roll(a[1], 1, 1)
                a = [b0, jnp.where(first_lane, b0, b1)]
                limits[0] = first_limit
            elif cx == -1:
                b0, b1 = pltpu.roll(a[0], 127, 1), pltpu.roll(a[1], 127, 1)
                a = [jnp.where(last_lane, b1, b0), b1]
                limits[1] = last_limit
            for h in range(2):
                back = source[POS[OPPOSITE[q]], z + 1, h, own, :]
                out[h][q] = jnp.where(a[h] > limits[h], a[h], back)
        return out

    def second_tile(z, t):
        fluids = fluid_tiles(z, t)
        f = arrive(r1, z, t)
        for h in range(2):
            store_relaxed(r2, z, t, h, collide(f[h], fluids[h], WALL_REST[1]))

    def lookup(tables, index, tags):
        picked = [jnp.take_along_axis(each, index, axis=1, mode="promise_in_bounds") for each in tables]
        return jnp.where(
            tags[0], jnp.where(tags[1], picked[3], picked[2]), jnp.where(tags[1], picked[1], picked[0])
        )

    def lookup_pair(parity, index, tags):
        word = lookup([pairs[k, parity] for k in range(4)], index, tags)
        return (word >> 16).astype(F32), (word & 65535).astype(F32)

    def lookup_one(c, parity, index, tags):
        return lookup([bins[k, c - 2, parity] for k in range(4)], index, tags)

    def classify(z, t, places):
        rows = pl.ds(pl.multiple_of(8 * t, 8), 8)
        padded = pl.ds(pl.multiple_of(8 * t + 8, 8), 8)
        fluids = fluid_tiles(z, t)
        for h in range(2):
            lanes = slice(h * 128, (h + 1) * 128)
            tags = tag[z, rows, lanes]
            tags = (tags >= 2, (tags & 1) == 1)
            place = []
            for where in places[2 * h:2 * h + 2]:
                lower = jnp.clip(where.astype(jnp.int32), 0, 254)
                even, odd = (lower + 1) >> 1, lower >> 1
                place.append((1.0 - jnp.abs(where - (even + even).astype(F32)), even, odd))
            result = []
            for (share, even, odd), c in zip(place, (2, 3)):
                at_odd = [lookup_one(c, 1, odd, tags)]
                if c == 2:
                    at_odd += lookup_pair(1, odd, tags)
                at_even = [lookup_one(c, 0, even, tags)]
                if c == 2:
                    at_even += lookup_pair(0, even, tags)
                result += [a + share * (b - a) for a, b in zip(at_odd, at_even)]
            blue, red, green, opacity = result
            result = [red * (1.0 / RED_STEPS), green * (1.0 / GREEN_STEPS), blue, opacity]
            coverage = jnp.where(fluids[h], result[3] * (3.0 / (NZL * ND)), 0.0)
            for c in range(3):
                cbuf[c, z, padded, lanes] = result[c] * coverage
            cbuf[3, z, padded, lanes] = coverage

    def third_tile(z, t):
        fluids = fluid_tiles(z, t)
        rows = pl.ds(pl.multiple_of(8 * t, 8), 8)
        f = arrive(r2, z, t)
        places = []
        for h in range(2):
            lanes = slice(h * 128, (h + 1) * 128)
            for q in range(19):
                pbuf[q, z, rows, lanes] = jnp.where(fluids[h], f[h][q], pbuf[q, z, rows, lanes])
            for value, scale in zip(diagnose(f[h]), (SPEED_SCALE, SHEAR_SCALE)):
                places.append(jnp.where(fluids[h], 255.0 * (value / (value + scale)), 0.0))
        return tuple(places)

    def tiles(count, body, z_of, t_of):
        def step(i, carry):
            body(z_of(i), t_of(i))
            return carry

        lax.fori_loop(0, count, step, 0, unroll=4)

    def outer_tiles(body, before, after):
        for t in range(4):
            if before is not None:
                before(t)
            body(5, t)
            body(0, t)
            if after is not None and t:
                start(after[2 * t - 2:2 * t])

    def remote(src, dst, send, recv, target):
        return pltpu.make_async_remote_copy(
            src_ref=src, dst_ref=dst, send_sem=send, recv_sem=recv, device_id=target, device_id_type=MESH
        )

    to_up, to_down, from_down, from_up = d < ND - 1, d > 0, d > 0, d < ND - 1
    to_right, to_left, from_left, from_right = r < NR - 1, r > 0, r > 0, r < NR - 1

    def start(copies):
        for copy, sends, _ in copies:
            pl.when(sends)(copy.start)

    def finish(copies):
        for copy, sends, receives in copies:
            pl.when(receives)(copy.wait_recv)
            pl.when(sends)(copy.wait_send)

    def layer_copies(s, rel, t):
        rows = pl.ds(8 * t + 8, 8)
        return [
            (remote(rel.at[UP_Z:UP_Z + 5, 6, :, rows, :], rel.at[UP_Z:UP_Z + 5, 0, :, rows, :],
                    ls_sem.at[s, 0, t], lr_sem.at[s, 0, t], at(up_d, r)), to_up, from_down),
            (remote(rel.at[DOWN_Z:DOWN_Z + 5, 1, :, rows, :], rel.at[DOWN_Z:DOWN_Z + 5, 7, :, rows, :],
                    ls_sem.at[s, 1, t], lr_sem.at[s, 1, t], at(down_d, r)), to_down, from_up),
        ]

    sides = ((at(d, up_r), to_right, from_left), (at(d, down_r), to_left, from_right))
    corner_sides = (
        (at(up_d, up_r), to_up & to_right, from_down & from_left),
        (at(down_d, down_r), to_down & to_left, from_up & from_right),
        (at(down_d, up_r), to_down & to_right, from_up & from_left),
        (at(up_d, down_r), to_up & to_left, from_down & from_right),
    )

    def halo_copies(s, rel):
        rows = [
            [
                (remote(ysend.at[s, side, part], yrecv.at[s, side, part], hs_sem.at[s, 4 * n + side],
                        hr_sem.at[s, 4 * n + side], target), sends, receives)
                for side, (target, sends, receives) in enumerate(sides)
            ]
            for n, part in enumerate((slice(0, 40), slice(40, 64)))
        ]
        corners = [
            (remote(csend.at[s, n], crecv.at[s, n], hs_sem.at[s, 8 + n], hr_sem.at[s, 8 + n], target), sends, receives)
            for n, (target, sends, receives) in enumerate(corner_sides)
        ]
        return rows, corners

    corner_places = ((15, 6, 39, 0, 7), (16, 1, 8, 7, 40), (17, 1, 39, 7, 7), (18, 6, 8, 0, 40))

    def pack_corners(s, rel):
        for n, (q, layer, row, _, _) in enumerate(corner_places):
            for h in range(2):
                csend[s, n, h:h + 1, :] = rel[POS[q], layer, h, row:row + 1, :]

    row_places = [[(10 * n + k, z, k // 2, k % 2) for n, z in enumerate(layers) for k in range(10)] for layers in (
        (1, 2, 3, 4), (None, None, None, None, 0, 5))]
    row_places = [[p for p in places if p[1] is not None] for places in row_places]

    def pack_rows(s, rel, part):
        for side, (slots, row) in enumerate(((UP_Y, 39), (DOWN_Y, 8))):
            for place, z, n, h in row_places[part]:
                ysend[s, side, place:place + 1, :] = rel[slots[n], z + 1, h, row:row + 1, :]

    def unpack_rows(s, rel, part):
        for side, (slots, row, edge) in enumerate(((UP_Y, 7, r == 0), (DOWN_Y, 40, r == NR - 1))):
            for place, z, n, h in row_places[part]:
                rel[slots[n], z + 1, h, row:row + 1, :] = jnp.where(
                    edge, WALL, yrecv[s, side, place:place + 1, :]
                )

    def take_layers(copies, t):
        finish(copies[2 * t:2 * t + 2])

    def take_corners(s, copies, rel):
        finish(copies)
        edges = (
            (d == 0) | (r == 0), (d == ND - 1) | (r == NR - 1), (d == ND - 1) | (r == 0), (d == 0) | (r == NR - 1)
        )
        for n, (q, _, _, layer, row) in enumerate(corner_places):
            for h in range(2):
                rel[POS[q], layer, h, row:row + 1, :] = jnp.where(edges[n], WALL, crecv[s, n, h:h + 1, :])

    loads[NZL].wait()
    for z in (5, 0):
        loads[z].wait()
        for t in range(4):
            first_tile(z, t)
    pack_corners(0, r1)
    pl.semaphore_wait(barrier, len(peers))
    layers1 = [copy for t in range(4) for copy in layer_copies(0, r1, t)]
    rows1, corners1 = halo_copies(0, r1)
    start(layers1 + corners1)
    for peer in columns_peers:
        pl.semaphore_signal(ready, inc=1, device_id=peer, device_id_type=MESH)
    pack_rows(0, r1, 1)
    start(rows1[1])
    for z in range(1, 5):
        loads[z].wait()
    tiles(8, first_tile, lambda i: 1 + (i >> 1), lambda i: 3 * (i & 1))
    pack_rows(0, r1, 0)
    start(rows1[0])
    tiles(8, first_tile, lambda i: 1 + (i >> 1), lambda i: 1 + (i & 1))

    tiles(8, second_tile, lambda i: 1 + (i >> 1), lambda i: 1 + (i & 1))
    for part in (1, 0):
        finish(rows1[part])
        unpack_rows(0, r1, part)
    tiles(8, second_tile, lambda i: 1 + (i >> 1), lambda i: 3 * (i & 1))
    rows2, corners2 = halo_copies(1, r2)
    pack_rows(1, r2, 0)
    start(rows2[0])
    layers2 = [copy for t in range(4) for copy in layer_copies(1, r2, t)]
    take_corners(0, corners1, r1)
    take_layers(layers1, 0)
    outer_tiles(second_tile, lambda t: take_layers(layers1, t + 1) if t < 3 else None, layers2)
    pack_rows(1, r2, 1)
    pack_corners(1, r2)
    start(layers2[6:] + rows2[1] + corners2)

    loads[NZL + 1].wait()

    def third_tiles(count, z_of, t_of, before, carry):
        def step(i, places):
            last = jnp.maximum(i - 1, 0)
            first = i == 0
            following = third_tile(z_of(i), t_of(i))
            classify(
                jnp.where(first, before[0], z_of(last)), jnp.where(first, before[1], t_of(last)), places
            )
            return following

        return lax.fori_loop(0, count, step, carry)

    site_copies = [
        [
            (remote(ssend.at[side, slots], srecv.at[side, slots], c_send_sem.at[part, side],
                    c_recv_sem.at[part, side], target), sends, receives)
            for side, (target, sends, receives) in enumerate(sides)
        ]
        for part, slots in enumerate((slice(0, 2), slice(2, 3)))
    ]
    def pack_sites(part, layers):
        for n, z in enumerate(layers):
            for side, row in enumerate((39, 8)):
                for c in range(4):
                    place = 4 * (n % 2) + c
                    ssend[side, 2 * part + n // 2, place:place + 1, :] = cbuf[c, z, row:row + 1, :]
        start(site_copies[part])

    def unpack_sites(part, layers):
        finish(site_copies[part])
        for n, z in enumerate(layers):
            for side, (row, edge) in enumerate(((7, r == 0), (40, r == NR - 1))):
                for c in range(4):
                    place = 4 * (n % 2) + c
                    cbuf[c, z, row:row + 1, :] = jnp.where(
                        edge, 0.0, srecv[side, 2 * part + n // 2, place:place + 1, :]
                    )

    places = tuple(jnp.zeros((8, 128), F32) for _ in range(4))
    places = third_tiles(8, lambda i: 1 + (i >> 1), lambda i: 1 + (i & 1), (1, 1), places)
    finish(rows2[0])
    unpack_rows(1, r2, 0)
    places = third_tiles(4, lambda i: 2 + (i >> 1), lambda i: 3 * (i & 1), (4, 2), places)
    finish(rows2[1])
    unpack_rows(1, r2, 1)
    places = third_tiles(4, lambda i: 1 + 3 * (i >> 1), lambda i: 3 * (i & 1), (3, 3), places)
    classify(4, 3, places)
    pack_sites(0, (1, 2, 3, 4))
    take_corners(1, corners2, r2)
    for t in range(2):
        take_layers(layers2, t)
    places = third_tiles(2, lambda i: i * 5, lambda i: 0, (4, 3), places)
    for t in range(2, 4):
        take_layers(layers2, t)
    places = third_tiles(2, lambda i: i * 5, lambda i: 3, (5, 0), places)

    classify(5, 3, places)
    pack_sites(1, (0, 5))
    places = third_tiles(4, lambda i: (i >> 1) * 5, lambda i: 1 + (i & 1), (5, 3), places)
    classify(5, 2, places)

    def columns(z):
        for c in range(4):
            sites = cbuf[c, z]
            high = sites.astype(BF16)
            low = (sites - high.astype(F32)).astype(BF16)
            wide = lax.dot_general(
                wcols[...], jnp.concatenate([high, low], axis=0), (((1,), (0,)), ((), ())),
                preferred_element_type=F32,
            )
            high = wide.astype(BF16)
            low = (wide - high.astype(F32)).astype(BF16)
            place = slice((c % 2) * 128, (c % 2) * 128 + 128)
            vbuf[z, c // 2, 0, place, :] = high
            vbuf[z, c // 2, 1, place, :] = low

    def columns_step(i, carry):
        columns(i + 1)
        return carry

    def render(group, layers):
        weights = wrows[group * 256:(group + 1) * 256, :]
        for z in layers:
            drawn = []
            for pair in (1, 0):
                parts = [
                    lax.dot_general(
                        weights, vbuf[z, pair, n], (((1,), (1,)), ((), ())), preferred_element_type=F32
                    )
                    for n in range(2)
                ]
                drawn.append(parts[0] + parts[1])
            for half in range(2):
                rows = slice(half * 128, half * 128 + 128)
                parts = [drawn[1 - c // 2][rows, (c % 2) * 128:(c % 2) * 128 + 128] for c in range(4)]
                if z == 0:
                    through = 1.0 - parts[3]
                    parts = [parts[c] + through * acc[group, half, c] for c in range(4)]
                elif z > 1:
                    through = 1.0 - acc[group, half, 3]
                    parts = [acc[group, half, c] + through * parts[c] for c in range(4)]
                for c in range(4):
                    acc[group, half, c] = parts[c]

    def columns_inner(i, carry):
        columns(i + 1)
        return carry

    def columns_outer(i, carry):
        columns(5 * i)
        return carry

    unpack_sites(0, (1, 2, 3, 4))
    lax.fori_loop(0, 4, columns_inner, 0, unroll=2)
    render(0, (1, 2, 3, 4))
    unpack_sites(1, (0, 5))
    lax.fori_loop(0, 2, columns_outer, 0, unroll=2)

    partner = at(d + 1 - 2 * core, r)
    swaps = [
        remote(acc.at[group, 1 - core], xrecv.at[group], x_sem.at[0, group], x_sem.at[1, group], partner)
        for group in range(2)
    ]
    chips = list(range(1, NC))
    exchange = [[], []]
    for group in range(2):
        for k in chips:
            other = lax.rem(chip + k, NC)
            exchange[group].append(
                remote(pieces.at[group, other], gathered.at[group, chip],
                       g_send_sem.at[group, k], g_recv_sem.at[group, k], at(2 * other + core, r))
            )

    def join(group):
        def step(n, carry):
            rows = pl.ds(pl.multiple_of(n * 8, 8), 8)
            front = core == 0
            mine = [acc[group, core, c, rows, :] for c in range(4)]
            theirs = [xrecv[group, c, rows, :] for c in range(4)]
            near = [jnp.where(front, mine[c], theirs[c]) for c in range(4)]
            far = [jnp.where(front, theirs[c], mine[c]) for c in range(4)]
            through = 1.0 - near[3]
            for c in range(4):
                pieces[group, n, c] = near[c] + through * far[c]
            return carry

        lax.fori_loop(0, NC, step, 0, unroll=4)
        if group == 0:
            pl.semaphore_wait(ready, len(columns_peers))
        for copy in exchange[group]:
            copy.start()
        gathered[group, chip] = pieces[group, chip]

    render(0, (0, 5))
    swaps[0].start()
    render(1, (1, 2, 3, 4, 0, 5))
    swaps[1].start()
    swaps[0].wait()
    join(0)
    swaps[1].wait()
    join(1)

    for group in range(2):
        for copy in exchange[group]:
            copy.wait()
        final = [gathered[group, 0, c] for c in range(4)]
        for n in range(1, NC):
            through = 1.0 - final[3]
            final = [final[c] + through * gathered[group, n, c] for c in range(4)]
        for half in range(2):
            for c in range(4):
                fsend[2 * group + half, 4 * c:4 * c + 4, :] = final[c][4 * half:4 * half + 4, :]
    last = []
    for k in range(1, NR):
        other = lax.rem(r + k, NR)
        last.append(remote(fsend.at[other], frecv.at[r], f_send_sem.at[k], f_recv_sem.at[k], at(d, other)))
        last[-1].start()
    frecv[r] = fsend[r]
    for copy in last:
        copy.wait()
    for rr in range(NR):
        for c in range(4):
            image[c, :, rr * 128:(rr + 1) * 128] = frecv[rr, 4 * c:4 * c + 4, :]


def shards(populations, fluid_mask, tissue_tag, colour_table):
    dma = pltpu.SemaphoreType.DMA
    vmem = pl.BlockSpec(memory_space=pltpu.VMEM)
    anywhere = pl.BlockSpec(memory_space=pl.ANY)
    advanced, drawn = pl.pallas_call(
        kernel,
        out_shape=(
            pltpu.VMEM(populations.shape, F32),
            pltpu.VMEM((4, IMG // (ND * NR), IMG), F32),
        ),
        in_specs=[anywhere, anywhere, anywhere, vmem],
        out_specs=(vmem, vmem),
        scratch_shapes=[
            pltpu.VMEM((NZL, NYL, NX), jnp.int32),
            pltpu.VMEM((NZL, NYL, NX), jnp.int32),
            pltpu.VMEM((NQ, NZL + 2, 2, 48, 128), F32),
            pltpu.VMEM((NQ, NZL + 2, 2, 48, 128), F32),
            pltpu.VMEM((2, 2, 64, 128), F32),
            pltpu.VMEM((2, 2, 64, 128), F32),
            pltpu.VMEM((2, 4, 8, 128), F32),
            pltpu.VMEM((2, 4, 8, 128), F32),
            pltpu.VMEM((4, 2, 2, 8, 128), F32),
            pltpu.VMEM((4, 2, 8, 128), jnp.int32),
            pltpu.VMEM((4, NZL, 48, NX), F32),
            pltpu.VMEM((2, 3, 8, NX), F32),
            pltpu.VMEM((2, 3, 8, NX), F32),
            pltpu.VMEM((128, 96), BF16),
            pltpu.VMEM((IMG, NX), BF16),
            pltpu.VMEM((NZL, 2, 2, 256, NX), BF16),
            pltpu.VMEM((2, 2, 4, 128, 128), F32),
            pltpu.VMEM((2, 4, 128, 128), F32),
            pltpu.VMEM((2, NC, 4, 8, 128), F32),
            pltpu.VMEM((2, NC, 4, 8, 128), F32),
            pltpu.VMEM((NR, 16, 128), F32),
            pltpu.VMEM((NR, 16, 128), F32),
            dma((NZL + 2,)), dma((2, 2, 4)), dma((2, 2, 4)), dma((2, 12)), dma((2, 12)), dma((2, 2)), dma((2, 2)), dma((2, 2)),
            dma((2, NC)), dma((2, NC)), dma((NR,)), dma((NR,)), pltpu.SemaphoreType.REGULAR,
        ],
        compiler_params=pltpu.CompilerParams(
            collective_id=0, has_side_effects=True, vmem_limit_bytes=56 * 2**20
        ),
        name="vessel",
    )(populations, fluid_mask, tissue_tag, colour_table)
    return pl.pallas_call(
        deliver,
        out_shape=(
            jax.ShapeDtypeStruct(populations.shape, F32),
            jax.ShapeDtypeStruct((4, IMG // (ND * NR), IMG), F32),
        ),
        in_specs=[vmem, vmem],
        out_specs=(anywhere, anywhere),
        scratch_shapes=[dma((8,))],
        compiler_params=pltpu.CompilerParams(vmem_limit_bytes=2**20),
        name="deliver",
    )(advanced, drawn)


def deliver(advanced, drawn, adv, image, sem):
    parts = [slice(3 * n, min(3 * n + 3, NQ)) for n in range(7)]
    copies = [pltpu.make_async_copy(advanced.at[p], adv.at[p], sem.at[n]) for n, p in enumerate(parts)]
    copies.append(pltpu.make_async_copy(drawn, image, sem.at[7]))
    for copy in copies:
        copy.start()
    for copy in copies:
        copy.wait()


def solution(mesh):
    placed = (
        P(None, "depth", "rows", None),
        P("depth", "rows", None),
        P("depth", "rows", None),
        P(),
    )
    return jax.shard_map(
        shards,
        mesh=mesh,
        in_specs=placed,
        out_specs=(P(None, "depth", "rows", None), P(None, ("rows", "depth"), None)),
        check_vma=False,
    )
```
